128 devices in a mesh: axial: 16 (over z, x), trans: 4 (over y), col: 2 (over core).
Axes of the slice: x: 4, y: 4, z: 4, core: 2. Of those that a mesh axis runs over, the one named last changes fastest.
Arguments:
- concentration: float32 [2, 4, 512, 32, 512], P('col', None, 'axial', None, 'trans'), may hold values from 0.05 to 4
- zone_map: int32 [2, 32, 512], P('col', None, 'trans'), may hold values from 0 to 7
- porosity: float32 [8], replicated, may hold values from 0.35 to 0.7
- axial_number: float32 [4], replicated, may hold values from 200 to 2000
- courant: float32 [4], replicated, may hold values from 2 to 20
- transverse: float32 [4], replicated, may hold values from 0.03 to 0.12
- feed_conc: float32 [2, 4], P('col'), may hold values from 0.5 to 3
- plan: int32 [2, 2, 4], P('col'), may hold values from 0 to 3
Outputs:
- advanced: float32 [2, 4, 512, 32, 512], P('col', None, 'axial', None, 'trans')
The draws below stay inside these ranges and needn't reach their ends.
All inputs are finite; a program needn't handle non-finite values.
Results may differ from the reference program's by a relative error of at most 0.0005.
Values sent between devices are 32-bit elements; how exact they have to be, the bound alone decides.
A program may use at most 128 MiB of HBM per device.

```python
import math
import jax
import jax.numpy as jnp
from jax import lax

SPECIES = 4
ZONES = 8
STEPS = 2
CX = 32
NZ = 512
NY = 512
COLUMNS = 2


def set_ends(drawn, stream_key, smallest, largest):
    shape = drawn.shape
    index_at = [jax.random.randint(jax.random.fold_in(stream_key, axis), (), 0, shape[axis]) for axis in range(len(shape))]
    drawn = drawn.at[tuple(index_at)].set(smallest)
    longest = shape.index(max(shape))
    index_at[longest] = (index_at[longest] + 1) % shape[longest]
    return drawn.at[tuple(index_at)].set(largest)


def levels(key, extent, pieces, smallest, top_value):
    gain, own = 1.0, jax.random.fold_in(key, 6)
    for position, parts in pieces:
        draws = jnp.exp(jax.random.uniform(jax.random.fold_in(own, position), (parts,), jnp.float32, smallest / len(pieces), top_value / len(pieces)))
        gain = gain * jnp.repeat(draws, extent[position] // parts).reshape([-1 if axis == position else 1 for axis in range(len(extent))])
    return gain


def setup_inputs(seed: int = 0) -> dict:
    key_of = jax.random.split(jax.random.key(seed), 9)
    return {
        "concentration": jnp.clip(jnp.exp(math.log(4.0) - 4.3820266 * jax.random.uniform(key_of[0], (COLUMNS, SPECIES, NZ, CX, NY), jnp.float32) ** levels(key_of[0], (COLUMNS, SPECIES, NZ, CX, NY), ((0, 2), (2, 16), (4, 4)), -0.2, 0.2)), 0.05, 4.0),
        "zone_map": set_ends(jax.random.randint(key_of[1], (COLUMNS, CX, NY), 0, ZONES), jax.random.fold_in(key_of[1], 1), 0, ZONES - 1).astype(jnp.int32),
        "porosity": jnp.clip(jax.random.uniform(key_of[2], (ZONES,), jnp.float32, 0.35, 0.7), 0.35, 0.7),
        "axial_number": jnp.clip(jnp.exp(jax.random.uniform(key_of[3], (SPECIES,), jnp.float32, math.log(200.0), math.log(2000.0))), 200.0, 2000.0),
        "courant": jnp.clip(jnp.exp(jax.random.uniform(key_of[4], (SPECIES,), jnp.float32, math.log(2.0), math.log(20.0))), 2.0, 20.0),
        "transverse": jnp.clip(jax.random.uniform(key_of[5], (SPECIES,), jnp.float32, 0.03, 0.12), 0.03, 0.12),
        "feed_conc": jnp.clip(0.5 + 2.5 * jax.random.uniform(key_of[6], (COLUMNS, SPECIES), jnp.float32) ** levels(key_of[6], (COLUMNS, SPECIES), ((0, 2),), -0.2, 0.2), 0.5, 3.0),
        "plan": set_ends(jax.random.randint(key_of[7], (COLUMNS, STEPS, SPECIES), 0, 4), jax.random.fold_in(key_of[7], 1), 0, 3).astype(jnp.int32),
    }


def void_map(zone_map, porosity):
    voids = jnp.zeros(zone_map.shape, porosity.dtype)
    for number in range(porosity.shape[0]):
        voids = voids + jnp.where(zone_map == number, porosity[number], 0.0)
    return voids


def dispersed(values, values_pad, voids_pad, transverse):
    wide = values.shape[3]
    tall = values.shape[4]
    centre = voids_pad[:, :, :, 1:wide + 1, 1:tall + 1]
    flux_sum = jnp.zeros(values.shape, values.dtype)
    for offset_x, offset_y in ((2, 1), (0, 1), (1, 2), (1, 0)):
        partner = voids_pad[:, :, :, offset_x:offset_x + wide, offset_y:offset_y + tall]
        beside = values_pad[:, :, :, offset_x:offset_x + wide, offset_y:offset_y + tall]
        flux_sum = flux_sum + 2.0 * centre * partner / (centre + partner) * (beside - values)
    return values + transverse[None, :, None, None, None] * flux_sum / centre


def sweep(sub_diag, super_diag, main_rows, rhs_rows):
    def forward(state, row_data):
        coef_prev, rhs_prev = state
        main_now, rhs_now = row_data
        pivot = main_now - sub_diag * coef_prev
        coef_next = super_diag / pivot
        rhs_next = (rhs_now - sub_diag * rhs_prev) / pivot
        return (coef_next, rhs_next), (coef_next, rhs_next)

    start = (jnp.zeros(main_rows.shape[1:], main_rows.dtype), jnp.zeros(rhs_rows.shape[1:], rhs_rows.dtype))
    final_state, (coefs, rhs_mod) = lax.scan(forward, start, (main_rows, rhs_rows))

    def backward(later, row_data):
        coef_now, rhs_now = row_data
        solved = rhs_now - coef_now * later
        return solved, solved

    first_row, solved_rows = lax.scan(backward, jnp.zeros(rhs_rows.shape[1:], rhs_rows.dtype), (coefs, rhs_mod), reverse=True)
    return solved_rows


def reference(concentration, zone_map, porosity, axial_number, courant, transverse, feed_conc, plan):
    voids = void_map(zone_map, porosity)
    voids_full = voids[:, None, None]
    flow_rate = courant[None, :, None, None] / voids[:, None]
    dispersion = axial_number[None, :, None, None] + jnp.zeros_like(flow_rate)
    sub_diag = -(dispersion + flow_rate)
    super_diag = -dispersion
    main_inner = 1.0 + 2.0 * dispersion + flow_rate
    main_end = 1.0 + dispersion + flow_rate
    depth = concentration.shape[2]
    main_rows = jnp.concatenate([jnp.broadcast_to(main_inner, (depth - 1,) + main_inner.shape), main_end[None]], 0)
    widen = ((0, 0), (0, 0), (0, 0), (1, 1), (1, 1))
    values = concentration
    for half_step in range(plan.shape[1]):
        inflow_face = values[:, :, 0]
        partner = inflow_face[::-1]
        recycled = (plan[:, half_step, :].astype(jnp.float32) + 1.0) * 0.25
        recycled = recycled[:, :, None, None]
        inlet = (1.0 - recycled) * feed_conc[:, :, None, None] + recycled * partner
        moved = dispersed(values, jnp.pad(values, widen), jnp.pad(voids_full, widen), transverse)
        rhs = moved.at[:, :, 0].add(-sub_diag * inlet)
        solved = sweep(sub_diag, super_diag, main_rows, jnp.moveaxis(rhs, 2, 0))
        values = jnp.moveaxis(solved, 0, 2)
    return values
```

```python
import jax
import jax.numpy as jnp
from jax import lax
from jax.experimental import pallas as pl
from jax.experimental.pallas import tpu as pltpu
from jax.sharding import PartitionSpec as P


def swapped(array, axis, distance):
    return lax.ppermute(array, axis, [(i, i ^ 1 << distance) for i in range(lax.axis_size(axis))])


def from_behind(value, axis, steps):
    count = lax.axis_size(axis)
    initial, last = (max(0, -steps), min(count, count - steps))
    return lax.ppermute(value, axis, [(source, source + steps) for source in range(initial, last)])


def void_map(zone_map, porosity):
    voids = jnp.zeros(zone_map.shape, porosity.dtype)
    for number in range(porosity.shape[0]):
        voids = voids + jnp.where(zone_map == number, porosity[number], 0.0)
    return voids


def _vmem():
    return pl.BlockSpec(memory_space=pltpu.VMEM)


def setup_kernel(sub_ref, sup_ref, mi_ref, me_ref, ml_ref, cp_ref, ip_ref, l_ref, r_ref, bnd_ref):
    species, depth = cp_ref.shape[0], cp_ref.shape[1]
    for s in range(species):
        sub = sub_ref[s]
        sup = sup_ref[s]
        mi = mi_ref[s]
        coef = None
        for z in range(depth - 1):
            pivot = mi if z == 0 else mi - sub * coef
            inv = 1.0 / pivot
            coef = sup * inv
            ip_ref[s, z] = inv
            cp_ref[s, z] = coef

        def ends(last):
            inv_last = 1.0 / (last - sub * cp_ref[s, depth - 2])
            down = ip_ref[s, 0]
            downs = [down]
            for z in range(1, depth - 1):
                down = -sub * down * ip_ref[s, z]
                downs.append(down)
            left = -sub * down * inv_last
            left_last = left
            for z in range(depth - 2, -1, -1):
                left = downs[z] - cp_ref[s, z] * left
            right = inv_last
            for z in range(depth - 2, -1, -1):
                right = -cp_ref[s, z] * right
            return left, left_last, right, inv_last

        for slot, last in ((0, mi), (4, me_ref[s])):
            l0, l1, r0, r1 = ends(last)
            bnd_ref[slot + 0, s] = l0
            bnd_ref[slot + 1, s] = l1
            bnd_ref[slot + 2, s] = r0
            bnd_ref[slot + 3, s] = r1

        own_last = ml_ref[s]
        inv_last = 1.0 / (own_last - sub * cp_ref[s, depth - 2])
        ip_ref[s, depth - 1] = inv_last
        cp_ref[s, depth - 1] = sup * inv_last
        down = ip_ref[s, 0]
        l_ref[s, 0] = down
        for z in range(1, depth):
            down = -sub * down * ip_ref[s, z]
            l_ref[s, z] = down
        left = down
        right = inv_last
        r_ref[s, depth - 1] = right
        for z in range(depth - 2, -1, -1):
            left = l_ref[s, z] - cp_ref[s, z] * left
            l_ref[s, z] = left
            right = -cp_ref[s, z] * right
            r_ref[s, z] = right


def local_kernel(v_ref, hlo_ref, hhi_ref, w_ref, inflow_ref, sub_ref, cp_ref, ip_ref, y_ref, pack_ref):
    species, depth, wide, tall = v_ref.shape
    lane = lax.broadcasted_iota(jnp.int32, (wide, tall), 1)
    for s in range(species):
        wxm = w_ref[0, s]
        wxp = w_ref[1, s]
        wym = w_ref[2, s]
        wyp = w_ref[3, s]
        sub = sub_ref[s]
        down = None
        for z in range(depth):
            v = v_ref[s, z]
            xm = pltpu.roll(v, 1, 0)
            xp = pltpu.roll(v, wide - 1, 0)
            ym = jnp.where(lane == 0, hlo_ref[s, :, z : z + 1], pltpu.roll(v, 1, 1))
            yp = jnp.where(lane == tall - 1, hhi_ref[s, :, z : z + 1], pltpu.roll(v, tall - 1, 1))
            moved = v + (wxp * (xp - v) + wxm * (xm - v) + wyp * (yp - v) + wym * (ym - v))
            if z == 0:
                down = (moved + inflow_ref[s]) * ip_ref[s, 0]
            else:
                down = (moved - sub * down) * ip_ref[s, z]
            y_ref[s, z] = down
        solved = down
        pack_ref[1, s] = solved
        for z in range(depth - 2, -1, -1):
            solved = y_ref[s, z] - cp_ref[s, z] * solved
            y_ref[s, z] = solved
        pack_ref[0, s] = solved


def body(concentration, zone_map, porosity, axial_number, courant, transverse, feed_conc, plan):
    f32 = jnp.float32
    count = lax.axis_size("axial")
    position = lax.axis_index("axial")
    at_inlet = position == 0
    at_outlet = position == count - 1
    values = concentration[0]
    species, depth, wide, tall = values.shape
    voids = void_map(zone_map, porosity)[0]
    dispersion = axial_number[:, None, None] + jnp.zeros((species, wide, tall), f32)
    flow_rate = courant[:, None, None] / voids[None]
    sub = -(dispersion + flow_rate)
    sup = -dispersion
    main_inner = 1.0 + 2.0 * dispersion + flow_rate
    main_end = 1.0 + dispersion + flow_rate
    main_last = jnp.where(at_outlet, main_end, main_inner)

    block = jax.ShapeDtypeStruct((species, depth, wide, tall), f32)
    cp, ip, left_spike, right_spike, bnd = pl.pallas_call(
        setup_kernel,
        out_shape=(block, block, block, block, jax.ShapeDtypeStruct((8, species, wide, tall), f32)),
        in_specs=[_vmem()] * 5,
        out_specs=(_vmem(),) * 5,
        cost_estimate=pl.CostEstimate(
            flops=40 * species * depth * wide * tall, transcendentals=0,
            bytes_accessed=4 * 4 * species * depth * wide * tall,
        ),
    )(sub, sup, main_inner, main_end, main_last)

    voids_lo = from_behind(voids[:, tall - 1], "trans", 1)
    voids_hi = from_behind(voids[:, 0], "trans", -1)
    zero_row = jnp.zeros((1, tall), f32)
    p_xm = jnp.concatenate([zero_row, voids[:-1]], 0)
    p_xp = jnp.concatenate([voids[1:], zero_row], 0)
    p_ym = jnp.concatenate([voids_lo[:, None], voids[:, :-1]], 1)
    p_yp = jnp.concatenate([voids[:, 1:], voids_hi[:, None]], 1)
    faces = jnp.stack([2.0 * p / (voids + p) for p in (p_xm, p_xp, p_ym, p_yp)])
    weights = faces[:, None] * transverse[None, :, None, None]

    local = pl.pallas_call(
        local_kernel,
        out_shape=(block, jax.ShapeDtypeStruct((2, species, wide, tall), f32)),
        in_specs=[_vmem()] * 8,
        out_specs=(_vmem(), _vmem()),
        cost_estimate=pl.CostEstimate(
            flops=30 * species * depth * wide * tall, transcendentals=0,
            bytes_accessed=4 * 4 * species * depth * wide * tall,
        ),
    )

    bounds_inner = [bnd[i] for i in range(4)]
    bounds_outlet = [bnd[4 + i] for i in range(4)]
    zeros = jnp.zeros((species, wide, tall), f32)

    for half_step in range(plan.shape[1]):
        face = values[:, 0]
        partner = swapped(face, "col", 0)
        recycled = (plan[0, half_step, :].astype(f32) + 1.0) * 0.25
        recycled = recycled[:, None, None]
        inlet = (1.0 - recycled) * feed_conc[0][:, None, None] + recycled * partner
        inflow = jnp.where(at_inlet, -sub * inlet, 0.0)
        halo_lo = from_behind(jnp.swapaxes(values[:, :, :, tall - 1], 1, 2), "trans", 1)
        halo_hi = from_behind(jnp.swapaxes(values[:, :, :, 0], 1, 2), "trans", -1)
        base, pack = local(values, halo_lo, halo_hi, weights, inflow, sub, cp, ip)
        gathered = lax.all_gather(pack, "axial")

        tops, coefs_t, bottoms, coefs_b = [], [], [], []
        bottom = coef_b = None
        for j in range(count):
            l0, l1, r0, r1 = bounds_outlet if j == count - 1 else bounds_inner
            first, last = gathered[j, 0], gathered[j, 1]
            up0 = zeros if j == count - 1 else sup * r0
            up1 = zeros if j == count - 1 else sup * r1
            if j == 0:
                top, coef_t, bottom, coef_b = first, -up0, last, -up1
            else:
                al0 = sub * l0
                al1 = sub * l1
                pivot = 1.0 + al0 * coef_b
                top = (first - al0 * bottom) / pivot
                coef_t = -up0 / pivot
                new_bottom = last - al1 * (bottom + coef_b * top)
                coef_b = -up1 - al1 * coef_b * coef_t
                bottom = new_bottom
            tops.append(top)
            coefs_t.append(coef_t)
            bottoms.append(bottom)
            coefs_b.append(coef_b)
        t_vals = [None] * (count + 1)
        t_vals[count] = zeros
        for j in range(count - 1, -1, -1):
            t_vals[j] = tops[j] + coefs_t[j] * t_vals[j + 1]
        u_prev = jnp.stack([zeros] + [bottoms[j] + coefs_b[j] * t_vals[j + 1] for j in range(count - 1)])
        t_next = jnp.stack([t_vals[j + 1] for j in range(count)])
        u_prev = lax.dynamic_index_in_dim(u_prev, position, 0, keepdims=False)
        t_next = lax.dynamic_index_in_dim(t_next, position, 0, keepdims=False)
        values = (
            base
            - (sub * u_prev)[:, None] * left_spike
            - (sup * t_next)[:, None] * right_spike
        )
    return values[None]


def solution(mesh):
    in_specs = (
        P("col", None, "axial", None, "trans"),
        P("col", None, "trans"),
        P(),
        P(),
        P(),
        P(),
        P("col", None),
        P("col", None, None),
    )
    out_specs = P("col", None, "axial", None, "trans")
    return jax.shard_map(body, mesh=mesh, in_specs=in_specs, out_specs=out_specs, check_vma=False)
```

```python
import functools

import jax
import jax.numpy as jnp
from jax import lax
from jax.experimental import pallas as pl
from jax.experimental.pallas import tpu as pltpu
from jax.sharding import PartitionSpec as P


def swapped(array, axis, distance):
    return lax.ppermute(array, axis, [(i, i ^ 1 << distance) for i in range(lax.axis_size(axis))])


def from_behind(value, axis, steps):
    count = lax.axis_size(axis)
    initial, last = (max(0, -steps), min(count, count - steps))
    return lax.ppermute(value, axis, [(source, source + steps) for source in range(initial, last)])


def void_map(zone_map, porosity):
    voids = jnp.zeros(zone_map.shape, porosity.dtype)
    for number in range(porosity.shape[0]):
        voids = voids + jnp.where(zone_map == number, porosity[number], 0.0)
    return voids


def _vmem():
    return pl.BlockSpec(memory_space=pltpu.VMEM)


ROUNDS = (1, 2, 4, 8)
MESH = pl.DeviceIdType.MESH


def setup_kernel(count, sub_ref, sup_ref, mi_ref, me_ref, ml_ref, cp_ref, ip_ref, l_ref, r_ref, co_ref,
                 qf_ref, qb_ref, mf_ref, mb_ref, cprev_ref, hnext_ref, exf_ref, exb_ref):
    species, depth = cp_ref.shape[0], cp_ref.shape[1]
    position = lax.axis_index("axial")
    rounds = len(ROUNDS)
    for s in range(species):
        sub = sub_ref[s]
        sup = sup_ref[s]
        mi = mi_ref[s]
        coef = None
        for z in range(depth - 1):
            pivot = mi if z == 0 else mi - sub * coef
            inv = 1.0 / pivot
            coef = sup * inv
            ip_ref[s, z] = inv
            cp_ref[s, z] = coef

        def ends(last):
            inv_last = 1.0 / (last - sub * cp_ref[s, depth - 2])
            down = ip_ref[s, 0]
            downs = [down]
            for z in range(1, depth - 1):
                down = -sub * down * ip_ref[s, z]
                downs.append(down)
            left = -sub * down * inv_last
            left_last = left
            for z in range(depth - 2, -1, -1):
                left = downs[z] - cp_ref[s, z] * left
            right = inv_last
            for z in range(depth - 2, -1, -1):
                right = -cp_ref[s, z] * right
            return left, left_last, right, inv_last

        l0i, l1i, r0i, r1i = ends(mi)
        l0o, l1o, r0o, r1o = ends(me_ref[s])

        own_last = ml_ref[s]
        inv_last = 1.0 / (own_last - sub * cp_ref[s, depth - 2])
        ip_ref[s, depth - 1] = inv_last
        cp_ref[s, depth - 1] = sup * inv_last
        down = ip_ref[s, 0]
        l_ref[s, 0] = down
        for z in range(1, depth):
            down = -sub * down * ip_ref[s, z]
            l_ref[s, z] = down
        left = down
        right = inv_last
        r_ref[s, depth - 1] = right
        for z in range(depth - 2, -1, -1):
            left = l_ref[s, z] - cp_ref[s, z] * left
            l_ref[s, z] = left
            right = -cp_ref[s, z] * right
            r_ref[s, z] = right

        zero = jnp.zeros_like(sub)
        one = jnp.ones_like(sub)
        inner = (-sub * l0i, -sub * l1i, -sup * r0i, -sup * r1i)
        first = (zero, zero, inner[2], inner[3])
        outlet = (-sub * l0o, -sub * l1o, zero, zero)

        def couplings(j):
            return first if j == 0 else outlet if j == count - 1 else inner

        c_prev = zero
        for j in range(count):
            p0, p1, q0, q1 = couplings(j)
            inv = one if j == 0 else 1.0 / (1.0 - p0 * c_prev)
            qf_ref[j] = p1 * inv
            mf_ref[j] = p1 * c_prev * inv
            cprev_ref[j] = c_prev
            c_prev = q1 + p1 * c_prev * q0 * inv
        h_next = zero
        for j in range(count - 1, -1, -1):
            p0, p1, q0, q1 = couplings(j)
            inv = one if j == count - 1 else 1.0 / (1.0 - q1 * h_next)
            qb_ref[j] = q0 * inv
            mb_ref[j] = q0 * h_next * inv
            hnext_ref[j] = h_next
            h_next = p0 + q0 * h_next * p1 * inv

        for kk in range(count):
            exf_ref[0, kk] = one
            exb_ref[0, kk] = one
        for r in range(rounds - 1):
            d = ROUNDS[r]
            for kk in range(count):
                if kk - d >= 0:
                    exf_ref[r + 1, kk] = exf_ref[r, kk] * qf_ref[kk - d] * exf_ref[r, kk - d]
                else:
                    exf_ref[r + 1, kk] = one
                if kk + d < count:
                    exb_ref[r + 1, kk] = exb_ref[r, kk] * qb_ref[kk + d] * exb_ref[r, kk + d]
                else:
                    exb_ref[r + 1, kk] = one

        co_ref[0, s] = mf_ref[position]
        co_ref[1, s] = mb_ref[position]
        qf_own = qf_ref[position]
        qb_own = qb_ref[position]
        for r in range(rounds):
            wef = exf_ref[r, position]
            web = exb_ref[r, position]
            co_ref[2 + r, s] = wef
            co_ref[2 + rounds + r, s] = qf_own * wef
            co_ref[2 + 2 * rounds + r, s] = web
            co_ref[2 + 3 * rounds + r, s] = qb_own * web
        at_first = position == 0
        at_last = position == count - 1
        p0 = jnp.where(at_first, zero, jnp.where(at_last, outlet[0], inner[0]))
        p1 = jnp.where(at_first, zero, jnp.where(at_last, outlet[1], inner[1]))
        q0 = jnp.where(at_last, zero, inner[2])
        q1 = jnp.where(at_last, zero, inner[3])
        c_own = cprev_ref[position]
        h_own = hnext_ref[position]
        a11 = 1.0 - p0 * c_own
        a12 = -q0 * h_own
        a21 = -p1 * c_own
        a22 = 1.0 - q1 * h_own
        inv_det = 1.0 / (a11 * a22 - a12 * a21)
        base = 2 + 4 * rounds
        for i, value in enumerate(
            (p0, p1, q0, q1, c_own, h_own, a22 * inv_det, -a12 * inv_det, -a21 * inv_det, a11 * inv_det)
        ):
            co_ref[base + i, s] = value


def scan_kernel(count, pack_ref, co_ref, out_ref, sf, sb, ef, eb, snd_f, snd_b, rcv_f, rcv_b,
                ssem_f, ssem_b, rsem_f, rsem_b):
    position = lax.axis_index("axial")
    trans = lax.axis_index("trans")
    col = lax.axis_index("col")
    rounds = len(ROUNDS)
    barrier = pltpu.get_barrier_semaphore()
    partners = 0
    for d in ROUNDS:
        has_right = position + d < count
        has_left = position - d >= 0

        @pl.when(has_right)
        def _():
            pl.semaphore_signal(barrier, 1, device_id=(position + d, trans, col), device_id_type=MESH)

        @pl.when(has_left)
        def _():
            pl.semaphore_signal(barrier, 1, device_id=(position - d, trans, col), device_id_type=MESH)

        partners = partners + has_right.astype(jnp.int32) + has_left.astype(jnp.int32)
    pl.semaphore_wait(barrier, partners)

    g0 = pack_ref[0]
    g1 = pack_ref[1]
    sf[...] = g1 + co_ref[0] * g0
    sb[...] = g0 + co_ref[1] * g1
    ef[...] = jnp.zeros_like(g0)
    eb[...] = jnp.zeros_like(g0)
    for r, d in enumerate(ROUNDS):
        snd_f[r] = sf[...]
        snd_b[r] = sb[...]
        has_right = position + d < count
        has_left = position - d >= 0
        right = jnp.minimum(position + d, count - 1)
        left = jnp.maximum(position - d, 0)
        copy_f = pltpu.make_async_remote_copy(
            src_ref=snd_f.at[r], dst_ref=rcv_f.at[r], send_sem=ssem_f.at[r], recv_sem=rsem_f.at[r],
            device_id=(right, trans, col), device_id_type=MESH,
        )
        copy_b = pltpu.make_async_remote_copy(
            src_ref=snd_b.at[r], dst_ref=rcv_b.at[r], send_sem=ssem_b.at[r], recv_sem=rsem_b.at[r],
            device_id=(left, trans, col), device_id_type=MESH,
        )
        pl.when(has_right)(copy_f.start)
        pl.when(has_left)(copy_b.start)
        last_round = r == rounds - 1

        @pl.when(has_left)
        def _():
            copy_f.wait_recv()
            got = rcv_f[r]
            ef[...] += co_ref[2 + r] * got
            if not last_round:
                sf[...] += co_ref[2 + rounds + r] * got

        @pl.when(has_right)
        def _():
            copy_b.wait_recv()
            got = rcv_b[r]
            eb[...] += co_ref[2 + 2 * rounds + r] * got
            if not last_round:
                sb[...] += co_ref[2 + 3 * rounds + r] * got

        pl.when(has_right)(copy_f.wait_send)
        pl.when(has_left)(copy_b.wait_send)

    base = 2 + 4 * rounds
    before = ef[...]
    after = eb[...]
    r1 = g0 + co_ref[base + 0] * before + co_ref[base + 2] * after
    r2 = g1 + co_ref[base + 1] * before + co_ref[base + 3] * after
    top = r1 * co_ref[base + 6] + r2 * co_ref[base + 7]
    bottom = r1 * co_ref[base + 8] + r2 * co_ref[base + 9]
    out_ref[0] = before + co_ref[base + 4] * top
    out_ref[1] = after + co_ref[base + 5] * bottom


def local_kernel(v_ref, hlo_ref, hhi_ref, w_ref, inflow_ref, sub_ref, cp_ref, ip_ref, y_ref, pack_ref):
    species, depth, wide, tall = v_ref.shape
    lane = lax.broadcasted_iota(jnp.int32, (wide, tall), 1)
    for s in range(species):
        wxm = w_ref[0, s]
        wxp = w_ref[1, s]
        wym = w_ref[2, s]
        wyp = w_ref[3, s]
        sub = sub_ref[s]
        down = None
        for z in range(depth):
            v = v_ref[s, z]
            xm = pltpu.roll(v, 1, 0)
            xp = pltpu.roll(v, wide - 1, 0)
            ym = jnp.where(lane == 0, hlo_ref[s, :, z : z + 1], pltpu.roll(v, 1, 1))
            yp = jnp.where(lane == tall - 1, hhi_ref[s, :, z : z + 1], pltpu.roll(v, tall - 1, 1))
            moved = v + (wxp * (xp - v) + wxm * (xm - v) + wyp * (yp - v) + wym * (ym - v))
            if z == 0:
                down = (moved + inflow_ref[s]) * ip_ref[s, 0]
            else:
                down = (moved - sub * down) * ip_ref[s, z]
            y_ref[s, z] = down
        solved = down
        pack_ref[1, s] = solved
        for z in range(depth - 2, -1, -1):
            solved = y_ref[s, z] - cp_ref[s, z] * solved
            y_ref[s, z] = solved
        pack_ref[0, s] = solved


def body(concentration, zone_map, porosity, axial_number, courant, transverse, feed_conc, plan):
    f32 = jnp.float32
    count = lax.axis_size("axial")
    position = lax.axis_index("axial")
    at_inlet = position == 0
    at_outlet = position == count - 1
    values = concentration[0]
    species, depth, wide, tall = values.shape
    voids = void_map(zone_map, porosity)[0]
    dispersion = axial_number[:, None, None] + jnp.zeros((species, wide, tall), f32)
    flow_rate = courant[:, None, None] / voids[None]
    sub = -(dispersion + flow_rate)
    sup = -dispersion
    main_inner = 1.0 + 2.0 * dispersion + flow_rate
    main_end = 1.0 + dispersion + flow_rate
    main_last = jnp.where(at_outlet, main_end, main_inner)

    block = jax.ShapeDtypeStruct((species, depth, wide, tall), f32)
    row = jax.ShapeDtypeStruct((species, wide, tall), f32)
    rounds = len(ROUNDS)
    n_co = 2 + 4 * rounds + 10
    slab = (wide, tall)
    cp, ip, left_spike, right_spike, co = pl.pallas_call(
        functools.partial(setup_kernel, count),
        out_shape=(block, block, block, block, jax.ShapeDtypeStruct((n_co, species, wide, tall), f32)),
        in_specs=[_vmem()] * 5,
        out_specs=(_vmem(),) * 5,
        scratch_shapes=[pltpu.VMEM((count,) + slab, f32)] * 6 + [pltpu.VMEM((rounds, count) + slab, f32)] * 2,
        cost_estimate=pl.CostEstimate(
            flops=40 * species * depth * wide * tall, transcendentals=0,
            bytes_accessed=4 * 4 * species * depth * wide * tall,
        ),
    )(sub, sup, main_inner, main_end, main_last)

    scan = pl.pallas_call(
        functools.partial(scan_kernel, count),
        out_shape=jax.ShapeDtypeStruct((2, species, wide, tall), f32),
        in_specs=[_vmem()] * 2,
        out_specs=_vmem(),
        scratch_shapes=[pltpu.VMEM((species,) + slab, f32)] * 4
        + [pltpu.VMEM((rounds, species) + slab, f32)] * 4
        + [pltpu.SemaphoreType.DMA((rounds,))] * 4,
        compiler_params=pltpu.CompilerParams(collective_id=0, has_side_effects=True),
        cost_estimate=pl.CostEstimate(
            flops=40 * species * wide * tall, transcendentals=0, bytes_accessed=40 * species * wide * tall * 4,
        ),
    )

    voids_lo = from_behind(voids[:, tall - 1], "trans", 1)
    voids_hi = from_behind(voids[:, 0], "trans", -1)
    zero_row = jnp.zeros((1, tall), f32)
    p_xm = jnp.concatenate([zero_row, voids[:-1]], 0)
    p_xp = jnp.concatenate([voids[1:], zero_row], 0)
    p_ym = jnp.concatenate([voids_lo[:, None], voids[:, :-1]], 1)
    p_yp = jnp.concatenate([voids[:, 1:], voids_hi[:, None]], 1)
    faces = jnp.stack([2.0 * p / (voids + p) for p in (p_xm, p_xp, p_ym, p_yp)])
    weights = faces[:, None] * transverse[None, :, None, None]

    local = pl.pallas_call(
        local_kernel,
        out_shape=(block, jax.ShapeDtypeStruct((2, species, wide, tall), f32)),
        in_specs=[_vmem()] * 8,
        out_specs=(_vmem(), _vmem()),
        cost_estimate=pl.CostEstimate(
            flops=30 * species * depth * wide * tall, transcendentals=0,
            bytes_accessed=4 * 4 * species * depth * wide * tall,
        ),
    )

    for half_step in range(plan.shape[1]):
        face = values[:, 0]
        partner = swapped(face, "col", 0)
        recycled = (plan[0, half_step, :].astype(f32) + 1.0) * 0.25
        recycled = recycled[:, None, None]
        inlet = (1.0 - recycled) * feed_conc[0][:, None, None] + recycled * partner
        inflow = jnp.where(at_inlet, -sub * inlet, 0.0)
        halo_lo = from_behind(jnp.swapaxes(values[:, :, :, tall - 1], 1, 2), "trans", 1)
        halo_hi = from_behind(jnp.swapaxes(values[:, :, :, 0], 1, 2), "trans", -1)
        base, pack = local(values, halo_lo, halo_hi, weights, inflow, sub, cp, ip)
        ends = scan(pack, co)
        u_prev, t_next = ends[0], ends[1]
        values = (
            base
            - (sub * u_prev)[:, None] * left_spike
            - (sup * t_next)[:, None] * right_spike
        )
    return values[None]


def solution(mesh):
    in_specs = (
        P("col", None, "axial", None, "trans"),
        P("col", None, "trans"),
        P(),
        P(),
        P(),
        P(),
        P("col", None),
        P("col", None, None),
    )
    out_specs = P("col", None, "axial", None, "trans")
    return jax.shard_map(body, mesh=mesh, in_specs=in_specs, out_specs=out_specs, check_vma=False)
```

```python
import functools

import jax
import jax.numpy as jnp
from jax import lax
from jax.experimental import pallas as pl
from jax.experimental.pallas import tpu as pltpu
from jax.sharding import PartitionSpec as P


def swapped(array, axis, distance):
    return lax.ppermute(array, axis, [(i, i ^ 1 << distance) for i in range(lax.axis_size(axis))])


def from_behind(value, axis, steps):
    count = lax.axis_size(axis)
    initial, last = (max(0, -steps), min(count, count - steps))
    return lax.ppermute(value, axis, [(source, source + steps) for source in range(initial, last)])


def void_map(zone_map, porosity):
    voids = jnp.zeros(zone_map.shape, porosity.dtype)
    for number in range(porosity.shape[0]):
        voids = voids + jnp.where(zone_map == number, porosity[number], 0.0)
    return voids


def _vmem():
    return pl.BlockSpec(memory_space=pltpu.VMEM)


ROUNDS = (1, 2, 4, 8)
MESH = pl.DeviceIdType.MESH


def setup_kernel(count, zone_ref, zlo_ref, zhi_ref, por_ref, ax_ref, cour_ref, tr_ref,
                 cp_ref, ip_ref, l_ref, r_ref, co_ref, w_ref, sub_ref, sup_ref,
                 qf_ref, qb_ref, mf_ref, mb_ref, cprev_ref, hnext_ref, exf_ref, exb_ref):
    species, depth, wide, tall = cp_ref.shape
    position = lax.axis_index("axial")
    trans = lax.axis_index("trans")
    n_trans = lax.axis_size("trans")
    rounds = len(ROUNDS)
    at_outlet = position == count - 1

    def porosity_of(zone):
        voids = jnp.zeros(zone.shape, jnp.float32)
        for number in range(por_ref.shape[0]):
            voids = voids + jnp.where(zone == number, por_ref[number], 0.0)
        return voids

    voids = porosity_of(zone_ref[...])
    voids_lo = jnp.where(trans == 0, 0.0, porosity_of(zlo_ref[...]))
    voids_hi = jnp.where(trans == n_trans - 1, 0.0, porosity_of(zhi_ref[...]))
    sublane = lax.broadcasted_iota(jnp.int32, (wide, tall), 0)
    lane = lax.broadcasted_iota(jnp.int32, (wide, tall), 1)
    p_xm = jnp.where(sublane == 0, 0.0, pltpu.roll(voids, 1, 0))
    p_xp = jnp.where(sublane == wide - 1, 0.0, pltpu.roll(voids, wide - 1, 0))
    p_ym = jnp.where(lane == 0, jnp.broadcast_to(voids_lo, (wide, tall)), pltpu.roll(voids, 1, 1))
    p_yp = jnp.where(lane == tall - 1, jnp.broadcast_to(voids_hi, (wide, tall)), pltpu.roll(voids, tall - 1, 1))
    faces = [2.0 * p / (voids + p) for p in (p_xm, p_xp, p_ym, p_yp)]

    for s in range(species):
        for direction in range(4):
            w_ref[direction, s] = tr_ref[s] * faces[direction]
        dispersion = ax_ref[s] + jnp.zeros((wide, tall), jnp.float32)
        flow_rate = cour_ref[s] / voids
        sub = -(dispersion + flow_rate)
        sup = -dispersion
        mi = 1.0 + 2.0 * dispersion + flow_rate
        me = 1.0 + dispersion + flow_rate
        sub_ref[s] = sub
        sup_ref[s] = sup
        coef = None
        for z in range(depth - 1):
            pivot = mi if z == 0 else mi - sub * coef
            inv = 1.0 / pivot
            coef = sup * inv
            ip_ref[s, z] = inv
            cp_ref[s, z] = coef

        def ends(last):
            inv_last = 1.0 / (last - sub * cp_ref[s, depth - 2])
            down = ip_ref[s, 0]
            downs = [down]
            for z in range(1, depth - 1):
                down = -sub * down * ip_ref[s, z]
                downs.append(down)
            left = -sub * down * inv_last
            left_last = left
            for z in range(depth - 2, -1, -1):
                left = downs[z] - cp_ref[s, z] * left
            right = inv_last
            for z in range(depth - 2, -1, -1):
                right = -cp_ref[s, z] * right
            return left, left_last, right, inv_last

        l0i, l1i, r0i, r1i = ends(mi)
        l0o, l1o, r0o, r1o = ends(me)

        own_last = jnp.where(at_outlet, me, mi)
        inv_last = 1.0 / (own_last - sub * cp_ref[s, depth - 2])
        ip_ref[s, depth - 1] = inv_last
        cp_ref[s, depth - 1] = sup * inv_last
        down = ip_ref[s, 0]
        l_ref[s, 0] = down
        for z in range(1, depth):
            down = -sub * down * ip_ref[s, z]
            l_ref[s, z] = down
        left = down
        right = inv_last
        r_ref[s, depth - 1] = right
        for z in range(depth - 2, -1, -1):
            left = l_ref[s, z] - cp_ref[s, z] * left
            l_ref[s, z] = left
            right = -cp_ref[s, z] * right
            r_ref[s, z] = right

        zero = jnp.zeros_like(sub)
        one = jnp.ones_like(sub)
        inner = (-sub * l0i, -sub * l1i, -sup * r0i, -sup * r1i)
        first = (zero, zero, inner[2], inner[3])
        outlet = (-sub * l0o, -sub * l1o, zero, zero)

        def couplings(j):
            return first if j == 0 else outlet if j == count - 1 else inner

        c_prev = zero
        for j in range(count):
            p0, p1, q0, q1 = couplings(j)
            inv = one if j == 0 else 1.0 / (1.0 - p0 * c_prev)
            qf_ref[j] = p1 * inv
            mf_ref[j] = p1 * c_prev * inv
            cprev_ref[j] = c_prev
            c_prev = q1 + p1 * c_prev * q0 * inv
        h_next = zero
        for j in range(count - 1, -1, -1):
            p0, p1, q0, q1 = couplings(j)
            inv = one if j == count - 1 else 1.0 / (1.0 - q1 * h_next)
            qb_ref[j] = q0 * inv
            mb_ref[j] = q0 * h_next * inv
            hnext_ref[j] = h_next
            h_next = p0 + q0 * h_next * p1 * inv

        for kk in range(count):
            exf_ref[0, kk] = one
            exb_ref[0, kk] = one
        for r in range(rounds - 1):
            d = ROUNDS[r]
            for kk in range(count):
                if kk - d >= 0:
                    exf_ref[r + 1, kk] = exf_ref[r, kk] * qf_ref[kk - d] * exf_ref[r, kk - d]
                else:
                    exf_ref[r + 1, kk] = one
                if kk + d < count:
                    exb_ref[r + 1, kk] = exb_ref[r, kk] * qb_ref[kk + d] * exb_ref[r, kk + d]
                else:
                    exb_ref[r + 1, kk] = one

        co_ref[0, s] = mf_ref[position]
        co_ref[1, s] = mb_ref[position]
        qf_own = qf_ref[position]
        qb_own = qb_ref[position]
        for r in range(rounds):
            wef = exf_ref[r, position]
            web = exb_ref[r, position]
            co_ref[2 + r, s] = wef
            co_ref[2 + rounds + r, s] = qf_own * wef
            co_ref[2 + 2 * rounds + r, s] = web
            co_ref[2 + 3 * rounds + r, s] = qb_own * web
        at_first = position == 0
        at_last = position == count - 1
        p0 = jnp.where(at_first, zero, jnp.where(at_last, outlet[0], inner[0]))
        p1 = jnp.where(at_first, zero, jnp.where(at_last, outlet[1], inner[1]))
        q0 = jnp.where(at_last, zero, inner[2])
        q1 = jnp.where(at_last, zero, inner[3])
        c_own = cprev_ref[position]
        h_own = hnext_ref[position]
        a11 = 1.0 - p0 * c_own
        a12 = -q0 * h_own
        a21 = -p1 * c_own
        a22 = 1.0 - q1 * h_own
        inv_det = 1.0 / (a11 * a22 - a12 * a21)
        base = 2 + 4 * rounds
        for i, value in enumerate(
            (p0, p1, q0, q1, c_own, h_own, a22 * inv_det, -a12 * inv_det, -a21 * inv_det, a11 * inv_det)
        ):
            co_ref[base + i, s] = value


def fused_kernel(count, v_ref, cp_ref, ip_ref, l_ref, r_ref, co_ref, w_ref, sub_ref, sup_ref, inl_ref,
                 o_ref, y_ref, hs_lo, hs_hi, hr_lo, hr_hi, face_in, g_ref, sf, sb, ef, eb,
                 snd_f, snd_b, rcv_f, rcv_b, send_sem, recv_sem):
    species, depth, wide, tall = v_ref.shape
    steps = inl_ref.shape[0]
    rounds = len(ROUNDS)
    position = lax.axis_index("axial")
    trans = lax.axis_index("trans")
    col = lax.axis_index("col")
    n_trans = lax.axis_size("trans")
    at_inlet = position == 0
    has_lo = trans > 0
    has_hi = trans < n_trans - 1
    lo_dev = (position, jnp.maximum(trans - 1, 0), col)
    hi_dev = (position, jnp.minimum(trans + 1, n_trans - 1), col)
    col_dev = (position, trans, 1 - col)
    lane = lax.broadcasted_iota(jnp.int32, (wide, tall), 1)
    base = 2 + 4 * rounds

    barrier = pltpu.get_barrier_semaphore()

    def greet(cond, device):
        @pl.when(cond)
        def _():
            pl.semaphore_signal(barrier, 1, device_id=device, device_id_type=MESH)

    greet(has_lo, lo_dev)
    greet(has_hi, hi_dev)
    greet(at_inlet, col_dev)
    partners = has_lo.astype(jnp.int32) + has_hi.astype(jnp.int32) + at_inlet.astype(jnp.int32)
    for d in ROUNDS:
        has_right = position + d < count
        has_left = position - d >= 0
        greet(has_right, (jnp.minimum(position + d, count - 1), trans, col))
        greet(has_left, (jnp.maximum(position - d, 0), trans, col))
        partners = partners + has_right.astype(jnp.int32) + has_left.astype(jnp.int32)
    pl.semaphore_wait(barrier, partners)

    zero_rows = jnp.zeros((species, wide, tall), jnp.float32)
    for h in range(steps):
        @pl.when(jnp.logical_not(has_lo))
        def _():
            hr_lo[h] = zero_rows

        @pl.when(jnp.logical_not(has_hi))
        def _():
            hr_hi[h] = zero_rows

        @pl.when(jnp.logical_not(at_inlet))
        def _():
            face_in[h] = zero_rows

    for h in range(steps):
        src = v_ref if h == 0 else o_ref
        for s in range(species):
            acc_lo = jnp.zeros((wide, tall), jnp.float32)
            acc_hi = jnp.zeros((wide, tall), jnp.float32)
            for z in range(depth):
                acc_lo = jnp.where(lane == z, jnp.broadcast_to(src[s, z, :, tall - 1 : tall], (wide, tall)), acc_lo)
                acc_hi = jnp.where(lane == z, jnp.broadcast_to(src[s, z, :, 0:1], (wide, tall)), acc_hi)
            hs_lo[h, s] = acc_lo
            hs_hi[h, s] = acc_hi
        copy_lo = pltpu.make_async_remote_copy(
            src_ref=hs_lo.at[h], dst_ref=hr_lo.at[h], send_sem=send_sem.at[h, 0], recv_sem=recv_sem.at[h, 0],
            device_id=hi_dev, device_id_type=MESH,
        )
        copy_hi = pltpu.make_async_remote_copy(
            src_ref=hs_hi.at[h], dst_ref=hr_hi.at[h], send_sem=send_sem.at[h, 1], recv_sem=recv_sem.at[h, 1],
            device_id=lo_dev, device_id_type=MESH,
        )
        copy_face = pltpu.make_async_remote_copy(
            src_ref=src.at[:, 0], dst_ref=face_in.at[h], send_sem=send_sem.at[h, 2], recv_sem=recv_sem.at[h, 2],
            device_id=col_dev, device_id_type=MESH,
        )
        pl.when(has_hi)(copy_lo.start)
        pl.when(has_lo)(copy_hi.start)
        pl.when(at_inlet)(copy_face.start)
        pl.when(has_lo)(copy_lo.wait_recv)
        pl.when(has_hi)(copy_hi.wait_recv)
        pl.when(at_inlet)(copy_face.wait_recv)
        pl.when(has_hi)(copy_lo.wait_send)
        pl.when(has_lo)(copy_hi.wait_send)
        pl.when(at_inlet)(copy_face.wait_send)

        for s in range(species):
            wxm = w_ref[0, s]
            wxp = w_ref[1, s]
            wym = w_ref[2, s]
            wyp = w_ref[3, s]
            sub = sub_ref[s]
            down = None
            for z in range(depth):
                v = src[s, z]
                xm = pltpu.roll(v, 1, 0)
                xp = pltpu.roll(v, wide - 1, 0)
                ym = jnp.where(lane == 0, hr_lo[h, s, :, z : z + 1], pltpu.roll(v, 1, 1))
                yp = jnp.where(lane == tall - 1, hr_hi[h, s, :, z : z + 1], pltpu.roll(v, tall - 1, 1))
                moved = v + (wxp * (xp - v) + wxm * (xm - v) + wyp * (yp - v) + wym * (ym - v))
                if z == 0:
                    inlet = inl_ref[h, 0, s] + inl_ref[h, 1, s] * face_in[h, s]
                    moved = moved + jnp.where(at_inlet, -sub * inlet, 0.0)
                    down = moved * ip_ref[s, 0]
                else:
                    down = (moved - sub * down) * ip_ref[s, z]
                y_ref[s, z] = down
            solved = down
            g_ref[1, s] = solved
            for z in range(depth - 2, -1, -1):
                solved = y_ref[s, z] - cp_ref[s, z] * solved
                y_ref[s, z] = solved
            g_ref[0, s] = solved

        g0 = g_ref[0]
        g1 = g_ref[1]
        sf[...] = g1 + co_ref[0] * g0
        sb[...] = g0 + co_ref[1] * g1
        ef[...] = zero_rows
        eb[...] = zero_rows
        for r, d in enumerate(ROUNDS):
            snd_f[h, r] = sf[...]
            snd_b[h, r] = sb[...]
            has_right = position + d < count
            has_left = position - d >= 0
            right = jnp.minimum(position + d, count - 1)
            left = jnp.maximum(position - d, 0)
            copy_f = pltpu.make_async_remote_copy(
                src_ref=snd_f.at[h, r], dst_ref=rcv_f.at[h, r],
                send_sem=send_sem.at[h, 3 + r], recv_sem=recv_sem.at[h, 3 + r],
                device_id=(right, trans, col), device_id_type=MESH,
            )
            copy_b = pltpu.make_async_remote_copy(
                src_ref=snd_b.at[h, r], dst_ref=rcv_b.at[h, r],
                send_sem=send_sem.at[h, 3 + rounds + r], recv_sem=recv_sem.at[h, 3 + rounds + r],
                device_id=(left, trans, col), device_id_type=MESH,
            )
            pl.when(has_right)(copy_f.start)
            pl.when(has_left)(copy_b.start)
            last_round = r == rounds - 1

            @pl.when(has_left)
            def _():
                copy_f.wait_recv()
                got = rcv_f[h, r]
                ef[...] += co_ref[2 + r] * got
                if not last_round:
                    sf[...] += co_ref[2 + rounds + r] * got

            @pl.when(has_right)
            def _():
                copy_b.wait_recv()
                got = rcv_b[h, r]
                eb[...] += co_ref[2 + 2 * rounds + r] * got
                if not last_round:
                    sb[...] += co_ref[2 + 3 * rounds + r] * got

            pl.when(has_right)(copy_f.wait_send)
            pl.when(has_left)(copy_b.wait_send)

        before = ef[...]
        after = eb[...]
        r1 = g0 + co_ref[base + 0] * before + co_ref[base + 2] * after
        r2 = g1 + co_ref[base + 1] * before + co_ref[base + 3] * after
        top = r1 * co_ref[base + 6] + r2 * co_ref[base + 7]
        bottom = r1 * co_ref[base + 8] + r2 * co_ref[base + 9]
        ef[...] = sub_ref[...] * (before + co_ref[base + 4] * top)
        eb[...] = sup_ref[...] * (after + co_ref[base + 5] * bottom)
        for s in range(species):
            left_coef = ef[s]
            right_coef = eb[s]
            for z in range(depth):
                o_ref[s, z] = y_ref[s, z] - left_coef * l_ref[s, z] - right_coef * r_ref[s, z]


def body(concentration, zone_map, porosity, axial_number, courant, transverse, feed_conc, plan):
    f32 = jnp.float32
    count = lax.axis_size("axial")
    values = concentration[0]
    species, depth, wide, tall = values.shape
    steps = plan.shape[1]
    zone = zone_map[0]
    zone_lo = from_behind(zone[:, tall - 1], "trans", 1)[:, None]
    zone_hi = from_behind(zone[:, 0], "trans", -1)[:, None]

    block = jax.ShapeDtypeStruct((species, depth, wide, tall), f32)
    row = jax.ShapeDtypeStruct((species, wide, tall), f32)
    rounds = len(ROUNDS)
    n_co = 2 + 4 * rounds + 10
    slab = (wide, tall)
    smem = pl.BlockSpec(memory_space=pltpu.SMEM)
    cp, ip, left_spike, right_spike, co, weights, sub, sup = pl.pallas_call(
        functools.partial(setup_kernel, count),
        out_shape=(block, block, block, block, jax.ShapeDtypeStruct((n_co, species, wide, tall), f32),
                   jax.ShapeDtypeStruct((4, species, wide, tall), f32), row, row),
        in_specs=[_vmem()] * 3 + [smem] * 4,
        out_specs=(_vmem(),) * 8,
        scratch_shapes=[pltpu.VMEM((count,) + slab, f32)] * 6 + [pltpu.VMEM((rounds, count) + slab, f32)] * 2,
        cost_estimate=pl.CostEstimate(
            flops=40 * species * depth * wide * tall, transcendentals=0,
            bytes_accessed=4 * 4 * species * depth * wide * tall,
        ),
    )(zone, zone_lo, zone_hi, porosity, axial_number, courant, transverse)

    recycled = (plan[0].astype(f32) + 1.0) * 0.25
    inlet_terms = jnp.stack([(1.0 - recycled) * feed_conc[0][None, :], recycled], 1)

    n_slot = 3 + 2 * rounds
    out = pl.pallas_call(
        functools.partial(fused_kernel, count),
        out_shape=block,
        in_specs=[_vmem()] * 9 + [smem],
        out_specs=_vmem(),
        scratch_shapes=[pltpu.VMEM((species, depth) + slab, f32)]
        + [pltpu.VMEM((steps, species) + slab, f32)] * 5
        + [pltpu.VMEM((2, species) + slab, f32)]
        + [pltpu.VMEM((species,) + slab, f32)] * 4
        + [pltpu.VMEM((steps, rounds, species) + slab, f32)] * 4
        + [pltpu.SemaphoreType.DMA((steps, n_slot))] * 2,
        compiler_params=pltpu.CompilerParams(collective_id=0, has_side_effects=True),
        cost_estimate=pl.CostEstimate(
            flops=60 * steps * species * depth * wide * tall, transcendentals=0,
            bytes_accessed=8 * 4 * species * depth * wide * tall,
        ),
    )(values, cp, ip, left_spike, right_spike, co, weights, sub, sup, inlet_terms)
    return out[None]


def solution(mesh):
    in_specs = (
        P("col", None, "axial", None, "trans"),
        P("col", None, "trans"),
        P(),
        P(),
        P(),
        P(),
        P("col", None),
        P("col", None, None),
    )
    out_specs = P("col", None, "axial", None, "trans")
    return jax.shard_map(body, mesh=mesh, in_specs=in_specs, out_specs=out_specs, check_vma=False)
```

```python
import functools

import jax
import jax.numpy as jnp
from jax import lax
from jax.experimental import pallas as pl
from jax.experimental.pallas import tpu as pltpu
from jax.sharding import PartitionSpec as P


def swapped(array, axis, distance):
    return lax.ppermute(array, axis, [(i, i ^ 1 << distance) for i in range(lax.axis_size(axis))])


def from_behind(value, axis, steps):
    count = lax.axis_size(axis)
    initial, last = (max(0, -steps), min(count, count - steps))
    return lax.ppermute(value, axis, [(source, source + steps) for source in range(initial, last)])


def void_map(zone_map, porosity):
    voids = jnp.zeros(zone_map.shape, porosity.dtype)
    for number in range(porosity.shape[0]):
        voids = voids + jnp.where(zone_map == number, porosity[number], 0.0)
    return voids


def _vmem():
    return pl.BlockSpec(memory_space=pltpu.VMEM)


ROUNDS = (1, 2, 4, 8)
MESH = pl.DeviceIdType.MESH


def setup_kernel(count, zone_ref, zlo_ref, zhi_ref, por_ref, ax_ref, cour_ref, tr_ref,
                 cp_ref, ip_ref, l_ref, r_ref, co_ref, w_ref, sub_ref, sup_ref,
                 qf_ref, qb_ref, mf_ref, mb_ref, cprev_ref, hnext_ref, exf_ref, exb_ref):
    species, depth, wide, tall = cp_ref.shape
    position = lax.axis_index("axial")
    trans = lax.axis_index("trans")
    n_trans = lax.axis_size("trans")
    rounds = len(ROUNDS)
    at_outlet = position == count - 1

    def porosity_of(zone):
        voids = jnp.zeros(zone.shape, jnp.float32)
        for number in range(por_ref.shape[0]):
            voids = voids + jnp.where(zone == number, por_ref[number], 0.0)
        return voids

    voids = porosity_of(zone_ref[...])
    voids_lo = jnp.where(trans == 0, 0.0, porosity_of(zlo_ref[...]))
    voids_hi = jnp.where(trans == n_trans - 1, 0.0, porosity_of(zhi_ref[...]))
    sublane = lax.broadcasted_iota(jnp.int32, (wide, tall), 0)
    lane = lax.broadcasted_iota(jnp.int32, (wide, tall), 1)
    p_xm = jnp.where(sublane == 0, 0.0, pltpu.roll(voids, 1, 0))
    p_xp = jnp.where(sublane == wide - 1, 0.0, pltpu.roll(voids, wide - 1, 0))
    p_ym = jnp.where(lane == 0, jnp.broadcast_to(voids_lo, (wide, tall)), pltpu.roll(voids, 1, 1))
    p_yp = jnp.where(lane == tall - 1, jnp.broadcast_to(voids_hi, (wide, tall)), pltpu.roll(voids, tall - 1, 1))
    faces = [2.0 * p / (voids + p) for p in (p_xm, p_xp, p_ym, p_yp)]

    for s in range(species):
        for direction in range(4):
            w_ref[direction, s] = tr_ref[s] * faces[direction]
        dispersion = ax_ref[s] + jnp.zeros((wide, tall), jnp.float32)
        flow_rate = cour_ref[s] / voids
        sub = -(dispersion + flow_rate)
        sup = -dispersion
        mi = 1.0 + 2.0 * dispersion + flow_rate
        me = 1.0 + dispersion + flow_rate
        sub_ref[s] = sub
        sup_ref[s] = sup
        coef = None
        for z in range(depth - 1):
            pivot = mi if z == 0 else mi - sub * coef
            inv = 1.0 / pivot
            coef = sup * inv
            ip_ref[s, z] = inv
            cp_ref[s, z] = coef

        def ends(last):
            inv_last = 1.0 / (last - sub * cp_ref[s, depth - 2])
            down = ip_ref[s, 0]
            downs = [down]
            for z in range(1, depth - 1):
                down = -sub * down * ip_ref[s, z]
                downs.append(down)
            left = -sub * down * inv_last
            left_last = left
            for z in range(depth - 2, -1, -1):
                left = downs[z] - cp_ref[s, z] * left
            right = inv_last
            for z in range(depth - 2, -1, -1):
                right = -cp_ref[s, z] * right
            return left, left_last, right, inv_last

        l0i, l1i, r0i, r1i = ends(mi)
        l0o, l1o, r0o, r1o = ends(me)

        own_last = jnp.where(at_outlet, me, mi)
        inv_last = 1.0 / (own_last - sub * cp_ref[s, depth - 2])
        ip_ref[s, depth - 1] = inv_last
        cp_ref[s, depth - 1] = sup * inv_last
        down = ip_ref[s, 0]
        l_ref[s, 0] = down
        for z in range(1, depth):
            down = -sub * down * ip_ref[s, z]
            l_ref[s, z] = down
        left = down
        right = inv_last
        r_ref[s, depth - 1] = right
        for z in range(depth - 2, -1, -1):
            left = l_ref[s, z] - cp_ref[s, z] * left
            l_ref[s, z] = left
            right = -cp_ref[s, z] * right
            r_ref[s, z] = right

        zero = jnp.zeros_like(sub)
        one = jnp.ones_like(sub)
        inner = (-sub * l0i, -sub * l1i, -sup * r0i, -sup * r1i)
        first = (zero, zero, inner[2], inner[3])
        outlet = (-sub * l0o, -sub * l1o, zero, zero)

        def couplings(j):
            return first if j == 0 else outlet if j == count - 1 else inner

        c_prev = zero
        for j in range(count):
            p0, p1, q0, q1 = couplings(j)
            inv = one if j == 0 else 1.0 / (1.0 - p0 * c_prev)
            qf_ref[j] = p1 * inv
            mf_ref[j] = p1 * c_prev * inv
            cprev_ref[j] = c_prev
            c_prev = q1 + p1 * c_prev * q0 * inv
        h_next = zero
        for j in range(count - 1, -1, -1):
            p0, p1, q0, q1 = couplings(j)
            inv = one if j == count - 1 else 1.0 / (1.0 - q1 * h_next)
            qb_ref[j] = q0 * inv
            mb_ref[j] = q0 * h_next * inv
            hnext_ref[j] = h_next
            h_next = p0 + q0 * h_next * p1 * inv

        for kk in range(count):
            exf_ref[0, kk] = one
            exb_ref[0, kk] = one
        for r in range(rounds - 1):
            d = ROUNDS[r]
            for kk in range(count):
                if kk - d >= 0:
                    exf_ref[r + 1, kk] = exf_ref[r, kk] * qf_ref[kk - d] * exf_ref[r, kk - d]
                else:
                    exf_ref[r + 1, kk] = one
                if kk + d < count:
                    exb_ref[r + 1, kk] = exb_ref[r, kk] * qb_ref[kk + d] * exb_ref[r, kk + d]
                else:
                    exb_ref[r + 1, kk] = one

        co_ref[0, s] = mf_ref[position]
        co_ref[1, s] = mb_ref[position]
        qf_own = qf_ref[position]
        qb_own = qb_ref[position]
        for r in range(rounds):
            wef = exf_ref[r, position]
            web = exb_ref[r, position]
            co_ref[2 + r, s] = wef
            co_ref[2 + rounds + r, s] = qf_own * wef
            co_ref[2 + 2 * rounds + r, s] = web
            co_ref[2 + 3 * rounds + r, s] = qb_own * web
        at_first = position == 0
        at_last = position == count - 1
        p0 = jnp.where(at_first, zero, jnp.where(at_last, outlet[0], inner[0]))
        p1 = jnp.where(at_first, zero, jnp.where(at_last, outlet[1], inner[1]))
        q0 = jnp.where(at_last, zero, inner[2])
        q1 = jnp.where(at_last, zero, inner[3])
        c_own = cprev_ref[position]
        h_own = hnext_ref[position]
        a11 = 1.0 - p0 * c_own
        a12 = -q0 * h_own
        a21 = -p1 * c_own
        a22 = 1.0 - q1 * h_own
        inv_det = 1.0 / (a11 * a22 - a12 * a21)
        base = 2 + 4 * rounds
        for i, value in enumerate(
            (p0, p1, q0, q1, c_own, h_own, a22 * inv_det, -a12 * inv_det, -a21 * inv_det, a11 * inv_det)
        ):
            co_ref[base + i, s] = value


def fused_kernel(count, v_ref, cp_ref, ip_ref, l_ref, r_ref, co_ref, w_ref, sub_ref, sup_ref, inl_ref,
                 o_ref, y_ref, hs_lo, hs_hi, hr_lo, hr_hi, face_in, g_ref, sf, sb, ef, eb,
                 snd_f, snd_b, rcv_f, rcv_b, send_sem, recv_sem):
    species, depth, wide, tall = v_ref.shape
    steps = inl_ref.shape[0]
    rounds = len(ROUNDS)
    position = lax.axis_index("axial")
    trans = lax.axis_index("trans")
    col = lax.axis_index("col")
    n_trans = lax.axis_size("trans")
    at_inlet = position == 0
    has_lo = trans > 0
    has_hi = trans < n_trans - 1
    lo_dev = (position, jnp.maximum(trans - 1, 0), col)
    hi_dev = (position, jnp.minimum(trans + 1, n_trans - 1), col)
    col_dev = (position, trans, 1 - col)
    lane = lax.broadcasted_iota(jnp.int32, (wide, tall), 1)
    base = 2 + 4 * rounds

    barrier = pltpu.get_barrier_semaphore()

    def greet(cond, device):
        @pl.when(cond)
        def _():
            pl.semaphore_signal(barrier, 1, device_id=device, device_id_type=MESH)

    greet(has_lo, lo_dev)
    greet(has_hi, hi_dev)
    greet(at_inlet, col_dev)
    partners = has_lo.astype(jnp.int32) + has_hi.astype(jnp.int32) + at_inlet.astype(jnp.int32)
    for d in ROUNDS:
        has_right = position + d < count
        has_left = position - d >= 0
        greet(has_right, (jnp.minimum(position + d, count - 1), trans, col))
        greet(has_left, (jnp.maximum(position - d, 0), trans, col))
        partners = partners + has_right.astype(jnp.int32) + has_left.astype(jnp.int32)
    pl.semaphore_wait(barrier, partners)

    zero_rows = jnp.zeros((species, wide, tall), jnp.float32)
    for h in range(steps):
        @pl.when(jnp.logical_not(has_lo))
        def _():
            hr_lo[h] = zero_rows

        @pl.when(jnp.logical_not(has_hi))
        def _():
            hr_hi[h] = zero_rows

        @pl.when(jnp.logical_not(at_inlet))
        def _():
            face_in[h] = zero_rows

    for h in range(steps):
        src = v_ref if h == 0 else o_ref
        for s in range(species):
            acc_lo = jnp.zeros((wide, tall), jnp.float32)
            acc_hi = jnp.zeros((wide, tall), jnp.float32)
            for z in range(depth):
                acc_lo = jnp.where(lane == z, jnp.broadcast_to(src[s, z, :, tall - 1 : tall], (wide, tall)), acc_lo)
                acc_hi = jnp.where(lane == z, jnp.broadcast_to(src[s, z, :, 0:1], (wide, tall)), acc_hi)
            hs_lo[h, s] = acc_lo
            hs_hi[h, s] = acc_hi
        copy_lo = pltpu.make_async_remote_copy(
            src_ref=hs_lo.at[h], dst_ref=hr_lo.at[h], send_sem=send_sem.at[h, 0], recv_sem=recv_sem.at[h, 0],
            device_id=hi_dev, device_id_type=MESH,
        )
        copy_hi = pltpu.make_async_remote_copy(
            src_ref=hs_hi.at[h], dst_ref=hr_hi.at[h], send_sem=send_sem.at[h, 1], recv_sem=recv_sem.at[h, 1],
            device_id=lo_dev, device_id_type=MESH,
        )
        copy_face = pltpu.make_async_remote_copy(
            src_ref=src.at[:, 0], dst_ref=face_in.at[h], send_sem=send_sem.at[h, 2], recv_sem=recv_sem.at[h, 2],
            device_id=col_dev, device_id_type=MESH,
        )
        pl.when(has_hi)(copy_lo.start)
        pl.when(has_lo)(copy_hi.start)
        pl.when(at_inlet)(copy_face.start)
        pl.when(has_lo)(copy_lo.wait_recv)
        pl.when(has_hi)(copy_hi.wait_recv)
        pl.when(at_inlet)(copy_face.wait_recv)
        pl.when(has_hi)(copy_lo.wait_send)
        pl.when(has_lo)(copy_hi.wait_send)
        pl.when(at_inlet)(copy_face.wait_send)

        def local_solve(s):
            wxm = w_ref[0, s]
            wxp = w_ref[1, s]
            wym = w_ref[2, s]
            wyp = w_ref[3, s]
            sub = sub_ref[s]
            down = None
            for z in range(depth):
                v = src[s, z]
                xm = pltpu.roll(v, 1, 0)
                xp = pltpu.roll(v, wide - 1, 0)
                ym = jnp.where(lane == 0, hr_lo[h, s, :, z : z + 1], pltpu.roll(v, 1, 1))
                yp = jnp.where(lane == tall - 1, hr_hi[h, s, :, z : z + 1], pltpu.roll(v, tall - 1, 1))
                moved = v + (wxp * (xp - v) + wxm * (xm - v) + wyp * (yp - v) + wym * (ym - v))
                if z == 0:
                    inlet = inl_ref[h, 0, s] + inl_ref[h, 1, s] * face_in[h, s]
                    moved = moved + jnp.where(at_inlet, -sub * inlet, 0.0)
                    down = moved * ip_ref[s, 0]
                else:
                    down = (moved - sub * down) * ip_ref[s, z]
                y_ref[s, z] = down
            last = down
            solved = down
            for z in range(depth - 2, -1, -1):
                solved = y_ref[s, z] - cp_ref[s, z] * solved
                y_ref[s, z] = solved
            g_ref[0, s] = solved
            g_ref[1, s] = last
            sf[s] = last + co_ref[0, s] * solved
            sb[s] = solved + co_ref[1, s] * last
            ef[s] = jnp.zeros((wide, tall), jnp.float32)
            eb[s] = jnp.zeros((wide, tall), jnp.float32)

        def copies(s, r):
            d = ROUNDS[r]
            right = jnp.minimum(position + d, count - 1)
            left = jnp.maximum(position - d, 0)
            slot_f = 3 + r * species + s
            slot_b = 3 + (rounds + r) * species + s
            copy_f = pltpu.make_async_remote_copy(
                src_ref=snd_f.at[h, r, s], dst_ref=rcv_f.at[h, r, s],
                send_sem=send_sem.at[h, slot_f], recv_sem=recv_sem.at[h, slot_f],
                device_id=(right, trans, col), device_id_type=MESH,
            )
            copy_b = pltpu.make_async_remote_copy(
                src_ref=snd_b.at[h, r, s], dst_ref=rcv_b.at[h, r, s],
                send_sem=send_sem.at[h, slot_b], recv_sem=recv_sem.at[h, slot_b],
                device_id=(left, trans, col), device_id_type=MESH,
            )
            return copy_f, copy_b, position + d < count, position - d >= 0

        def start_round(s, r):
            snd_f[h, r, s] = sf[s]
            snd_b[h, r, s] = sb[s]
            copy_f, copy_b, has_right, has_left = copies(s, r)
            pl.when(has_right)(copy_f.start)
            pl.when(has_left)(copy_b.start)

        def finish_round(s, r):
            copy_f, copy_b, has_right, has_left = copies(s, r)
            last_round = r == rounds - 1

            @pl.when(has_left)
            def _():
                copy_f.wait_recv()
                got = rcv_f[h, r, s]
                ef[s] += co_ref[2 + r, s] * got
                if not last_round:
                    sf[s] += co_ref[2 + rounds + r, s] * got

            @pl.when(has_right)
            def _():
                copy_b.wait_recv()
                got = rcv_b[h, r, s]
                eb[s] += co_ref[2 + 2 * rounds + r, s] * got
                if not last_round:
                    sb[s] += co_ref[2 + 3 * rounds + r, s] * got

            pl.when(has_right)(copy_f.wait_send)
            pl.when(has_left)(copy_b.wait_send)

        def correct(s):
            g0 = g_ref[0, s]
            g1 = g_ref[1, s]
            before = ef[s]
            after = eb[s]
            r1 = g0 + co_ref[base + 0, s] * before + co_ref[base + 2, s] * after
            r2 = g1 + co_ref[base + 1, s] * before + co_ref[base + 3, s] * after
            top = r1 * co_ref[base + 6, s] + r2 * co_ref[base + 7, s]
            bottom = r1 * co_ref[base + 8, s] + r2 * co_ref[base + 9, s]
            left_coef = sub_ref[s] * (before + co_ref[base + 4, s] * top)
            right_coef = sup_ref[s] * (after + co_ref[base + 5, s] * bottom)
            for z in range(depth):
                o_ref[s, z] = y_ref[s, z] - left_coef * l_ref[s, z] - right_coef * r_ref[s, z]

        for t in range(species + rounds):
            if t < species:
                local_solve(t)
                start_round(t, 0)
            for s in range(min(t, species)):
                r = t - s - 1
                if 0 <= r < rounds:
                    finish_round(s, r)
                    if r + 1 < rounds:
                        start_round(s, r + 1)
                    else:
                        correct(s)


def body(concentration, zone_map, porosity, axial_number, courant, transverse, feed_conc, plan):
    f32 = jnp.float32
    count = lax.axis_size("axial")
    values = concentration[0]
    species, depth, wide, tall = values.shape
    steps = plan.shape[1]
    zone = zone_map[0]
    zone_lo = from_behind(zone[:, tall - 1], "trans", 1)[:, None]
    zone_hi = from_behind(zone[:, 0], "trans", -1)[:, None]

    block = jax.ShapeDtypeStruct((species, depth, wide, tall), f32)
    row = jax.ShapeDtypeStruct((species, wide, tall), f32)
    rounds = len(ROUNDS)
    n_co = 2 + 4 * rounds + 10
    slab = (wide, tall)
    smem = pl.BlockSpec(memory_space=pltpu.SMEM)
    cp, ip, left_spike, right_spike, co, weights, sub, sup = pl.pallas_call(
        functools.partial(setup_kernel, count),
        out_shape=(block, block, block, block, jax.ShapeDtypeStruct((n_co, species, wide, tall), f32),
                   jax.ShapeDtypeStruct((4, species, wide, tall), f32), row, row),
        in_specs=[_vmem()] * 3 + [smem] * 4,
        out_specs=(_vmem(),) * 8,
        scratch_shapes=[pltpu.VMEM((count,) + slab, f32)] * 6 + [pltpu.VMEM((rounds, count) + slab, f32)] * 2,
        cost_estimate=pl.CostEstimate(
            flops=40 * species * depth * wide * tall, transcendentals=0,
            bytes_accessed=4 * 4 * species * depth * wide * tall,
        ),
    )(zone, zone_lo, zone_hi, porosity, axial_number, courant, transverse)

    recycled = (plan[0].astype(f32) + 1.0) * 0.25
    inlet_terms = jnp.stack([(1.0 - recycled) * feed_conc[0][None, :], recycled], 1)

    n_slot = 3 + 2 * rounds * species
    out = pl.pallas_call(
        functools.partial(fused_kernel, count),
        out_shape=block,
        in_specs=[_vmem()] * 9 + [smem],
        out_specs=_vmem(),
        scratch_shapes=[pltpu.VMEM((species, depth) + slab, f32)]
        + [pltpu.VMEM((steps, species) + slab, f32)] * 5
        + [pltpu.VMEM((2, species) + slab, f32)]
        + [pltpu.VMEM((species,) + slab, f32)] * 4
        + [pltpu.VMEM((steps, rounds, species) + slab, f32)] * 4
        + [pltpu.SemaphoreType.DMA((steps, n_slot))] * 2,
        compiler_params=pltpu.CompilerParams(collective_id=0, has_side_effects=True),
        cost_estimate=pl.CostEstimate(
            flops=60 * steps * species * depth * wide * tall, transcendentals=0,
            bytes_accessed=8 * 4 * species * depth * wide * tall,
        ),
    )(values, cp, ip, left_spike, right_spike, co, weights, sub, sup, inlet_terms)
    return out[None]


def solution(mesh):
    in_specs = (
        P("col", None, "axial", None, "trans"),
        P("col", None, "trans"),
        P(),
        P(),
        P(),
        P(),
        P("col", None),
        P("col", None, None),
    )
    out_specs = P("col", None, "axial", None, "trans")
    return jax.shard_map(body, mesh=mesh, in_specs=in_specs, out_specs=out_specs, check_vma=False)
```

```python
import functools

import jax
import jax.numpy as jnp
from jax import lax
from jax.experimental import pallas as pl
from jax.experimental.pallas import tpu as pltpu
from jax.sharding import PartitionSpec as P


def swapped(array, axis, distance):
    return lax.ppermute(array, axis, [(i, i ^ 1 << distance) for i in range(lax.axis_size(axis))])


def from_behind(value, axis, steps):
    count = lax.axis_size(axis)
    initial, last = (max(0, -steps), min(count, count - steps))
    return lax.ppermute(value, axis, [(source, source + steps) for source in range(initial, last)])


def void_map(zone_map, porosity):
    voids = jnp.zeros(zone_map.shape, porosity.dtype)
    for number in range(porosity.shape[0]):
        voids = voids + jnp.where(zone_map == number, porosity[number], 0.0)
    return voids


def _vmem():
    return pl.BlockSpec(memory_space=pltpu.VMEM)


ROUNDS = (1, 2, 4, 8)
MESH = pl.DeviceIdType.MESH


def porosity_of(zone, por_ref):
    voids = jnp.zeros(zone.shape, jnp.float32)
    for number in range(por_ref.shape[0]):
        voids = voids + jnp.where(zone == number, por_ref[number], 0.0)
    return voids


def stencil_weights(voids, voids_lo, voids_hi, tr_ref, w_ref):
    wide, tall = voids.shape
    sublane = lax.broadcasted_iota(jnp.int32, (wide, tall), 0)
    lane = lax.broadcasted_iota(jnp.int32, (wide, tall), 1)
    p_xm = jnp.where(sublane == 0, 0.0, pltpu.roll(voids, 1, 0))
    p_xp = jnp.where(sublane == wide - 1, 0.0, pltpu.roll(voids, wide - 1, 0))
    p_ym = jnp.where(lane == 0, jnp.broadcast_to(voids_lo, (wide, tall)), pltpu.roll(voids, 1, 1))
    p_yp = jnp.where(lane == tall - 1, jnp.broadcast_to(voids_hi, (wide, tall)), pltpu.roll(voids, tall - 1, 1))
    faces = [2.0 * p / (voids + p) for p in (p_xm, p_xp, p_ym, p_yp)]
    for s in range(w_ref.shape[1]):
        for direction in range(4):
            w_ref[direction, s] = tr_ref[s] * faces[direction]


def setup(count, voids, ax_ref, cour_ref, cp_ref, ip_ref, l_ref, r_ref, co_ref, sub_ref, sup_ref,
          qf_ref, qb_ref, mf_ref, mb_ref, cprev_ref, hnext_ref, exf_ref, exb_ref):
    species, depth, wide, tall = cp_ref.shape
    position = lax.axis_index("axial")
    rounds = len(ROUNDS)
    at_outlet = position == count - 1
    for s in range(species):
        dispersion = ax_ref[s] + jnp.zeros((wide, tall), jnp.float32)
        flow_rate = cour_ref[s] / voids
        sub = -(dispersion + flow_rate)
        sup = -dispersion
        mi = 1.0 + 2.0 * dispersion + flow_rate
        me = 1.0 + dispersion + flow_rate
        sub_ref[s] = sub
        sup_ref[s] = sup
        coef = None
        for z in range(depth - 1):
            pivot = mi if z == 0 else mi - sub * coef
            inv = 1.0 / pivot
            coef = sup * inv
            ip_ref[s, z] = inv
            cp_ref[s, z] = coef

        def ends(last):
            inv_last = 1.0 / (last - sub * cp_ref[s, depth - 2])
            down = ip_ref[s, 0]
            downs = [down]
            for z in range(1, depth - 1):
                down = -sub * down * ip_ref[s, z]
                downs.append(down)
            left = -sub * down * inv_last
            left_last = left
            for z in range(depth - 2, -1, -1):
                left = downs[z] - cp_ref[s, z] * left
            right = inv_last
            for z in range(depth - 2, -1, -1):
                right = -cp_ref[s, z] * right
            return left, left_last, right, inv_last

        l0i, l1i, r0i, r1i = ends(mi)
        l0o, l1o, r0o, r1o = ends(me)

        own_last = jnp.where(at_outlet, me, mi)
        inv_last = 1.0 / (own_last - sub * cp_ref[s, depth - 2])
        ip_ref[s, depth - 1] = inv_last
        cp_ref[s, depth - 1] = sup * inv_last
        down = ip_ref[s, 0]
        l_ref[s, 0] = down
        for z in range(1, depth):
            down = -sub * down * ip_ref[s, z]
            l_ref[s, z] = down
        left = down
        right = inv_last
        r_ref[s, depth - 1] = right
        for z in range(depth - 2, -1, -1):
            left = l_ref[s, z] - cp_ref[s, z] * left
            l_ref[s, z] = left
            right = -cp_ref[s, z] * right
            r_ref[s, z] = right

        zero = jnp.zeros_like(sub)
        one = jnp.ones_like(sub)
        inner = (-sub * l0i, -sub * l1i, -sup * r0i, -sup * r1i)
        first = (zero, zero, inner[2], inner[3])
        outlet = (-sub * l0o, -sub * l1o, zero, zero)

        def couplings(j):
            return first if j == 0 else outlet if j == count - 1 else inner

        c_prev = zero
        for j in range(count):
            p0, p1, q0, q1 = couplings(j)
            inv = one if j == 0 else 1.0 / (1.0 - p0 * c_prev)
            qf_ref[j] = p1 * inv
            mf_ref[j] = p1 * c_prev * inv
            cprev_ref[j] = c_prev
            c_prev = q1 + p1 * c_prev * q0 * inv
        h_next = zero
        for j in range(count - 1, -1, -1):
            p0, p1, q0, q1 = couplings(j)
            inv = one if j == count - 1 else 1.0 / (1.0 - q1 * h_next)
            qb_ref[j] = q0 * inv
            mb_ref[j] = q0 * h_next * inv
            hnext_ref[j] = h_next
            h_next = p0 + q0 * h_next * p1 * inv

        for kk in range(count):
            exf_ref[0, kk] = one
            exb_ref[0, kk] = one
        for r in range(rounds - 1):
            d = ROUNDS[r]
            for kk in range(count):
                if kk - d >= 0:
                    exf_ref[r + 1, kk] = exf_ref[r, kk] * qf_ref[kk - d] * exf_ref[r, kk - d]
                else:
                    exf_ref[r + 1, kk] = one
                if kk + d < count:
                    exb_ref[r + 1, kk] = exb_ref[r, kk] * qb_ref[kk + d] * exb_ref[r, kk + d]
                else:
                    exb_ref[r + 1, kk] = one

        co_ref[0, s] = mf_ref[position]
        co_ref[1, s] = mb_ref[position]
        qf_own = qf_ref[position]
        qb_own = qb_ref[position]
        for r in range(rounds):
            wef = exf_ref[r, position]
            web = exb_ref[r, position]
            co_ref[2 + r, s] = wef
            co_ref[2 + rounds + r, s] = qf_own * wef
            co_ref[2 + 2 * rounds + r, s] = web
            co_ref[2 + 3 * rounds + r, s] = qb_own * web
        at_first = position == 0
        at_last = position == count - 1
        p0 = jnp.where(at_first, zero, jnp.where(at_last, outlet[0], inner[0]))
        p1 = jnp.where(at_first, zero, jnp.where(at_last, outlet[1], inner[1]))
        q0 = jnp.where(at_last, zero, inner[2])
        q1 = jnp.where(at_last, zero, inner[3])
        c_own = cprev_ref[position]
        h_own = hnext_ref[position]
        a11 = 1.0 - p0 * c_own
        a12 = -q0 * h_own
        a21 = -p1 * c_own
        a22 = 1.0 - q1 * h_own
        inv_det = 1.0 / (a11 * a22 - a12 * a21)
        base = 2 + 4 * rounds
        for i, value in enumerate(
            (p0, p1, q0, q1, c_own, h_own, a22 * inv_det, -a12 * inv_det, -a21 * inv_det, a11 * inv_det)
        ):
            co_ref[base + i, s] = value


def fused_kernel(count, v_ref, zone_ref, por_ref, ax_ref, cour_ref, tr_ref, inl_ref,
                 o_ref,
                 cp_ref, ip_ref, l_ref, r_ref, co_ref, w_ref, sub_ref, sup_ref,
                 qf_ref, qb_ref, mf_ref, mb_ref, cprev_ref, hnext_ref, exf_ref, exb_ref,
                 vs_ref, vr_ref, vsem_s, vsem_r,
                 y_ref, hs_lo, hs_hi, hr_lo, hr_hi, face_in, g_ref, sf, sb, ef, eb,
                 snd_f, snd_b, rcv_f, rcv_b, send_sem, recv_sem):
    species, depth, wide, tall = v_ref.shape
    steps = inl_ref.shape[0]
    rounds = len(ROUNDS)
    position = lax.axis_index("axial")
    trans = lax.axis_index("trans")
    col = lax.axis_index("col")
    n_trans = lax.axis_size("trans")
    at_inlet = position == 0
    has_lo = trans > 0
    has_hi = trans < n_trans - 1
    lo_dev = (position, jnp.maximum(trans - 1, 0), col)
    hi_dev = (position, jnp.minimum(trans + 1, n_trans - 1), col)
    col_dev = (position, trans, 1 - col)
    lane = lax.broadcasted_iota(jnp.int32, (wide, tall), 1)
    base = 2 + 4 * rounds

    barrier = pltpu.get_barrier_semaphore()

    def greet(cond, device):
        @pl.when(cond)
        def _():
            pl.semaphore_signal(barrier, 1, device_id=device, device_id_type=MESH)

    greet(has_lo, lo_dev)
    greet(has_hi, hi_dev)
    greet(at_inlet, col_dev)
    partners = has_lo.astype(jnp.int32) + has_hi.astype(jnp.int32) + at_inlet.astype(jnp.int32)
    for d in ROUNDS:
        has_right = position + d < count
        has_left = position - d >= 0
        greet(has_right, (jnp.minimum(position + d, count - 1), trans, col))
        greet(has_left, (jnp.maximum(position - d, 0), trans, col))
        partners = partners + has_right.astype(jnp.int32) + has_left.astype(jnp.int32)
    pl.semaphore_wait(barrier, partners)

    zero_rows = jnp.zeros((species, wide, tall), jnp.float32)
    for h in range(steps):
        @pl.when(jnp.logical_not(has_lo))
        def _():
            hr_lo[h] = zero_rows

        @pl.when(jnp.logical_not(has_hi))
        def _():
            hr_hi[h] = zero_rows

        @pl.when(jnp.logical_not(at_inlet))
        def _():
            face_in[h] = zero_rows

    @pl.when(jnp.logical_not(has_lo))
    def _():
        vr_ref[0] = jnp.zeros((wide, tall), jnp.float32)

    @pl.when(jnp.logical_not(has_hi))
    def _():
        vr_ref[1] = jnp.zeros((wide, tall), jnp.float32)

    voids = porosity_of(zone_ref[...], por_ref)
    vs_ref[...] = voids
    voids_up = pltpu.make_async_remote_copy(
        src_ref=vs_ref, dst_ref=vr_ref.at[0], send_sem=vsem_s.at[0], recv_sem=vsem_r.at[0],
        device_id=hi_dev, device_id_type=MESH,
    )
    voids_down = pltpu.make_async_remote_copy(
        src_ref=vs_ref, dst_ref=vr_ref.at[1], send_sem=vsem_s.at[1], recv_sem=vsem_r.at[1],
        device_id=lo_dev, device_id_type=MESH,
    )
    pl.when(has_hi)(voids_up.start)
    pl.when(has_lo)(voids_down.start)

    def exchange_start(h):
        src = v_ref if h == 0 else o_ref
        for s in range(species):
            acc_lo = jnp.zeros((wide, tall), jnp.float32)
            acc_hi = jnp.zeros((wide, tall), jnp.float32)
            for z in range(depth):
                acc_lo = jnp.where(lane == z, jnp.broadcast_to(src[s, z, :, tall - 1 : tall], (wide, tall)), acc_lo)
                acc_hi = jnp.where(lane == z, jnp.broadcast_to(src[s, z, :, 0:1], (wide, tall)), acc_hi)
            hs_lo[h, s] = acc_lo
            hs_hi[h, s] = acc_hi
        copy_lo = pltpu.make_async_remote_copy(
            src_ref=hs_lo.at[h], dst_ref=hr_lo.at[h], send_sem=send_sem.at[h, 0], recv_sem=recv_sem.at[h, 0],
            device_id=hi_dev, device_id_type=MESH,
        )
        copy_hi = pltpu.make_async_remote_copy(
            src_ref=hs_hi.at[h], dst_ref=hr_hi.at[h], send_sem=send_sem.at[h, 1], recv_sem=recv_sem.at[h, 1],
            device_id=lo_dev, device_id_type=MESH,
        )
        copy_face = pltpu.make_async_remote_copy(
            src_ref=src.at[:, 0], dst_ref=face_in.at[h], send_sem=send_sem.at[h, 2], recv_sem=recv_sem.at[h, 2],
            device_id=col_dev, device_id_type=MESH,
        )
        pl.when(has_hi)(copy_lo.start)
        pl.when(has_lo)(copy_hi.start)
        pl.when(at_inlet)(copy_face.start)
        return copy_lo, copy_hi, copy_face

    def exchange_wait(copy_lo, copy_hi, copy_face):
        pl.when(has_lo)(copy_lo.wait_recv)
        pl.when(has_hi)(copy_hi.wait_recv)
        pl.when(at_inlet)(copy_face.wait_recv)
        pl.when(has_hi)(copy_lo.wait_send)
        pl.when(has_lo)(copy_hi.wait_send)
        pl.when(at_inlet)(copy_face.wait_send)

    first_copies = exchange_start(0)
    setup(count, voids, ax_ref, cour_ref, cp_ref, ip_ref, l_ref, r_ref, co_ref, sub_ref, sup_ref,
          qf_ref, qb_ref, mf_ref, mb_ref, cprev_ref, hnext_ref, exf_ref, exb_ref)
    pl.when(has_lo)(voids_up.wait_recv)
    pl.when(has_hi)(voids_down.wait_recv)
    pl.when(has_hi)(voids_up.wait_send)
    pl.when(has_lo)(voids_down.wait_send)
    voids_lo = jnp.where(has_lo, vr_ref[0, :, tall - 1 : tall], 0.0)
    voids_hi = jnp.where(has_hi, vr_ref[1, :, 0:1], 0.0)
    stencil_weights(voids, voids_lo, voids_hi, tr_ref, w_ref)

    for h in range(steps):
        src = v_ref if h == 0 else o_ref
        exchange_wait(*(first_copies if h == 0 else exchange_start(h)))

        for s in range(species):
            wxm = w_ref[0, s]
            wxp = w_ref[1, s]
            wym = w_ref[2, s]
            wyp = w_ref[3, s]
            sub = sub_ref[s]
            down = None
            for z in range(depth):
                v = src[s, z]
                xm = pltpu.roll(v, 1, 0)
                xp = pltpu.roll(v, wide - 1, 0)
                ym = jnp.where(lane == 0, hr_lo[h, s, :, z : z + 1], pltpu.roll(v, 1, 1))
                yp = jnp.where(lane == tall - 1, hr_hi[h, s, :, z : z + 1], pltpu.roll(v, tall - 1, 1))
                moved = v + (wxp * (xp - v) + wxm * (xm - v) + wyp * (yp - v) + wym * (ym - v))
                if z == 0:
                    inlet = inl_ref[h, 0, s] + inl_ref[h, 1, s] * face_in[h, s]
                    moved = moved + jnp.where(at_inlet, -sub * inlet, 0.0)
                    down = moved * ip_ref[s, 0]
                else:
                    down = (moved - sub * down) * ip_ref[s, z]
                y_ref[s, z] = down
            solved = down
            g_ref[1, s] = solved
            for z in range(depth - 2, -1, -1):
                solved = y_ref[s, z] - cp_ref[s, z] * solved
                y_ref[s, z] = solved
            g_ref[0, s] = solved

        g0 = g_ref[0]
        g1 = g_ref[1]
        sf[...] = g1 + co_ref[0] * g0
        sb[...] = g0 + co_ref[1] * g1
        ef[...] = zero_rows
        eb[...] = zero_rows
        for r, d in enumerate(ROUNDS):
            snd_f[h, r] = sf[...]
            snd_b[h, r] = sb[...]
            has_right = position + d < count
            has_left = position - d >= 0
            right = jnp.minimum(position + d, count - 1)
            left = jnp.maximum(position - d, 0)
            copy_f = pltpu.make_async_remote_copy(
                src_ref=snd_f.at[h, r], dst_ref=rcv_f.at[h, r],
                send_sem=send_sem.at[h, 3 + r], recv_sem=recv_sem.at[h, 3 + r],
                device_id=(right, trans, col), device_id_type=MESH,
            )
            copy_b = pltpu.make_async_remote_copy(
                src_ref=snd_b.at[h, r], dst_ref=rcv_b.at[h, r],
                send_sem=send_sem.at[h, 3 + rounds + r], recv_sem=recv_sem.at[h, 3 + rounds + r],
                device_id=(left, trans, col), device_id_type=MESH,
            )
            pl.when(has_right)(copy_f.start)
            pl.when(has_left)(copy_b.start)
            last_round = r == rounds - 1

            @pl.when(has_left)
            def _():
                copy_f.wait_recv()
                got = rcv_f[h, r]
                ef[...] += co_ref[2 + r] * got
                if not last_round:
                    sf[...] += co_ref[2 + rounds + r] * got

            @pl.when(has_right)
            def _():
                copy_b.wait_recv()
                got = rcv_b[h, r]
                eb[...] += co_ref[2 + 2 * rounds + r] * got
                if not last_round:
                    sb[...] += co_ref[2 + 3 * rounds + r] * got

            pl.when(has_right)(copy_f.wait_send)
            pl.when(has_left)(copy_b.wait_send)

        before = ef[...]
        after = eb[...]
        r1 = g0 + co_ref[base + 0] * before + co_ref[base + 2] * after
        r2 = g1 + co_ref[base + 1] * before + co_ref[base + 3] * after
        top = r1 * co_ref[base + 6] + r2 * co_ref[base + 7]
        bottom = r1 * co_ref[base + 8] + r2 * co_ref[base + 9]
        ef[...] = sub_ref[...] * (before + co_ref[base + 4] * top)
        eb[...] = sup_ref[...] * (after + co_ref[base + 5] * bottom)
        for s in range(species):
            left_coef = ef[s]
            right_coef = eb[s]
            for z in range(depth):
                o_ref[s, z] = y_ref[s, z] - left_coef * l_ref[s, z] - right_coef * r_ref[s, z]


def body(concentration, zone_map, porosity, axial_number, courant, transverse, feed_conc, plan):
    f32 = jnp.float32
    count = lax.axis_size("axial")
    values = concentration[0]
    species, depth, wide, tall = values.shape
    steps = plan.shape[1]
    zone = zone_map[0]
    rounds = len(ROUNDS)
    n_co = 2 + 4 * rounds + 10
    slab = (wide, tall)
    block = (species, depth) + slab
    smem = pl.BlockSpec(memory_space=pltpu.SMEM)
    recycled = (plan[0].astype(f32) + 1.0) * 0.25
    inlet_terms = jnp.stack([(1.0 - recycled) * feed_conc[0][None, :], recycled], 1)

    n_slot = 3 + 2 * rounds
    out = pl.pallas_call(
        functools.partial(fused_kernel, count),
        out_shape=jax.ShapeDtypeStruct(block, f32),
        in_specs=[_vmem()] * 2 + [smem] * 5,
        out_specs=_vmem(),
        scratch_shapes=[pltpu.VMEM(block, f32)] * 4
        + [pltpu.VMEM((n_co, species) + slab, f32), pltpu.VMEM((4, species) + slab, f32)]
        + [pltpu.VMEM((species,) + slab, f32)] * 2
        + [pltpu.VMEM((count,) + slab, f32)] * 6
        + [pltpu.VMEM((rounds, count) + slab, f32)] * 2
        + [pltpu.VMEM(slab, f32), pltpu.VMEM((2,) + slab, f32)]
        + [pltpu.SemaphoreType.DMA((2,))] * 2
        + [pltpu.VMEM(block, f32)]
        + [pltpu.VMEM((steps, species) + slab, f32)] * 5
        + [pltpu.VMEM((2, species) + slab, f32)]
        + [pltpu.VMEM((species,) + slab, f32)] * 4
        + [pltpu.VMEM((steps, rounds, species) + slab, f32)] * 4
        + [pltpu.SemaphoreType.DMA((steps, n_slot))] * 2,
        compiler_params=pltpu.CompilerParams(collective_id=0, has_side_effects=True),
        cost_estimate=pl.CostEstimate(
            flops=100 * steps * species * depth * wide * tall, transcendentals=0,
            bytes_accessed=3 * 4 * species * depth * wide * tall,
        ),
    )(values, zone, porosity, axial_number, courant, transverse, inlet_terms)
    return out[None]


def solution(mesh):
    in_specs = (
        P("col", None, "axial", None, "trans"),
        P("col", None, "trans"),
        P(),
        P(),
        P(),
        P(),
        P("col", None),
        P("col", None, None),
    )
    out_specs = P("col", None, "axial", None, "trans")
    return jax.shard_map(body, mesh=mesh, in_specs=in_specs, out_specs=out_specs, check_vma=False)
```

```python
import functools

import jax
import jax.numpy as jnp
from jax import lax
from jax.experimental import pallas as pl
from jax.experimental.pallas import tpu as pltpu
from jax.sharding import PartitionSpec as P


def swapped(array, axis, distance):
    return lax.ppermute(array, axis, [(i, i ^ 1 << distance) for i in range(lax.axis_size(axis))])


def from_behind(value, axis, steps):
    count = lax.axis_size(axis)
    initial, last = (max(0, -steps), min(count, count - steps))
    return lax.ppermute(value, axis, [(source, source + steps) for source in range(initial, last)])


def void_map(zone_map, porosity):
    voids = jnp.zeros(zone_map.shape, porosity.dtype)
    for number in range(porosity.shape[0]):
        voids = voids + jnp.where(zone_map == number, porosity[number], 0.0)
    return voids


def _vmem():
    return pl.BlockSpec(memory_space=pltpu.VMEM)


ROUNDS = (1, 2, 4, 8)
MESH = pl.DeviceIdType.MESH


def porosity_of(zone, por_ref):
    voids = jnp.zeros(zone.shape, jnp.float32)
    for number in range(por_ref.shape[0]):
        voids = voids + jnp.where(zone == number, por_ref[number], 0.0)
    return voids


def stencil_weights(voids, voids_lo, voids_hi, tr_ref, w_ref):
    wide, tall = voids.shape
    sublane = lax.broadcasted_iota(jnp.int32, (wide, tall), 0)
    lane = lax.broadcasted_iota(jnp.int32, (wide, tall), 1)
    p_xm = jnp.where(sublane == 0, 0.0, pltpu.roll(voids, 1, 0))
    p_xp = jnp.where(sublane == wide - 1, 0.0, pltpu.roll(voids, wide - 1, 0))
    p_ym = jnp.where(lane == 0, jnp.broadcast_to(voids_lo, (wide, tall)), pltpu.roll(voids, 1, 1))
    p_yp = jnp.where(lane == tall - 1, jnp.broadcast_to(voids_hi, (wide, tall)), pltpu.roll(voids, tall - 1, 1))
    faces = [2.0 * p / (voids + p) for p in (p_xm, p_xp, p_ym, p_yp)]
    for s in range(w_ref.shape[1]):
        for direction in range(4):
            w_ref[direction, s] = tr_ref[s] * faces[direction]


def setup(count, voids, ax_ref, cour_ref, cp_ref, ip_ref, l_ref, r_ref, co_ref, sub_ref, sup_ref,
          qf_ref, qb_ref, mf_ref, mb_ref, cprev_ref, hnext_ref, exf_ref, exb_ref):
    species, depth, wide, tall = cp_ref.shape
    position = lax.axis_index("axial")
    rounds = len(ROUNDS)
    at_outlet = position == count - 1
    for s in range(species):
        dispersion = ax_ref[s] + jnp.zeros((wide, tall), jnp.float32)
        flow_rate = cour_ref[s] / voids
        sub = -(dispersion + flow_rate)
        sup = -dispersion
        mi = 1.0 + 2.0 * dispersion + flow_rate
        me = 1.0 + dispersion + flow_rate
        sub_ref[s] = sub
        sup_ref[s] = sup
        coef = None
        for z in range(depth - 1):
            pivot = mi if z == 0 else mi - sub * coef
            inv = 1.0 / pivot
            coef = sup * inv
            ip_ref[s, z] = inv
            cp_ref[s, z] = coef

        def ends(last):
            inv_last = 1.0 / (last - sub * cp_ref[s, depth - 2])
            down = ip_ref[s, 0]
            downs = [down]
            for z in range(1, depth - 1):
                down = -sub * down * ip_ref[s, z]
                downs.append(down)
            left = -sub * down * inv_last
            left_last = left
            for z in range(depth - 2, -1, -1):
                left = downs[z] - cp_ref[s, z] * left
            right = inv_last
            for z in range(depth - 2, -1, -1):
                right = -cp_ref[s, z] * right
            return left, left_last, right, inv_last

        l0i, l1i, r0i, r1i = ends(mi)
        l0o, l1o, r0o, r1o = ends(me)

        own_last = jnp.where(at_outlet, me, mi)
        inv_last = 1.0 / (own_last - sub * cp_ref[s, depth - 2])
        ip_ref[s, depth - 1] = inv_last
        cp_ref[s, depth - 1] = sup * inv_last
        down = ip_ref[s, 0]
        l_ref[s, 0] = down
        for z in range(1, depth):
            down = -sub * down * ip_ref[s, z]
            l_ref[s, z] = down
        left = down
        right = inv_last
        r_ref[s, depth - 1] = right
        for z in range(depth - 2, -1, -1):
            left = l_ref[s, z] - cp_ref[s, z] * left
            l_ref[s, z] = left
            right = -cp_ref[s, z] * right
            r_ref[s, z] = right

        zero = jnp.zeros_like(sub)
        one = jnp.ones_like(sub)
        inner = (-sub * l0i, -sub * l1i, -sup * r0i, -sup * r1i)
        first = (zero, zero, inner[2], inner[3])
        outlet = (-sub * l0o, -sub * l1o, zero, zero)

        def couplings(j):
            return first if j == 0 else outlet if j == count - 1 else inner

        c_prev = zero
        for j in range(count):
            p0, p1, q0, q1 = couplings(j)
            inv = one if j == 0 else 1.0 / (1.0 - p0 * c_prev)
            qf_ref[j] = p1 * inv
            mf_ref[j] = p1 * c_prev * inv
            cprev_ref[j] = c_prev
            c_prev = q1 + p1 * c_prev * q0 * inv
        h_next = zero
        for j in range(count - 1, -1, -1):
            p0, p1, q0, q1 = couplings(j)
            inv = one if j == count - 1 else 1.0 / (1.0 - q1 * h_next)
            qb_ref[j] = q0 * inv
            mb_ref[j] = q0 * h_next * inv
            hnext_ref[j] = h_next
            h_next = p0 + q0 * h_next * p1 * inv

        for kk in range(count):
            exf_ref[0, kk] = one
            exb_ref[0, kk] = one
        for r in range(rounds - 1):
            d = ROUNDS[r]
            for kk in range(count):
                if kk - d >= 0:
                    exf_ref[r + 1, kk] = exf_ref[r, kk] * qf_ref[kk - d] * exf_ref[r, kk - d]
                else:
                    exf_ref[r + 1, kk] = one
                if kk + d < count:
                    exb_ref[r + 1, kk] = exb_ref[r, kk] * qb_ref[kk + d] * exb_ref[r, kk + d]
                else:
                    exb_ref[r + 1, kk] = one

        co_ref[0, s] = mf_ref[position]
        co_ref[1, s] = mb_ref[position]
        qf_own = qf_ref[position]
        qb_own = qb_ref[position]
        for r in range(rounds):
            wef = exf_ref[r, position]
            web = exb_ref[r, position]
            co_ref[2 + r, s] = wef
            co_ref[2 + rounds + r, s] = qf_own * wef
            co_ref[2 + 2 * rounds + r, s] = web
            co_ref[2 + 3 * rounds + r, s] = qb_own * web
        at_first = position == 0
        at_last = position == count - 1
        p0 = jnp.where(at_first, zero, jnp.where(at_last, outlet[0], inner[0]))
        p1 = jnp.where(at_first, zero, jnp.where(at_last, outlet[1], inner[1]))
        q0 = jnp.where(at_last, zero, inner[2])
        q1 = jnp.where(at_last, zero, inner[3])
        c_own = cprev_ref[position]
        h_own = hnext_ref[position]
        a11 = 1.0 - p0 * c_own
        a12 = -q0 * h_own
        a21 = -p1 * c_own
        a22 = 1.0 - q1 * h_own
        inv_det = 1.0 / (a11 * a22 - a12 * a21)
        base = 2 + 4 * rounds
        for i, value in enumerate(
            (p0, p1, q0, q1, c_own, h_own, a22 * inv_det, -a12 * inv_det, -a21 * inv_det, a11 * inv_det)
        ):
            co_ref[base + i, s] = value


def fused_kernel(count, v_ref, zone_ref, por_ref, ax_ref, cour_ref, tr_ref, inl_ref,
                 o_ref,
                 cp_ref, ip_ref, l_ref, r_ref, co_ref, w_ref, sub_ref, sup_ref,
                 qf_ref, qb_ref, mf_ref, mb_ref, cprev_ref, hnext_ref, exf_ref, exb_ref,
                 vs_ref, vr_ref, vsem_s, vsem_r,
                 y_ref, hs_lo, hs_hi, hr_lo, hr_hi, face_in, g_ref, sf, sb, ef, eb,
                 snd_f, snd_b, rcv_f, rcv_b, send_sem, recv_sem):
    species, depth, wide, tall = v_ref.shape
    steps = inl_ref.shape[0]
    rounds = len(ROUNDS)
    position = lax.axis_index("axial")
    trans = lax.axis_index("trans")
    col = lax.axis_index("col")
    n_trans = lax.axis_size("trans")
    at_inlet = position == 0
    has_lo = trans > 0
    has_hi = trans < n_trans - 1
    lo_dev = (position, jnp.maximum(trans - 1, 0), col)
    hi_dev = (position, jnp.minimum(trans + 1, n_trans - 1), col)
    col_dev = (position, trans, 1 - col)
    lane = lax.broadcasted_iota(jnp.int32, (wide, tall), 1)
    base = 2 + 4 * rounds

    barrier = pltpu.get_barrier_semaphore()

    def greet(cond, device):
        @pl.when(cond)
        def _():
            pl.semaphore_signal(barrier, 1, device_id=device, device_id_type=MESH)

    greet(has_lo, lo_dev)
    greet(has_hi, hi_dev)
    greet(at_inlet, col_dev)
    partners = has_lo.astype(jnp.int32) + has_hi.astype(jnp.int32) + at_inlet.astype(jnp.int32)
    for d in ROUNDS:
        has_right = position + d < count
        has_left = position - d >= 0
        greet(has_right, (jnp.minimum(position + d, count - 1), trans, col))
        greet(has_left, (jnp.maximum(position - d, 0), trans, col))
        partners = partners + has_right.astype(jnp.int32) + has_left.astype(jnp.int32)
    pl.semaphore_wait(barrier, partners)

    zero_rows = jnp.zeros((species, wide, tall), jnp.float32)
    for h in range(steps):
        @pl.when(jnp.logical_not(has_lo))
        def _():
            hr_lo[h] = zero_rows

        @pl.when(jnp.logical_not(has_hi))
        def _():
            hr_hi[h] = zero_rows

        @pl.when(jnp.logical_not(at_inlet))
        def _():
            face_in[h] = zero_rows

    @pl.when(jnp.logical_not(has_lo))
    def _():
        vr_ref[0] = jnp.zeros((wide, tall), jnp.float32)

    @pl.when(jnp.logical_not(has_hi))
    def _():
        vr_ref[1] = jnp.zeros((wide, tall), jnp.float32)

    voids = porosity_of(zone_ref[...], por_ref)
    vs_ref[...] = voids
    voids_up = pltpu.make_async_remote_copy(
        src_ref=vs_ref, dst_ref=vr_ref.at[0], send_sem=vsem_s.at[0], recv_sem=vsem_r.at[0],
        device_id=hi_dev, device_id_type=MESH,
    )
    voids_down = pltpu.make_async_remote_copy(
        src_ref=vs_ref, dst_ref=vr_ref.at[1], send_sem=vsem_s.at[1], recv_sem=vsem_r.at[1],
        device_id=lo_dev, device_id_type=MESH,
    )
    pl.when(has_hi)(voids_up.start)
    pl.when(has_lo)(voids_down.start)

    def exchange_start(h):
        src = v_ref if h == 0 else o_ref
        for s in range(species):
            acc_lo = jnp.zeros((wide, tall), jnp.float32)
            acc_hi = jnp.zeros((wide, tall), jnp.float32)
            for z in range(depth):
                acc_lo = jnp.where(lane == z, jnp.broadcast_to(src[s, z, :, tall - 1 : tall], (wide, tall)), acc_lo)
                acc_hi = jnp.where(lane == z, jnp.broadcast_to(src[s, z, :, 0:1], (wide, tall)), acc_hi)
            hs_lo[h, s] = acc_lo
            hs_hi[h, s] = acc_hi
        copy_lo = pltpu.make_async_remote_copy(
            src_ref=hs_lo.at[h], dst_ref=hr_lo.at[h], send_sem=send_sem.at[h, 0], recv_sem=recv_sem.at[h, 0],
            device_id=hi_dev, device_id_type=MESH,
        )
        copy_hi = pltpu.make_async_remote_copy(
            src_ref=hs_hi.at[h], dst_ref=hr_hi.at[h], send_sem=send_sem.at[h, 1], recv_sem=recv_sem.at[h, 1],
            device_id=lo_dev, device_id_type=MESH,
        )
        copy_face = pltpu.make_async_remote_copy(
            src_ref=src.at[:, 0], dst_ref=face_in.at[h], send_sem=send_sem.at[h, 2], recv_sem=recv_sem.at[h, 2],
            device_id=col_dev, device_id_type=MESH,
        )
        pl.when(has_hi)(copy_lo.start)
        pl.when(has_lo)(copy_hi.start)
        pl.when(at_inlet)(copy_face.start)
        return copy_lo, copy_hi, copy_face

    def exchange_wait(copy_lo, copy_hi, copy_face):
        pl.when(has_lo)(copy_lo.wait_recv)
        pl.when(has_hi)(copy_hi.wait_recv)
        pl.when(at_inlet)(copy_face.wait_recv)
        pl.when(has_hi)(copy_lo.wait_send)
        pl.when(has_lo)(copy_hi.wait_send)
        pl.when(at_inlet)(copy_face.wait_send)

    first_copies = exchange_start(0)
    setup(count, voids, ax_ref, cour_ref, cp_ref, ip_ref, l_ref, r_ref, co_ref, sub_ref, sup_ref,
          qf_ref, qb_ref, mf_ref, mb_ref, cprev_ref, hnext_ref, exf_ref, exb_ref)
    pl.when(has_lo)(voids_up.wait_recv)
    pl.when(has_hi)(voids_down.wait_recv)
    pl.when(has_hi)(voids_up.wait_send)
    pl.when(has_lo)(voids_down.wait_send)
    voids_lo = jnp.where(has_lo, vr_ref[0, :, tall - 1 : tall], 0.0)
    voids_hi = jnp.where(has_hi, vr_ref[1, :, 0:1], 0.0)
    stencil_weights(voids, voids_lo, voids_hi, tr_ref, w_ref)

    for h in range(steps):
        src = v_ref if h == 0 else o_ref
        exchange_wait(*(first_copies if h == 0 else exchange_start(h)))

        for s in range(species):
            wxm = w_ref[0, s]
            wxp = w_ref[1, s]
            wym = w_ref[2, s]
            wyp = w_ref[3, s]
            sub = sub_ref[s]
            down = None
            for z in range(depth):
                v = src[s, z]
                xm = pltpu.roll(v, 1, 0)
                xp = pltpu.roll(v, wide - 1, 0)
                ym = jnp.where(lane == 0, hr_lo[h, s, :, z : z + 1], pltpu.roll(v, 1, 1))
                yp = jnp.where(lane == tall - 1, hr_hi[h, s, :, z : z + 1], pltpu.roll(v, tall - 1, 1))
                moved = v + (wxp * (xp - v) + wxm * (xm - v) + wyp * (yp - v) + wym * (ym - v))
                if z == 0:
                    inlet = inl_ref[h, 0, s] + inl_ref[h, 1, s] * face_in[h, s]
                    moved = moved + jnp.where(at_inlet, -sub * inlet, 0.0)
                    down = moved * ip_ref[s, 0]
                else:
                    down = (moved - sub * down) * ip_ref[s, z]
                y_ref[s, z] = down
            solved = down
            g_ref[1, s] = solved
            for z in range(depth - 2, -1, -1):
                solved = y_ref[s, z] - cp_ref[s, z] * solved
                y_ref[s, z] = solved
            g_ref[0, s] = solved

        g0 = g_ref[0]
        g1 = g_ref[1]
        sf[...] = g1 + co_ref[0] * g0
        sb[...] = g0 + co_ref[1] * g1
        ef[...] = zero_rows
        eb[...] = zero_rows
        for r in range(rounds):
            snd_f[h, r] = sf[...]
            snd_b[h, r] = sb[...]
            rank = jnp.where(col == 0, r, rounds - 1 - r)
            d = jnp.where(col == 0, ROUNDS[r], ROUNDS[rounds - 1 - r])
            has_right = position + d < count
            has_left = position - d >= 0
            right = jnp.minimum(position + d, count - 1)
            left = jnp.maximum(position - d, 0)
            copy_f = pltpu.make_async_remote_copy(
                src_ref=snd_f.at[h, r], dst_ref=rcv_f.at[h, r],
                send_sem=send_sem.at[h, 3 + r], recv_sem=recv_sem.at[h, 3 + r],
                device_id=(right, trans, col), device_id_type=MESH,
            )
            copy_b = pltpu.make_async_remote_copy(
                src_ref=snd_b.at[h, r], dst_ref=rcv_b.at[h, r],
                send_sem=send_sem.at[h, 3 + rounds + r], recv_sem=recv_sem.at[h, 3 + rounds + r],
                device_id=(left, trans, col), device_id_type=MESH,
            )
            pl.when(has_right)(copy_f.start)
            pl.when(has_left)(copy_b.start)
            last_round = r == rounds - 1

            @pl.when(has_left)
            def _():
                copy_f.wait_recv()
                got = rcv_f[h, r]
                ef[...] += co_ref[2 + rank] * got
                if not last_round:
                    sf[...] += co_ref[2 + rounds + rank] * got

            @pl.when(has_right)
            def _():
                copy_b.wait_recv()
                got = rcv_b[h, r]
                eb[...] += co_ref[2 + 2 * rounds + rank] * got
                if not last_round:
                    sb[...] += co_ref[2 + 3 * rounds + rank] * got

            pl.when(has_right)(copy_f.wait_send)
            pl.when(has_left)(copy_b.wait_send)

        before = ef[...]
        after = eb[...]
        r1 = g0 + co_ref[base + 0] * before + co_ref[base + 2] * after
        r2 = g1 + co_ref[base + 1] * before + co_ref[base + 3] * after
        top = r1 * co_ref[base + 6] + r2 * co_ref[base + 7]
        bottom = r1 * co_ref[base + 8] + r2 * co_ref[base + 9]
        ef[...] = sub_ref[...] * (before + co_ref[base + 4] * top)
        eb[...] = sup_ref[...] * (after + co_ref[base + 5] * bottom)
        for s in range(species):
            left_coef = ef[s]
            right_coef = eb[s]
            for z in range(depth):
                o_ref[s, z] = y_ref[s, z] - left_coef * l_ref[s, z] - right_coef * r_ref[s, z]


def body(concentration, zone_map, porosity, axial_number, courant, transverse, feed_conc, plan):
    f32 = jnp.float32
    count = lax.axis_size("axial")
    values = concentration[0]
    species, depth, wide, tall = values.shape
    steps = plan.shape[1]
    zone = zone_map[0]
    rounds = len(ROUNDS)
    n_co = 2 + 4 * rounds + 10
    slab = (wide, tall)
    block = (species, depth) + slab
    smem = pl.BlockSpec(memory_space=pltpu.SMEM)
    recycled = (plan[0].astype(f32) + 1.0) * 0.25
    inlet_terms = jnp.stack([(1.0 - recycled) * feed_conc[0][None, :], recycled], 1)

    n_slot = 3 + 2 * rounds
    out = pl.pallas_call(
        functools.partial(fused_kernel, count),
        out_shape=jax.ShapeDtypeStruct(block, f32),
        in_specs=[_vmem()] * 2 + [smem] * 5,
        out_specs=_vmem(),
        scratch_shapes=[pltpu.VMEM(block, f32)] * 4
        + [pltpu.VMEM((n_co, species) + slab, f32), pltpu.VMEM((4, species) + slab, f32)]
        + [pltpu.VMEM((species,) + slab, f32)] * 2
        + [pltpu.VMEM((count,) + slab, f32)] * 6
        + [pltpu.VMEM((rounds, count) + slab, f32)] * 2
        + [pltpu.VMEM(slab, f32), pltpu.VMEM((2,) + slab, f32)]
        + [pltpu.SemaphoreType.DMA((2,))] * 2
        + [pltpu.VMEM(block, f32)]
        + [pltpu.VMEM((steps, species) + slab, f32)] * 5
        + [pltpu.VMEM((2, species) + slab, f32)]
        + [pltpu.VMEM((species,) + slab, f32)] * 4
        + [pltpu.VMEM((steps, rounds, species) + slab, f32)] * 4
        + [pltpu.SemaphoreType.DMA((steps, n_slot))] * 2,
        compiler_params=pltpu.CompilerParams(collective_id=0, has_side_effects=True),
        cost_estimate=pl.CostEstimate(
            flops=100 * steps * species * depth * wide * tall, transcendentals=0,
            bytes_accessed=3 * 4 * species * depth * wide * tall,
        ),
    )(values, zone, porosity, axial_number, courant, transverse, inlet_terms)
    return out[None]


def solution(mesh):
    in_specs = (
        P("col", None, "axial", None, "trans"),
        P("col", None, "trans"),
        P(),
        P(),
        P(),
        P(),
        P("col", None),
        P("col", None, None),
    )
    out_specs = P("col", None, "axial", None, "trans")
    return jax.shard_map(body, mesh=mesh, in_specs=in_specs, out_specs=out_specs, check_vma=False)
```

```python
import functools

import jax
import jax.numpy as jnp
from jax import lax
from jax.experimental import pallas as pl
from jax.experimental.pallas import tpu as pltpu
from jax.sharding import PartitionSpec as P


def swapped(array, axis, distance):
    return lax.ppermute(array, axis, [(i, i ^ 1 << distance) for i in range(lax.axis_size(axis))])


def from_behind(value, axis, steps):
    count = lax.axis_size(axis)
    initial, last = (max(0, -steps), min(count, count - steps))
    return lax.ppermute(value, axis, [(source, source + steps) for source in range(initial, last)])


def void_map(zone_map, porosity):
    voids = jnp.zeros(zone_map.shape, porosity.dtype)
    for number in range(porosity.shape[0]):
        voids = voids + jnp.where(zone_map == number, porosity[number], 0.0)
    return voids


def _vmem():
    return pl.BlockSpec(memory_space=pltpu.VMEM)


ROUNDS = (1, 2, 4, 8)
MESH = pl.DeviceIdType.MESH


def porosity_of(zone, por_ref):
    voids = jnp.zeros(zone.shape, jnp.float32)
    for number in range(por_ref.shape[0]):
        voids = voids + jnp.where(zone == number, por_ref[number], 0.0)
    return voids


def stencil_weights(voids, voids_lo, voids_hi, tr_ref, w_ref):
    wide, tall = voids.shape
    sublane = lax.broadcasted_iota(jnp.int32, (wide, tall), 0)
    lane = lax.broadcasted_iota(jnp.int32, (wide, tall), 1)
    p_xm = jnp.where(sublane == 0, 0.0, pltpu.roll(voids, 1, 0))
    p_xp = jnp.where(sublane == wide - 1, 0.0, pltpu.roll(voids, wide - 1, 0))
    p_ym = jnp.where(lane == 0, jnp.broadcast_to(voids_lo, (wide, tall)), pltpu.roll(voids, 1, 1))
    p_yp = jnp.where(lane == tall - 1, jnp.broadcast_to(voids_hi, (wide, tall)), pltpu.roll(voids, tall - 1, 1))
    faces = [2.0 * p / (voids + p) for p in (p_xm, p_xp, p_ym, p_yp)]
    for s in range(w_ref.shape[1]):
        for direction in range(4):
            w_ref[direction, s] = tr_ref[s] * faces[direction]


def setup(count, voids, ax_ref, cour_ref, cp_ref, ip_ref, l_ref, r_ref, co_ref, sub_ref, sup_ref,
          qf_ref, qb_ref, mf_ref, mb_ref, cprev_ref, hnext_ref, exf_ref, exb_ref):
    species, depth, wide, tall = cp_ref.shape
    position = lax.axis_index("axial")
    rounds = len(ROUNDS)
    at_outlet = position == count - 1
    for s in range(species):
        dispersion = ax_ref[s] + jnp.zeros((wide, tall), jnp.float32)
        flow_rate = cour_ref[s] / voids
        sub = -(dispersion + flow_rate)
        sup = -dispersion
        mi = 1.0 + 2.0 * dispersion + flow_rate
        me = 1.0 + dispersion + flow_rate
        sub_ref[s] = sub
        sup_ref[s] = sup
        coef = None
        for z in range(depth - 1):
            pivot = mi if z == 0 else mi - sub * coef
            inv = 1.0 / pivot
            coef = sup * inv
            ip_ref[s, z] = inv
            cp_ref[s, z] = coef

        def ends(last):
            inv_last = 1.0 / (last - sub * cp_ref[s, depth - 2])
            down = ip_ref[s, 0]
            downs = [down]
            for z in range(1, depth - 1):
                down = -sub * down * ip_ref[s, z]
                downs.append(down)
            left = -sub * down * inv_last
            left_last = left
            for z in range(depth - 2, -1, -1):
                left = downs[z] - cp_ref[s, z] * left
            right = inv_last
            for z in range(depth - 2, -1, -1):
                right = -cp_ref[s, z] * right
            return left, left_last, right, inv_last

        l0i, l1i, r0i, r1i = ends(mi)
        l0o, l1o, r0o, r1o = ends(me)

        own_last = jnp.where(at_outlet, me, mi)
        inv_last = 1.0 / (own_last - sub * cp_ref[s, depth - 2])
        ip_ref[s, depth - 1] = inv_last
        cp_ref[s, depth - 1] = sup * inv_last
        down = ip_ref[s, 0]
        l_ref[s, 0] = down
        for z in range(1, depth):
            down = -sub * down * ip_ref[s, z]
            l_ref[s, z] = down
        left = down
        right = inv_last
        r_ref[s, depth - 1] = right
        for z in range(depth - 2, -1, -1):
            left = l_ref[s, z] - cp_ref[s, z] * left
            l_ref[s, z] = left
            right = -cp_ref[s, z] * right
            r_ref[s, z] = right

        zero = jnp.zeros_like(sub)
        one = jnp.ones_like(sub)
        inner = (-sub * l0i, -sub * l1i, -sup * r0i, -sup * r1i)
        first = (zero, zero, inner[2], inner[3])
        outlet = (-sub * l0o, -sub * l1o, zero, zero)

        def couplings(j):
            return first if j == 0 else outlet if j == count - 1 else inner

        c_prev = zero
        for j in range(count):
            p0, p1, q0, q1 = couplings(j)
            inv = one if j == 0 else 1.0 / (1.0 - p0 * c_prev)
            qf_ref[j] = p1 * inv
            mf_ref[j] = p1 * c_prev * inv
            cprev_ref[j] = c_prev
            c_prev = q1 + p1 * c_prev * q0 * inv
        h_next = zero
        for j in range(count - 1, -1, -1):
            p0, p1, q0, q1 = couplings(j)
            inv = one if j == count - 1 else 1.0 / (1.0 - q1 * h_next)
            qb_ref[j] = q0 * inv
            mb_ref[j] = q0 * h_next * inv
            hnext_ref[j] = h_next
            h_next = p0 + q0 * h_next * p1 * inv

        for kk in range(count):
            exf_ref[0, kk] = one
            exb_ref[0, kk] = one
        for r in range(rounds - 1):
            d = ROUNDS[r]
            for kk in range(count):
                if kk - d >= 0:
                    exf_ref[r + 1, kk] = exf_ref[r, kk] * qf_ref[kk - d] * exf_ref[r, kk - d]
                else:
                    exf_ref[r + 1, kk] = one
                if kk + d < count:
                    exb_ref[r + 1, kk] = exb_ref[r, kk] * qb_ref[kk + d] * exb_ref[r, kk + d]
                else:
                    exb_ref[r + 1, kk] = one

        co_ref[0, s] = mf_ref[position]
        co_ref[1, s] = mb_ref[position]
        qf_own = qf_ref[position]
        qb_own = qb_ref[position]
        for r in range(rounds):
            wef = exf_ref[r, position]
            web = exb_ref[r, position]
            co_ref[2 + r, s] = wef
            co_ref[2 + rounds + r, s] = qf_own * wef
            co_ref[2 + 2 * rounds + r, s] = web
            co_ref[2 + 3 * rounds + r, s] = qb_own * web
        at_first = position == 0
        at_last = position == count - 1
        p0 = jnp.where(at_first, zero, jnp.where(at_last, outlet[0], inner[0]))
        p1 = jnp.where(at_first, zero, jnp.where(at_last, outlet[1], inner[1]))
        q0 = jnp.where(at_last, zero, inner[2])
        q1 = jnp.where(at_last, zero, inner[3])
        c_own = cprev_ref[position]
        h_own = hnext_ref[position]
        a11 = 1.0 - p0 * c_own
        a12 = -q0 * h_own
        a21 = -p1 * c_own
        a22 = 1.0 - q1 * h_own
        inv_det = 1.0 / (a11 * a22 - a12 * a21)
        base = 2 + 4 * rounds
        for i, value in enumerate(
            (p0, p1, q0, q1, c_own, h_own, a22 * inv_det, -a12 * inv_det, -a21 * inv_det, a11 * inv_det)
        ):
            co_ref[base + i, s] = value


def fused_kernel(count, v_ref, zone_ref, por_ref, ax_ref, cour_ref, tr_ref, plan_ref, feed_ref,
                 o_ref,
                 cp_ref, ip_ref, l_ref, r_ref, co_ref, w_ref, sub_ref, sup_ref,
                 qf_ref, qb_ref, mf_ref, mb_ref, cprev_ref, hnext_ref, exf_ref, exb_ref,
                 vs_ref, vr_ref, vsem_s, vsem_r,
                 y_ref, hs_lo, hs_hi, hr_lo, hr_hi, face_in, g_ref, sf, sb, ef, eb,
                 snd_f, snd_b, rcv_f, rcv_b, send_sem, recv_sem):
    species, depth, wide, tall = v_ref.shape
    steps = plan_ref.shape[0]
    rounds = len(ROUNDS)
    position = lax.axis_index("axial")
    trans = lax.axis_index("trans")
    col = lax.axis_index("col")
    n_trans = lax.axis_size("trans")
    at_inlet = position == 0
    has_lo = trans > 0
    has_hi = trans < n_trans - 1
    lo_dev = (position, jnp.maximum(trans - 1, 0), col)
    hi_dev = (position, jnp.minimum(trans + 1, n_trans - 1), col)
    col_dev = (position, trans, 1 - col)
    lane = lax.broadcasted_iota(jnp.int32, (wide, tall), 1)
    base = 2 + 4 * rounds

    barrier = pltpu.get_barrier_semaphore()

    def greet(cond, device):
        @pl.when(cond)
        def _():
            pl.semaphore_signal(barrier, 1, device_id=device, device_id_type=MESH)

    greet(has_lo, lo_dev)
    greet(has_hi, hi_dev)
    greet(at_inlet, col_dev)
    partners = has_lo.astype(jnp.int32) + has_hi.astype(jnp.int32) + at_inlet.astype(jnp.int32)
    for d in ROUNDS:
        has_right = position + d < count
        has_left = position - d >= 0
        greet(has_right, (jnp.minimum(position + d, count - 1), trans, col))
        greet(has_left, (jnp.maximum(position - d, 0), trans, col))
        partners = partners + has_right.astype(jnp.int32) + has_left.astype(jnp.int32)
    pl.semaphore_wait(barrier, partners)

    zero_rows = jnp.zeros((species, wide, tall), jnp.float32)
    for h in range(steps):
        @pl.when(jnp.logical_not(has_lo))
        def _():
            hr_lo[h] = zero_rows

        @pl.when(jnp.logical_not(has_hi))
        def _():
            hr_hi[h] = zero_rows

        @pl.when(jnp.logical_not(at_inlet))
        def _():
            face_in[h] = zero_rows

    @pl.when(jnp.logical_not(has_lo))
    def _():
        vr_ref[0] = jnp.zeros((wide, tall), jnp.float32)

    @pl.when(jnp.logical_not(has_hi))
    def _():
        vr_ref[1] = jnp.zeros((wide, tall), jnp.float32)

    voids = porosity_of(zone_ref[...], por_ref)
    vs_ref[...] = voids
    voids_up = pltpu.make_async_remote_copy(
        src_ref=vs_ref, dst_ref=vr_ref.at[0], send_sem=vsem_s.at[0], recv_sem=vsem_r.at[0],
        device_id=hi_dev, device_id_type=MESH,
    )
    voids_down = pltpu.make_async_remote_copy(
        src_ref=vs_ref, dst_ref=vr_ref.at[1], send_sem=vsem_s.at[1], recv_sem=vsem_r.at[1],
        device_id=lo_dev, device_id_type=MESH,
    )
    pl.when(has_hi)(voids_up.start)
    pl.when(has_lo)(voids_down.start)

    def exchange_start(h):
        src = v_ref if h == 0 else o_ref
        for s in range(species):
            acc_lo = jnp.zeros((wide, tall), jnp.float32)
            acc_hi = jnp.zeros((wide, tall), jnp.float32)
            for z in range(depth):
                acc_lo = jnp.where(lane == z, jnp.broadcast_to(src[s, z, :, tall - 1 : tall], (wide, tall)), acc_lo)
                acc_hi = jnp.where(lane == z, jnp.broadcast_to(src[s, z, :, 0:1], (wide, tall)), acc_hi)
            hs_lo[h, s] = acc_lo
            hs_hi[h, s] = acc_hi
        copy_lo = pltpu.make_async_remote_copy(
            src_ref=hs_lo.at[h], dst_ref=hr_lo.at[h], send_sem=send_sem.at[h, 0], recv_sem=recv_sem.at[h, 0],
            device_id=hi_dev, device_id_type=MESH,
        )
        copy_hi = pltpu.make_async_remote_copy(
            src_ref=hs_hi.at[h], dst_ref=hr_hi.at[h], send_sem=send_sem.at[h, 1], recv_sem=recv_sem.at[h, 1],
            device_id=lo_dev, device_id_type=MESH,
        )
        copy_face = pltpu.make_async_remote_copy(
            src_ref=src.at[:, 0], dst_ref=face_in.at[h], send_sem=send_sem.at[h, 2], recv_sem=recv_sem.at[h, 2],
            device_id=col_dev, device_id_type=MESH,
        )
        pl.when(has_hi)(copy_lo.start)
        pl.when(has_lo)(copy_hi.start)
        pl.when(at_inlet)(copy_face.start)
        return copy_lo, copy_hi, copy_face

    def exchange_wait(copy_lo, copy_hi, copy_face):
        pl.when(has_lo)(copy_lo.wait_recv)
        pl.when(has_hi)(copy_hi.wait_recv)
        pl.when(has_hi)(copy_lo.wait_send)
        pl.when(has_lo)(copy_hi.wait_send)

    first_copies = exchange_start(0)
    setup(count, voids, ax_ref, cour_ref, cp_ref, ip_ref, l_ref, r_ref, co_ref, sub_ref, sup_ref,
          qf_ref, qb_ref, mf_ref, mb_ref, cprev_ref, hnext_ref, exf_ref, exb_ref)
    pl.when(has_lo)(voids_up.wait_recv)
    pl.when(has_hi)(voids_down.wait_recv)
    pl.when(has_hi)(voids_up.wait_send)
    pl.when(has_lo)(voids_down.wait_send)
    voids_lo = jnp.where(has_lo, vr_ref[0, :, tall - 1 : tall], 0.0)
    voids_hi = jnp.where(has_hi, vr_ref[1, :, 0:1], 0.0)
    stencil_weights(voids, voids_lo, voids_hi, tr_ref, w_ref)

    for h in range(steps):
        src = v_ref if h == 0 else o_ref
        copy_lo, copy_hi, copy_face = first_copies if h == 0 else exchange_start(h)
        exchange_wait(copy_lo, copy_hi, copy_face)

        for s in range(species):
            wxm = w_ref[0, s]
            wxp = w_ref[1, s]
            wym = w_ref[2, s]
            wyp = w_ref[3, s]
            sub = sub_ref[s]
            down = None
            for z in range(depth):
                v = src[s, z]
                xm = pltpu.roll(v, 1, 0)
                xp = pltpu.roll(v, wide - 1, 0)
                ym = jnp.where(lane == 0, hr_lo[h, s, :, z : z + 1], pltpu.roll(v, 1, 1))
                yp = jnp.where(lane == tall - 1, hr_hi[h, s, :, z : z + 1], pltpu.roll(v, tall - 1, 1))
                moved = v + (wxp * (xp - v) + wxm * (xm - v) + wyp * (yp - v) + wym * (ym - v))
                if z == 0:
                    down = moved * ip_ref[s, 0]
                else:
                    down = (moved - sub * down) * ip_ref[s, z]
                y_ref[s, z] = down
            solved = down
            g_ref[1, s] = solved
            for z in range(depth - 2, -1, -1):
                solved = y_ref[s, z] - cp_ref[s, z] * solved
                y_ref[s, z] = solved
            g_ref[0, s] = solved

        pl.when(at_inlet)(copy_face.wait_recv)
        pl.when(at_inlet)(copy_face.wait_send)
        for s in range(species):
            recycled = (plan_ref[h, s].astype(jnp.float32) + 1.0) * 0.25
            inlet = (1.0 - recycled) * feed_ref[s] + recycled * face_in[h, s]
            entry = jnp.where(at_inlet, -sub_ref[s] * inlet, 0.0)
            g_ref[2, s] = entry
            g_ref[0, s] = g_ref[0, s] + entry * l_ref[s, 0]
            g_ref[1, s] = g_ref[1, s] + entry * l_ref[s, depth - 1]
        g0 = g_ref[0]
        g1 = g_ref[1]
        sf[...] = g1 + co_ref[0] * g0
        sb[...] = g0 + co_ref[1] * g1
        ef[...] = zero_rows
        eb[...] = zero_rows
        for r in range(rounds):
            snd_f[h, r] = sf[...]
            snd_b[h, r] = sb[...]
            rank = jnp.where(col == 0, r, rounds - 1 - r)
            d = jnp.where(col == 0, ROUNDS[r], ROUNDS[rounds - 1 - r])
            has_right = position + d < count
            has_left = position - d >= 0
            right = jnp.minimum(position + d, count - 1)
            left = jnp.maximum(position - d, 0)
            copy_f = pltpu.make_async_remote_copy(
                src_ref=snd_f.at[h, r], dst_ref=rcv_f.at[h, r],
                send_sem=send_sem.at[h, 3 + r], recv_sem=recv_sem.at[h, 3 + r],
                device_id=(right, trans, col), device_id_type=MESH,
            )
            copy_b = pltpu.make_async_remote_copy(
                src_ref=snd_b.at[h, r], dst_ref=rcv_b.at[h, r],
                send_sem=send_sem.at[h, 3 + rounds + r], recv_sem=recv_sem.at[h, 3 + rounds + r],
                device_id=(left, trans, col), device_id_type=MESH,
            )
            pl.when(has_right)(copy_f.start)
            pl.when(has_left)(copy_b.start)
            last_round = r == rounds - 1

            @pl.when(has_left)
            def _():
                copy_f.wait_recv()
                got = rcv_f[h, r]
                ef[...] += co_ref[2 + rank] * got
                if not last_round:
                    sf[...] += co_ref[2 + rounds + rank] * got

            @pl.when(has_right)
            def _():
                copy_b.wait_recv()
                got = rcv_b[h, r]
                eb[...] += co_ref[2 + 2 * rounds + rank] * got
                if not last_round:
                    sb[...] += co_ref[2 + 3 * rounds + rank] * got

            pl.when(has_right)(copy_f.wait_send)
            pl.when(has_left)(copy_b.wait_send)

        before = ef[...]
        after = eb[...]
        r1 = g0 + co_ref[base + 0] * before + co_ref[base + 2] * after
        r2 = g1 + co_ref[base + 1] * before + co_ref[base + 3] * after
        top = r1 * co_ref[base + 6] + r2 * co_ref[base + 7]
        bottom = r1 * co_ref[base + 8] + r2 * co_ref[base + 9]
        ef[...] = sub_ref[...] * (before + co_ref[base + 4] * top)
        eb[...] = sup_ref[...] * (after + co_ref[base + 5] * bottom)
        for s in range(species):
            left_coef = ef[s] - g_ref[2, s]
            right_coef = eb[s]
            for z in range(depth):
                o_ref[s, z] = y_ref[s, z] - left_coef * l_ref[s, z] - right_coef * r_ref[s, z]


def body(concentration, zone_map, porosity, axial_number, courant, transverse, feed_conc, plan):
    f32 = jnp.float32
    count = lax.axis_size("axial")
    values = concentration[0]
    species, depth, wide, tall = values.shape
    steps = plan.shape[1]
    zone = zone_map[0]
    rounds = len(ROUNDS)
    n_co = 2 + 4 * rounds + 10
    slab = (wide, tall)
    block = (species, depth) + slab
    smem = pl.BlockSpec(memory_space=pltpu.SMEM)

    n_slot = 3 + 2 * rounds
    out = pl.pallas_call(
        functools.partial(fused_kernel, count),
        out_shape=jax.ShapeDtypeStruct(block, f32),
        in_specs=[_vmem()] * 2 + [smem] * 6,
        out_specs=_vmem(),
        scratch_shapes=[pltpu.VMEM(block, f32)] * 4
        + [pltpu.VMEM((n_co, species) + slab, f32), pltpu.VMEM((4, species) + slab, f32)]
        + [pltpu.VMEM((species,) + slab, f32)] * 2
        + [pltpu.VMEM((count,) + slab, f32)] * 6
        + [pltpu.VMEM((rounds, count) + slab, f32)] * 2
        + [pltpu.VMEM(slab, f32), pltpu.VMEM((2,) + slab, f32)]
        + [pltpu.SemaphoreType.DMA((2,))] * 2
        + [pltpu.VMEM(block, f32)]
        + [pltpu.VMEM((steps, species) + slab, f32)] * 5
        + [pltpu.VMEM((3, species) + slab, f32)]
        + [pltpu.VMEM((species,) + slab, f32)] * 4
        + [pltpu.VMEM((steps, rounds, species) + slab, f32)] * 4
        + [pltpu.SemaphoreType.DMA((steps, n_slot))] * 2,
        compiler_params=pltpu.CompilerParams(collective_id=0, has_side_effects=True),
        cost_estimate=pl.CostEstimate(
            flops=100 * steps * species * depth * wide * tall, transcendentals=0,
            bytes_accessed=3 * 4 * species * depth * wide * tall,
        ),
    )(values, zone, porosity, axial_number, courant, transverse, plan[0], feed_conc[0])
    return out[None]


def solution(mesh):
    in_specs = (
        P("col", None, "axial", None, "trans"),
        P("col", None, "trans"),
        P(),
        P(),
        P(),
        P(),
        P("col", None),
        P("col", None, None),
    )
    out_specs = P("col", None, "axial", None, "trans")
    return jax.shard_map(body, mesh=mesh, in_specs=in_specs, out_specs=out_specs, check_vma=False)
```

```python
import functools

import jax
import jax.numpy as jnp
from jax import lax
from jax.experimental import pallas as pl
from jax.experimental.pallas import tpu as pltpu
from jax.sharding import PartitionSpec as P


def swapped(array, axis, distance):
    return lax.ppermute(array, axis, [(i, i ^ 1 << distance) for i in range(lax.axis_size(axis))])


def from_behind(value, axis, steps):
    count = lax.axis_size(axis)
    initial, last = (max(0, -steps), min(count, count - steps))
    return lax.ppermute(value, axis, [(source, source + steps) for source in range(initial, last)])


def void_map(zone_map, porosity):
    voids = jnp.zeros(zone_map.shape, porosity.dtype)
    for number in range(porosity.shape[0]):
        voids = voids + jnp.where(zone_map == number, porosity[number], 0.0)
    return voids


def _vmem():
    return pl.BlockSpec(memory_space=pltpu.VMEM)


ROUNDS = (1, 2, 4, 8)
MESH = pl.DeviceIdType.MESH


def porosity_of(zone, por_ref):
    voids = jnp.zeros(zone.shape, jnp.float32)
    for number in range(por_ref.shape[0]):
        voids = voids + jnp.where(zone == number, por_ref[number], 0.0)
    return voids


def stencil_weights(voids, voids_lo, voids_hi, tr_ref, w_ref):
    wide, tall = voids.shape
    sublane = lax.broadcasted_iota(jnp.int32, (wide, tall), 0)
    lane = lax.broadcasted_iota(jnp.int32, (wide, tall), 1)
    p_xm = jnp.where(sublane == 0, 0.0, pltpu.roll(voids, 1, 0))
    p_xp = jnp.where(sublane == wide - 1, 0.0, pltpu.roll(voids, wide - 1, 0))
    p_ym = jnp.where(lane == 0, jnp.broadcast_to(voids_lo, (wide, tall)), pltpu.roll(voids, 1, 1))
    p_yp = jnp.where(lane == tall - 1, jnp.broadcast_to(voids_hi, (wide, tall)), pltpu.roll(voids, tall - 1, 1))
    faces = [2.0 * p / (voids + p) for p in (p_xm, p_xp, p_ym, p_yp)]
    for s in range(w_ref.shape[1]):
        scaled = [tr_ref[s] * face for face in faces]
        for direction in range(4):
            w_ref[1 + direction, s] = scaled[direction]
        w_ref[0, s] = 1.0 - (scaled[0] + scaled[1] + scaled[2] + scaled[3])


def setup(count, voids, ax_ref, cour_ref, cp_ref, ip_ref, l_ref, r_ref, co_ref, sub_ref, sup_ref,
          qf_ref, qb_ref, mf_ref, mb_ref, cprev_ref, hnext_ref, exf_ref, exb_ref):
    species, depth, wide, tall = cp_ref.shape
    position = lax.axis_index("axial")
    rounds = len(ROUNDS)
    at_outlet = position == count - 1
    for s in range(species):
        dispersion = ax_ref[s] + jnp.zeros((wide, tall), jnp.float32)
        flow_rate = cour_ref[s] / voids
        sub = -(dispersion + flow_rate)
        sup = -dispersion
        mi = 1.0 + 2.0 * dispersion + flow_rate
        me = 1.0 + dispersion + flow_rate
        sub_ref[s] = sub
        sup_ref[s] = sup
        coef = None
        for z in range(depth - 1):
            pivot = mi if z == 0 else mi - sub * coef
            inv = 1.0 / pivot
            coef = sup * inv
            ip_ref[s, z] = inv
            cp_ref[s, z] = coef

        def ends(last):
            inv_last = 1.0 / (last - sub * cp_ref[s, depth - 2])
            down = ip_ref[s, 0]
            downs = [down]
            for z in range(1, depth - 1):
                down = -sub * down * ip_ref[s, z]
                downs.append(down)
            left = -sub * down * inv_last
            left_last = left
            for z in range(depth - 2, -1, -1):
                left = downs[z] - cp_ref[s, z] * left
            right = inv_last
            for z in range(depth - 2, -1, -1):
                right = -cp_ref[s, z] * right
            return left, left_last, right, inv_last

        l0i, l1i, r0i, r1i = ends(mi)
        l0o, l1o, r0o, r1o = ends(me)

        own_last = jnp.where(at_outlet, me, mi)
        inv_last = 1.0 / (own_last - sub * cp_ref[s, depth - 2])
        ip_ref[s, depth - 1] = inv_last
        cp_ref[s, depth - 1] = sup * inv_last
        down = ip_ref[s, 0]
        l_ref[s, 0] = down
        for z in range(1, depth):
            down = -sub * down * ip_ref[s, z]
            l_ref[s, z] = down
        left = down
        right = inv_last
        r_ref[s, depth - 1] = right
        for z in range(depth - 2, -1, -1):
            left = l_ref[s, z] - cp_ref[s, z] * left
            l_ref[s, z] = left
            right = -cp_ref[s, z] * right
            r_ref[s, z] = right

        zero = jnp.zeros_like(sub)
        one = jnp.ones_like(sub)
        inner = (-sub * l0i, -sub * l1i, -sup * r0i, -sup * r1i)
        first = (zero, zero, inner[2], inner[3])
        outlet = (-sub * l0o, -sub * l1o, zero, zero)

        def couplings(j):
            return first if j == 0 else outlet if j == count - 1 else inner

        c_prev = zero
        for j in range(count):
            p0, p1, q0, q1 = couplings(j)
            inv = one if j == 0 else 1.0 / (1.0 - p0 * c_prev)
            qf_ref[j] = p1 * inv
            mf_ref[j] = p1 * c_prev * inv
            cprev_ref[j] = c_prev
            c_prev = q1 + p1 * c_prev * q0 * inv
        h_next = zero
        for j in range(count - 1, -1, -1):
            p0, p1, q0, q1 = couplings(j)
            inv = one if j == count - 1 else 1.0 / (1.0 - q1 * h_next)
            qb_ref[j] = q0 * inv
            mb_ref[j] = q0 * h_next * inv
            hnext_ref[j] = h_next
            h_next = p0 + q0 * h_next * p1 * inv

        for kk in range(count):
            exf_ref[0, kk] = one
            exb_ref[0, kk] = one
        for r in range(rounds - 1):
            d = ROUNDS[r]
            for kk in range(count):
                if kk - d >= 0:
                    exf_ref[r + 1, kk] = exf_ref[r, kk] * qf_ref[kk - d] * exf_ref[r, kk - d]
                else:
                    exf_ref[r + 1, kk] = one
                if kk + d < count:
                    exb_ref[r + 1, kk] = exb_ref[r, kk] * qb_ref[kk + d] * exb_ref[r, kk + d]
                else:
                    exb_ref[r + 1, kk] = one

        co_ref[0, s] = mf_ref[position]
        co_ref[1, s] = mb_ref[position]
        qf_own = qf_ref[position]
        qb_own = qb_ref[position]
        for r in range(rounds):
            wef = exf_ref[r, position]
            web = exb_ref[r, position]
            co_ref[2 + r, s] = wef
            co_ref[2 + rounds + r, s] = qf_own * wef
            co_ref[2 + 2 * rounds + r, s] = web
            co_ref[2 + 3 * rounds + r, s] = qb_own * web
        at_first = position == 0
        at_last = position == count - 1
        p0 = jnp.where(at_first, zero, jnp.where(at_last, outlet[0], inner[0]))
        p1 = jnp.where(at_first, zero, jnp.where(at_last, outlet[1], inner[1]))
        q0 = jnp.where(at_last, zero, inner[2])
        q1 = jnp.where(at_last, zero, inner[3])
        c_own = cprev_ref[position]
        h_own = hnext_ref[position]
        a11 = 1.0 - p0 * c_own
        a12 = -q0 * h_own
        a21 = -p1 * c_own
        a22 = 1.0 - q1 * h_own
        inv_det = 1.0 / (a11 * a22 - a12 * a21)
        base = 2 + 4 * rounds
        for i, value in enumerate(
            (p0, p1, q0, q1, c_own, h_own, a22 * inv_det, -a12 * inv_det, -a21 * inv_det, a11 * inv_det)
        ):
            co_ref[base + i, s] = value


def fused_kernel(count, v_ref, zone_ref, por_ref, ax_ref, cour_ref, tr_ref, plan_ref, feed_ref,
                 o_ref,
                 cp_ref, ip_ref, l_ref, r_ref, co_ref, w_ref, sub_ref, sup_ref,
                 qf_ref, qb_ref, mf_ref, mb_ref, cprev_ref, hnext_ref, exf_ref, exb_ref,
                 vs_ref, vr_ref, vsem_s, vsem_r,
                 y_ref, hs_lo, hs_hi, hr_lo, hr_hi, face_in, g_ref, sf, sb, ef, eb,
                 snd_f, snd_b, rcv_f, rcv_b, send_sem, recv_sem):
    species, depth, wide, tall = v_ref.shape
    steps = plan_ref.shape[0]
    rounds = len(ROUNDS)
    position = lax.axis_index("axial")
    trans = lax.axis_index("trans")
    col = lax.axis_index("col")
    n_trans = lax.axis_size("trans")
    at_inlet = position == 0
    has_lo = trans > 0
    has_hi = trans < n_trans - 1
    lo_dev = (position, jnp.maximum(trans - 1, 0), col)
    hi_dev = (position, jnp.minimum(trans + 1, n_trans - 1), col)
    col_dev = (position, trans, 1 - col)
    lane = lax.broadcasted_iota(jnp.int32, (wide, tall), 1)
    base = 2 + 4 * rounds

    barrier = pltpu.get_barrier_semaphore()

    def greet(cond, device):
        @pl.when(cond)
        def _():
            pl.semaphore_signal(barrier, 1, device_id=device, device_id_type=MESH)

    greet(has_lo, lo_dev)
    greet(has_hi, hi_dev)
    greet(at_inlet, col_dev)
    partners = has_lo.astype(jnp.int32) + has_hi.astype(jnp.int32) + at_inlet.astype(jnp.int32)
    for d in ROUNDS:
        has_right = position + d < count
        has_left = position - d >= 0
        greet(has_right, (jnp.minimum(position + d, count - 1), trans, col))
        greet(has_left, (jnp.maximum(position - d, 0), trans, col))
        partners = partners + has_right.astype(jnp.int32) + has_left.astype(jnp.int32)
    pl.semaphore_wait(barrier, partners)

    zero_rows = jnp.zeros((species, wide, tall), jnp.float32)
    for h in range(steps):
        @pl.when(jnp.logical_not(has_lo))
        def _():
            hr_lo[h] = jnp.zeros((wide, tall), jnp.float32)

        @pl.when(jnp.logical_not(has_hi))
        def _():
            hr_hi[h] = jnp.zeros((wide, tall), jnp.float32)

        @pl.when(jnp.logical_not(at_inlet))
        def _():
            face_in[h] = zero_rows

    @pl.when(jnp.logical_not(has_lo))
    def _():
        vr_ref[0] = jnp.zeros((wide, tall), jnp.float32)

    @pl.when(jnp.logical_not(has_hi))
    def _():
        vr_ref[1] = jnp.zeros((wide, tall), jnp.float32)

    voids = porosity_of(zone_ref[...], por_ref)
    vs_ref[...] = voids
    voids_up = pltpu.make_async_remote_copy(
        src_ref=vs_ref, dst_ref=vr_ref.at[0], send_sem=vsem_s.at[0], recv_sem=vsem_r.at[0],
        device_id=hi_dev, device_id_type=MESH,
    )
    voids_down = pltpu.make_async_remote_copy(
        src_ref=vs_ref, dst_ref=vr_ref.at[1], send_sem=vsem_s.at[1], recv_sem=vsem_r.at[1],
        device_id=lo_dev, device_id_type=MESH,
    )
    pl.when(has_hi)(voids_up.start)
    pl.when(has_lo)(voids_down.start)

    def exchange_start(h):
        src = v_ref if h == 0 else o_ref
        acc_lo = jnp.zeros((wide, tall), jnp.float32)
        acc_hi = jnp.zeros((wide, tall), jnp.float32)
        for s in range(species):
            for z in range(depth):
                at = s * depth + z
                acc_lo = jnp.where(lane == at, jnp.broadcast_to(src[s, z, :, tall - 1 : tall], (wide, tall)), acc_lo)
                acc_hi = jnp.where(lane == at, jnp.broadcast_to(src[s, z, :, 0:1], (wide, tall)), acc_hi)
        hs_lo[h] = acc_lo
        hs_hi[h] = acc_hi
        copy_lo = pltpu.make_async_remote_copy(
            src_ref=hs_lo.at[h], dst_ref=hr_lo.at[h], send_sem=send_sem.at[h, 0], recv_sem=recv_sem.at[h, 0],
            device_id=hi_dev, device_id_type=MESH,
        )
        copy_hi = pltpu.make_async_remote_copy(
            src_ref=hs_hi.at[h], dst_ref=hr_hi.at[h], send_sem=send_sem.at[h, 1], recv_sem=recv_sem.at[h, 1],
            device_id=lo_dev, device_id_type=MESH,
        )
        copy_face = pltpu.make_async_remote_copy(
            src_ref=src.at[:, 0], dst_ref=face_in.at[h], send_sem=send_sem.at[h, 2], recv_sem=recv_sem.at[h, 2],
            device_id=col_dev, device_id_type=MESH,
        )
        pl.when(has_hi)(copy_lo.start)
        pl.when(has_lo)(copy_hi.start)
        pl.when(at_inlet)(copy_face.start)
        return copy_lo, copy_hi, copy_face

    def exchange_wait(copy_lo, copy_hi, copy_face):
        pl.when(has_lo)(copy_lo.wait_recv)
        pl.when(has_hi)(copy_hi.wait_recv)
        pl.when(has_hi)(copy_lo.wait_send)
        pl.when(has_lo)(copy_hi.wait_send)

    first_copies = exchange_start(0)
    setup(count, voids, ax_ref, cour_ref, cp_ref, ip_ref, l_ref, r_ref, co_ref, sub_ref, sup_ref,
          qf_ref, qb_ref, mf_ref, mb_ref, cprev_ref, hnext_ref, exf_ref, exb_ref)
    pl.when(has_lo)(voids_up.wait_recv)
    pl.when(has_hi)(voids_down.wait_recv)
    pl.when(has_hi)(voids_up.wait_send)
    pl.when(has_lo)(voids_down.wait_send)
    voids_lo = jnp.where(has_lo, vr_ref[0, :, tall - 1 : tall], 0.0)
    voids_hi = jnp.where(has_hi, vr_ref[1, :, 0:1], 0.0)
    stencil_weights(voids, voids_lo, voids_hi, tr_ref, w_ref)

    for h in range(steps):
        src = v_ref if h == 0 else o_ref
        copy_lo, copy_hi, copy_face = first_copies if h == 0 else exchange_start(h)
        exchange_wait(copy_lo, copy_hi, copy_face)

        for s in range(species):
            w0 = w_ref[0, s]
            wxm = w_ref[1, s]
            wxp = w_ref[2, s]
            wym = w_ref[3, s]
            wyp = w_ref[4, s]
            sub = sub_ref[s]
            down = None
            for z in range(depth):
                v = src[s, z]
                xm = pltpu.roll(v, 1, 0)
                xp = pltpu.roll(v, wide - 1, 0)
                at = s * depth + z
                ym = jnp.where(lane == 0, hr_lo[h, :, at : at + 1], pltpu.roll(v, 1, 1))
                yp = jnp.where(lane == tall - 1, hr_hi[h, :, at : at + 1], pltpu.roll(v, tall - 1, 1))
                moved = w0 * v + ((wxp * xp + wxm * xm) + (wyp * yp + wym * ym))
                if z == 0:
                    down = moved * ip_ref[s, 0]
                else:
                    down = (moved - sub * down) * ip_ref[s, z]
                y_ref[s, z] = down
            solved = down
            g_ref[1, s] = solved
            for z in range(depth - 2, -1, -1):
                solved = y_ref[s, z] - cp_ref[s, z] * solved
                y_ref[s, z] = solved
            g_ref[0, s] = solved

        pl.when(at_inlet)(copy_face.wait_recv)
        pl.when(at_inlet)(copy_face.wait_send)
        for s in range(species):
            recycled = (plan_ref[h, s].astype(jnp.float32) + 1.0) * 0.25
            inlet = (1.0 - recycled) * feed_ref[s] + recycled * face_in[h, s]
            entry = jnp.where(at_inlet, -sub_ref[s] * inlet, 0.0)
            g_ref[2, s] = entry
            g_ref[0, s] = g_ref[0, s] + entry * l_ref[s, 0]
            g_ref[1, s] = g_ref[1, s] + entry * l_ref[s, depth - 1]
        g0 = g_ref[0]
        g1 = g_ref[1]
        sf[...] = g1 + co_ref[0] * g0
        sb[...] = g0 + co_ref[1] * g1
        ef[...] = zero_rows
        eb[...] = zero_rows
        for r in range(rounds):
            snd_f[h, r] = sf[...]
            snd_b[h, r] = sb[...]
            rank = jnp.where(col == 0, r, rounds - 1 - r)
            d = jnp.where(col == 0, ROUNDS[r], ROUNDS[rounds - 1 - r])
            has_right = position + d < count
            has_left = position - d >= 0
            right = jnp.minimum(position + d, count - 1)
            left = jnp.maximum(position - d, 0)
            copy_f = pltpu.make_async_remote_copy(
                src_ref=snd_f.at[h, r], dst_ref=rcv_f.at[h, r],
                send_sem=send_sem.at[h, 3 + r], recv_sem=recv_sem.at[h, 3 + r],
                device_id=(right, trans, col), device_id_type=MESH,
            )
            copy_b = pltpu.make_async_remote_copy(
                src_ref=snd_b.at[h, r], dst_ref=rcv_b.at[h, r],
                send_sem=send_sem.at[h, 3 + rounds + r], recv_sem=recv_sem.at[h, 3 + rounds + r],
                device_id=(left, trans, col), device_id_type=MESH,
            )
            pl.when(has_right)(copy_f.start)
            pl.when(has_left)(copy_b.start)
            last_round = r == rounds - 1

            @pl.when(has_left)
            def _():
                copy_f.wait_recv()
                got = rcv_f[h, r]
                ef[...] += co_ref[2 + rank] * got
                if not last_round:
                    sf[...] += co_ref[2 + rounds + rank] * got

            @pl.when(has_right)
            def _():
                copy_b.wait_recv()
                got = rcv_b[h, r]
                eb[...] += co_ref[2 + 2 * rounds + rank] * got
                if not last_round:
                    sb[...] += co_ref[2 + 3 * rounds + rank] * got

            pl.when(has_right)(copy_f.wait_send)
            pl.when(has_left)(copy_b.wait_send)

        before = ef[...]
        after = eb[...]
        r1 = g0 + co_ref[base + 0] * before + co_ref[base + 2] * after
        r2 = g1 + co_ref[base + 1] * before + co_ref[base + 3] * after
        top = r1 * co_ref[base + 6] + r2 * co_ref[base + 7]
        bottom = r1 * co_ref[base + 8] + r2 * co_ref[base + 9]
        ef[...] = sub_ref[...] * (before + co_ref[base + 4] * top)
        eb[...] = sup_ref[...] * (after + co_ref[base + 5] * bottom)
        for s in range(species):
            left_coef = ef[s] - g_ref[2, s]
            right_coef = eb[s]
            for z in range(depth):
                o_ref[s, z] = y_ref[s, z] - left_coef * l_ref[s, z] - right_coef * r_ref[s, z]


def body(concentration, zone_map, porosity, axial_number, courant, transverse, feed_conc, plan):
    f32 = jnp.float32
    count = lax.axis_size("axial")
    values = concentration[0]
    species, depth, wide, tall = values.shape
    steps = plan.shape[1]
    zone = zone_map[0]
    assert species * depth <= tall
    rounds = len(ROUNDS)
    n_co = 2 + 4 * rounds + 10
    slab = (wide, tall)
    block = (species, depth) + slab
    smem = pl.BlockSpec(memory_space=pltpu.SMEM)

    n_slot = 3 + 2 * rounds
    out = pl.pallas_call(
        functools.partial(fused_kernel, count),
        out_shape=jax.ShapeDtypeStruct(block, f32),
        in_specs=[_vmem()] * 2 + [smem] * 6,
        out_specs=_vmem(),
        scratch_shapes=[pltpu.VMEM(block, f32)] * 4
        + [pltpu.VMEM((n_co, species) + slab, f32), pltpu.VMEM((5, species) + slab, f32)]
        + [pltpu.VMEM((species,) + slab, f32)] * 2
        + [pltpu.VMEM((count,) + slab, f32)] * 6
        + [pltpu.VMEM((rounds, count) + slab, f32)] * 2
        + [pltpu.VMEM(slab, f32), pltpu.VMEM((2,) + slab, f32)]
        + [pltpu.SemaphoreType.DMA((2,))] * 2
        + [pltpu.VMEM(block, f32)]
        + [pltpu.VMEM((steps,) + slab, f32)] * 4
        + [pltpu.VMEM((steps, species) + slab, f32)]
        + [pltpu.VMEM((3, species) + slab, f32)]
        + [pltpu.VMEM((species,) + slab, f32)] * 4
        + [pltpu.VMEM((steps, rounds, species) + slab, f32)] * 4
        + [pltpu.SemaphoreType.DMA((steps, n_slot))] * 2,
        compiler_params=pltpu.CompilerParams(collective_id=0, has_side_effects=True),
        cost_estimate=pl.CostEstimate(
            flops=100 * steps * species * depth * wide * tall, transcendentals=0,
            bytes_accessed=3 * 4 * species * depth * wide * tall,
        ),
    )(values, zone, porosity, axial_number, courant, transverse, plan[0], feed_conc[0])
    return out[None]


def solution(mesh):
    in_specs = (
        P("col", None, "axial", None, "trans"),
        P("col", None, "trans"),
        P(),
        P(),
        P(),
        P(),
        P("col", None),
        P("col", None, None),
    )
    out_specs = P("col", None, "axial", None, "trans")
    return jax.shard_map(body, mesh=mesh, in_specs=in_specs, out_specs=out_specs, check_vma=False)
```

```python
import functools

import jax
import jax.numpy as jnp
from jax import lax
from jax.experimental import pallas as pl
from jax.experimental.pallas import tpu as pltpu
from jax.sharding import PartitionSpec as P


def swapped(array, axis, distance):
    return lax.ppermute(array, axis, [(i, i ^ 1 << distance) for i in range(lax.axis_size(axis))])


def from_behind(value, axis, steps):
    count = lax.axis_size(axis)
    initial, last = (max(0, -steps), min(count, count - steps))
    return lax.ppermute(value, axis, [(source, source + steps) for source in range(initial, last)])


def void_map(zone_map, porosity):
    voids = jnp.zeros(zone_map.shape, porosity.dtype)
    for number in range(porosity.shape[0]):
        voids = voids + jnp.where(zone_map == number, porosity[number], 0.0)
    return voids


def _vmem():
    return pl.BlockSpec(memory_space=pltpu.VMEM)


ROUNDS = (1, 2, 4, 8)
MESH = pl.DeviceIdType.MESH


def porosity_of(zone, por_ref):
    voids = jnp.zeros(zone.shape, jnp.float32)
    for number in range(por_ref.shape[0]):
        voids = voids + jnp.where(zone == number, por_ref[number], 0.0)
    return voids


def stencil_weights(voids, voids_lo, voids_hi, tr_ref, w_ref):
    wide, tall = voids.shape
    sublane = lax.broadcasted_iota(jnp.int32, (wide, tall), 0)
    lane = lax.broadcasted_iota(jnp.int32, (wide, tall), 1)
    p_xm = jnp.where(sublane == 0, 0.0, pltpu.roll(voids, 1, 0))
    p_xp = jnp.where(sublane == wide - 1, 0.0, pltpu.roll(voids, wide - 1, 0))
    p_ym = jnp.where(lane == 0, jnp.broadcast_to(voids_lo, (wide, tall)), pltpu.roll(voids, 1, 1))
    p_yp = jnp.where(lane == tall - 1, jnp.broadcast_to(voids_hi, (wide, tall)), pltpu.roll(voids, tall - 1, 1))
    faces = [2.0 * p / (voids + p) for p in (p_xm, p_xp, p_ym, p_yp)]
    for s in range(w_ref.shape[1]):
        scaled = [tr_ref[s] * face for face in faces]
        for direction in range(4):
            w_ref[1 + direction, s] = scaled[direction]
        w_ref[0, s] = 1.0 - (scaled[0] + scaled[1] + scaled[2] + scaled[3])


def setup(count, voids, ax_ref, cour_ref, cp_ref, ip_ref, l_ref, r_ref, co_ref, sub_ref, sup_ref,
          qf_ref, qb_ref, mf_ref, mb_ref, cprev_ref, hnext_ref, exf_ref, exb_ref):
    species, depth, wide, tall = cp_ref.shape
    position = lax.axis_index("axial")
    rounds = len(ROUNDS)
    at_outlet = position == count - 1
    for s in range(species):
        dispersion = ax_ref[s] + jnp.zeros((wide, tall), jnp.float32)
        flow_rate = cour_ref[s] / voids
        sub = -(dispersion + flow_rate)
        sup = -dispersion
        mi = 1.0 + 2.0 * dispersion + flow_rate
        me = 1.0 + dispersion + flow_rate
        sub_ref[s] = sub
        sup_ref[s] = sup
        coef = None
        for z in range(depth - 1):
            pivot = mi if z == 0 else mi - sub * coef
            inv = 1.0 / pivot
            coef = sup * inv
            ip_ref[s, z] = inv
            cp_ref[s, z] = coef

        def ends(last):
            inv_last = 1.0 / (last - sub * cp_ref[s, depth - 2])
            down = ip_ref[s, 0]
            downs = [down]
            for z in range(1, depth - 1):
                down = -sub * down * ip_ref[s, z]
                downs.append(down)
            left = -sub * down * inv_last
            left_last = left
            for z in range(depth - 2, -1, -1):
                left = downs[z] - cp_ref[s, z] * left
            right = inv_last
            for z in range(depth - 2, -1, -1):
                right = -cp_ref[s, z] * right
            return left, left_last, right, inv_last

        l0i, l1i, r0i, r1i = ends(mi)
        l0o, l1o, r0o, r1o = ends(me)

        own_last = jnp.where(at_outlet, me, mi)
        inv_last = 1.0 / (own_last - sub * cp_ref[s, depth - 2])
        ip_ref[s, depth - 1] = inv_last
        cp_ref[s, depth - 1] = sup * inv_last
        down = ip_ref[s, 0]
        l_ref[s, 0] = down
        for z in range(1, depth):
            down = -sub * down * ip_ref[s, z]
            l_ref[s, z] = down
        left = down
        right = inv_last
        r_ref[s, depth - 1] = right
        for z in range(depth - 2, -1, -1):
            left = l_ref[s, z] - cp_ref[s, z] * left
            l_ref[s, z] = left
            right = -cp_ref[s, z] * right
            r_ref[s, z] = right

        zero = jnp.zeros_like(sub)
        one = jnp.ones_like(sub)
        inner = (-sub * l0i, -sub * l1i, -sup * r0i, -sup * r1i)
        first = (zero, zero, inner[2], inner[3])
        outlet = (-sub * l0o, -sub * l1o, zero, zero)

        def couplings(j):
            return first if j == 0 else outlet if j == count - 1 else inner

        c_prev = zero
        for j in range(count):
            p0, p1, q0, q1 = couplings(j)
            inv = one if j == 0 else 1.0 / (1.0 - p0 * c_prev)
            qf_ref[j] = p1 * inv
            mf_ref[j] = p1 * c_prev * inv
            cprev_ref[j] = c_prev
            c_prev = q1 + p1 * c_prev * q0 * inv
        h_next = zero
        for j in range(count - 1, -1, -1):
            p0, p1, q0, q1 = couplings(j)
            inv = one if j == count - 1 else 1.0 / (1.0 - q1 * h_next)
            qb_ref[j] = q0 * inv
            mb_ref[j] = q0 * h_next * inv
            hnext_ref[j] = h_next
            h_next = p0 + q0 * h_next * p1 * inv

        for kk in range(count):
            exf_ref[0, kk] = one
            exb_ref[0, kk] = one
        for r in range(rounds - 1):
            d = ROUNDS[r]
            for kk in range(count):
                if kk - d >= 0:
                    exf_ref[r + 1, kk] = exf_ref[r, kk] * qf_ref[kk - d] * exf_ref[r, kk - d]
                else:
                    exf_ref[r + 1, kk] = one
                if kk + d < count:
                    exb_ref[r + 1, kk] = exb_ref[r, kk] * qb_ref[kk + d] * exb_ref[r, kk + d]
                else:
                    exb_ref[r + 1, kk] = one

        co_ref[0, s] = mf_ref[position]
        co_ref[1, s] = mb_ref[position]
        qf_own = qf_ref[position]
        qb_own = qb_ref[position]
        for r in range(rounds):
            wef = exf_ref[r, position]
            web = exb_ref[r, position]
            co_ref[2 + r, s] = wef
            co_ref[2 + rounds + r, s] = qf_own * wef
            co_ref[2 + 2 * rounds + r, s] = web
            co_ref[2 + 3 * rounds + r, s] = qb_own * web
        at_first = position == 0
        at_last = position == count - 1
        p0 = jnp.where(at_first, zero, jnp.where(at_last, outlet[0], inner[0]))
        p1 = jnp.where(at_first, zero, jnp.where(at_last, outlet[1], inner[1]))
        q0 = jnp.where(at_last, zero, inner[2])
        q1 = jnp.where(at_last, zero, inner[3])
        c_own = cprev_ref[position]
        h_own = hnext_ref[position]
        a11 = 1.0 - p0 * c_own
        a12 = -q0 * h_own
        a21 = -p1 * c_own
        a22 = 1.0 - q1 * h_own
        inv_det = 1.0 / (a11 * a22 - a12 * a21)
        base = 2 + 4 * rounds
        for i, value in enumerate(
            (p0, p1, q0, q1, c_own, h_own, a22 * inv_det, -a12 * inv_det, -a21 * inv_det, a11 * inv_det)
        ):
            co_ref[base + i, s] = value


def fused_kernel(count, v_ref, zone_ref, por_ref, ax_ref, cour_ref, tr_ref, plan_ref, feed_ref,
                 o_ref,
                 cp_ref, ip_ref, l_ref, r_ref, co_ref, w_ref, sub_ref, sup_ref,
                 qf_ref, qb_ref, mf_ref, mb_ref, cprev_ref, hnext_ref, exf_ref, exb_ref,
                 vs_ref, vr_ref, vsem_s, vsem_r,
                 y_ref, hs_lo, hs_hi, hr_lo, hr_hi, face_in, g_ref, sf, sb, ef, eb,
                 snd_f, snd_b, rcv_f, rcv_b, send_sem, recv_sem):
    species, depth, wide, tall = v_ref.shape
    steps = plan_ref.shape[0]
    rounds = len(ROUNDS)
    position = lax.axis_index("axial")
    trans = lax.axis_index("trans")
    col = lax.axis_index("col")
    n_trans = lax.axis_size("trans")
    at_inlet = position == 0
    has_lo = trans > 0
    has_hi = trans < n_trans - 1
    lo_dev = (position, jnp.maximum(trans - 1, 0), col)
    hi_dev = (position, jnp.minimum(trans + 1, n_trans - 1), col)
    col_dev = (position, trans, 1 - col)
    lane = lax.broadcasted_iota(jnp.int32, (wide, tall), 1)
    base = 2 + 4 * rounds

    barrier = pltpu.get_barrier_semaphore()

    def greet(cond, device):
        @pl.when(cond)
        def _():
            pl.semaphore_signal(barrier, 1, device_id=device, device_id_type=MESH)

    greet(has_lo, lo_dev)
    greet(has_hi, hi_dev)
    greet(at_inlet, col_dev)
    partners = has_lo.astype(jnp.int32) + has_hi.astype(jnp.int32) + at_inlet.astype(jnp.int32)
    for d in ROUNDS:
        has_right = position + d < count
        has_left = position - d >= 0
        greet(has_right, (jnp.minimum(position + d, count - 1), trans, col))
        greet(has_left, (jnp.maximum(position - d, 0), trans, col))
        partners = partners + has_right.astype(jnp.int32) + has_left.astype(jnp.int32)
    voids = porosity_of(zone_ref[...], por_ref)
    vs_ref[...] = voids

    def run_setup():
        setup(count, voids, ax_ref, cour_ref, cp_ref, ip_ref, l_ref, r_ref, co_ref, sub_ref, sup_ref,
              qf_ref, qb_ref, mf_ref, mb_ref, cprev_ref, hnext_ref, exf_ref, exb_ref)

    pl.when(col == 0)(run_setup)
    pl.semaphore_wait(barrier, partners)

    zero_rows = jnp.zeros((species, wide, tall), jnp.float32)
    for h in range(steps):
        @pl.when(jnp.logical_not(has_lo))
        def _():
            hr_lo[h] = jnp.zeros((wide, tall), jnp.float32)

        @pl.when(jnp.logical_not(has_hi))
        def _():
            hr_hi[h] = jnp.zeros((wide, tall), jnp.float32)

        @pl.when(jnp.logical_not(at_inlet))
        def _():
            face_in[h] = zero_rows

    @pl.when(jnp.logical_not(has_lo))
    def _():
        vr_ref[0] = jnp.zeros((wide, tall), jnp.float32)

    @pl.when(jnp.logical_not(has_hi))
    def _():
        vr_ref[1] = jnp.zeros((wide, tall), jnp.float32)

    voids_up = pltpu.make_async_remote_copy(
        src_ref=vs_ref, dst_ref=vr_ref.at[0], send_sem=vsem_s.at[0], recv_sem=vsem_r.at[0],
        device_id=hi_dev, device_id_type=MESH,
    )
    voids_down = pltpu.make_async_remote_copy(
        src_ref=vs_ref, dst_ref=vr_ref.at[1], send_sem=vsem_s.at[1], recv_sem=vsem_r.at[1],
        device_id=lo_dev, device_id_type=MESH,
    )
    pl.when(has_hi)(voids_up.start)
    pl.when(has_lo)(voids_down.start)

    def exchange_start(h):
        src = v_ref if h == 0 else o_ref
        acc_lo = jnp.zeros((wide, tall), jnp.float32)
        acc_hi = jnp.zeros((wide, tall), jnp.float32)
        for s in range(species):
            for z in range(depth):
                at = s * depth + z
                acc_lo = jnp.where(lane == at, jnp.broadcast_to(src[s, z, :, tall - 1 : tall], (wide, tall)), acc_lo)
                acc_hi = jnp.where(lane == at, jnp.broadcast_to(src[s, z, :, 0:1], (wide, tall)), acc_hi)
        hs_lo[h] = acc_lo
        hs_hi[h] = acc_hi
        copy_lo = pltpu.make_async_remote_copy(
            src_ref=hs_lo.at[h], dst_ref=hr_lo.at[h], send_sem=send_sem.at[h, 0], recv_sem=recv_sem.at[h, 0],
            device_id=hi_dev, device_id_type=MESH,
        )
        copy_hi = pltpu.make_async_remote_copy(
            src_ref=hs_hi.at[h], dst_ref=hr_hi.at[h], send_sem=send_sem.at[h, 1], recv_sem=recv_sem.at[h, 1],
            device_id=lo_dev, device_id_type=MESH,
        )
        copy_face = pltpu.make_async_remote_copy(
            src_ref=src.at[:, 0], dst_ref=face_in.at[h], send_sem=send_sem.at[h, 2], recv_sem=recv_sem.at[h, 2],
            device_id=col_dev, device_id_type=MESH,
        )
        pl.when(has_hi)(copy_lo.start)
        pl.when(has_lo)(copy_hi.start)
        pl.when(at_inlet)(copy_face.start)
        return copy_lo, copy_hi, copy_face

    def exchange_wait(copy_lo, copy_hi, copy_face):
        pl.when(has_lo)(copy_lo.wait_recv)
        pl.when(has_hi)(copy_hi.wait_recv)
        pl.when(has_hi)(copy_lo.wait_send)
        pl.when(has_lo)(copy_hi.wait_send)

    first_copies = exchange_start(0)
    pl.when(col != 0)(run_setup)
    pl.when(has_lo)(voids_up.wait_recv)
    pl.when(has_hi)(voids_down.wait_recv)
    pl.when(has_hi)(voids_up.wait_send)
    pl.when(has_lo)(voids_down.wait_send)
    voids_lo = jnp.where(has_lo, vr_ref[0, :, tall - 1 : tall], 0.0)
    voids_hi = jnp.where(has_hi, vr_ref[1, :, 0:1], 0.0)
    stencil_weights(voids, voids_lo, voids_hi, tr_ref, w_ref)

    for h in range(steps):
        src = v_ref if h == 0 else o_ref
        copy_lo, copy_hi, copy_face = first_copies if h == 0 else exchange_start(h)
        exchange_wait(copy_lo, copy_hi, copy_face)

        for s in range(species):
            w0 = w_ref[0, s]
            wxm = w_ref[1, s]
            wxp = w_ref[2, s]
            wym = w_ref[3, s]
            wyp = w_ref[4, s]
            sub = sub_ref[s]
            down = None
            for z in range(depth):
                v = src[s, z]
                xm = pltpu.roll(v, 1, 0)
                xp = pltpu.roll(v, wide - 1, 0)
                at = s * depth + z
                ym = jnp.where(lane == 0, hr_lo[h, :, at : at + 1], pltpu.roll(v, 1, 1))
                yp = jnp.where(lane == tall - 1, hr_hi[h, :, at : at + 1], pltpu.roll(v, tall - 1, 1))
                moved = w0 * v + ((wxp * xp + wxm * xm) + (wyp * yp + wym * ym))
                if z == 0:
                    down = moved * ip_ref[s, 0]
                else:
                    down = (moved - sub * down) * ip_ref[s, z]
                y_ref[s, z] = down
            solved = down
            g_ref[1, s] = solved
            for z in range(depth - 2, -1, -1):
                solved = y_ref[s, z] - cp_ref[s, z] * solved
                y_ref[s, z] = solved
            g_ref[0, s] = solved

        pl.when(at_inlet)(copy_face.wait_recv)
        pl.when(at_inlet)(copy_face.wait_send)
        for s in range(species):
            recycled = (plan_ref[h, s].astype(jnp.float32) + 1.0) * 0.25
            inlet = (1.0 - recycled) * feed_ref[s] + recycled * face_in[h, s]
            entry = jnp.where(at_inlet, -sub_ref[s] * inlet, 0.0)
            g_ref[2, s] = entry
            g_ref[0, s] = g_ref[0, s] + entry * l_ref[s, 0]
            g_ref[1, s] = g_ref[1, s] + entry * l_ref[s, depth - 1]
        g0 = g_ref[0]
        g1 = g_ref[1]
        sf[...] = g1 + co_ref[0] * g0
        sb[...] = g0 + co_ref[1] * g1
        ef[...] = zero_rows
        eb[...] = zero_rows
        for r in range(rounds):
            snd_f[h, r] = sf[...]
            snd_b[h, r] = sb[...]
            rank = jnp.where(col == 0, r, rounds - 1 - r)
            d = jnp.where(col == 0, ROUNDS[r], ROUNDS[rounds - 1 - r])
            has_right = position + d < count
            has_left = position - d >= 0
            right = jnp.minimum(position + d, count - 1)
            left = jnp.maximum(position - d, 0)
            copy_f = pltpu.make_async_remote_copy(
                src_ref=snd_f.at[h, r], dst_ref=rcv_f.at[h, r],
                send_sem=send_sem.at[h, 3 + r], recv_sem=recv_sem.at[h, 3 + r],
                device_id=(right, trans, col), device_id_type=MESH,
            )
            copy_b = pltpu.make_async_remote_copy(
                src_ref=snd_b.at[h, r], dst_ref=rcv_b.at[h, r],
                send_sem=send_sem.at[h, 3 + rounds + r], recv_sem=recv_sem.at[h, 3 + rounds + r],
                device_id=(left, trans, col), device_id_type=MESH,
            )
            pl.when(has_right)(copy_f.start)
            pl.when(has_left)(copy_b.start)
            last_round = r == rounds - 1

            @pl.when(has_left)
            def _():
                copy_f.wait_recv()
                got = rcv_f[h, r]
                ef[...] += co_ref[2 + rank] * got
                if not last_round:
                    sf[...] += co_ref[2 + rounds + rank] * got

            @pl.when(has_right)
            def _():
                copy_b.wait_recv()
                got = rcv_b[h, r]
                eb[...] += co_ref[2 + 2 * rounds + rank] * got
                if not last_round:
                    sb[...] += co_ref[2 + 3 * rounds + rank] * got

            pl.when(has_right)(copy_f.wait_send)
            pl.when(has_left)(copy_b.wait_send)

        before = ef[...]
        after = eb[...]
        r1 = g0 + co_ref[base + 0] * before + co_ref[base + 2] * after
        r2 = g1 + co_ref[base + 1] * before + co_ref[base + 3] * after
        top = r1 * co_ref[base + 6] + r2 * co_ref[base + 7]
        bottom = r1 * co_ref[base + 8] + r2 * co_ref[base + 9]
        ef[...] = sub_ref[...] * (before + co_ref[base + 4] * top)
        eb[...] = sup_ref[...] * (after + co_ref[base + 5] * bottom)
        for s in range(species):
            left_coef = ef[s] - g_ref[2, s]
            right_coef = eb[s]
            for z in range(depth):
                o_ref[s, z] = y_ref[s, z] - left_coef * l_ref[s, z] - right_coef * r_ref[s, z]


def body(concentration, zone_map, porosity, axial_number, courant, transverse, feed_conc, plan):
    f32 = jnp.float32
    count = lax.axis_size("axial")
    values = concentration[0]
    species, depth, wide, tall = values.shape
    steps = plan.shape[1]
    zone = zone_map[0]
    assert species * depth <= tall
    rounds = len(ROUNDS)
    n_co = 2 + 4 * rounds + 10
    slab = (wide, tall)
    block = (species, depth) + slab
    smem = pl.BlockSpec(memory_space=pltpu.SMEM)

    n_slot = 3 + 2 * rounds
    out = pl.pallas_call(
        functools.partial(fused_kernel, count),
        out_shape=jax.ShapeDtypeStruct(block, f32),
        in_specs=[_vmem()] * 2 + [smem] * 6,
        out_specs=_vmem(),
        scratch_shapes=[pltpu.VMEM(block, f32)] * 4
        + [pltpu.VMEM((n_co, species) + slab, f32), pltpu.VMEM((5, species) + slab, f32)]
        + [pltpu.VMEM((species,) + slab, f32)] * 2
        + [pltpu.VMEM((count,) + slab, f32)] * 6
        + [pltpu.VMEM((rounds, count) + slab, f32)] * 2
        + [pltpu.VMEM(slab, f32), pltpu.VMEM((2,) + slab, f32)]
        + [pltpu.SemaphoreType.DMA((2,))] * 2
        + [pltpu.VMEM(block, f32)]
        + [pltpu.VMEM((steps,) + slab, f32)] * 4
        + [pltpu.VMEM((steps, species) + slab, f32)]
        + [pltpu.VMEM((3, species) + slab, f32)]
        + [pltpu.VMEM((species,) + slab, f32)] * 4
        + [pltpu.VMEM((steps, rounds, species) + slab, f32)] * 4
        + [pltpu.SemaphoreType.DMA((steps, n_slot))] * 2,
        compiler_params=pltpu.CompilerParams(collective_id=0, has_side_effects=True),
        cost_estimate=pl.CostEstimate(
            flops=100 * steps * species * depth * wide * tall, transcendentals=0,
            bytes_accessed=3 * 4 * species * depth * wide * tall,
        ),
    )(values, zone, porosity, axial_number, courant, transverse, plan[0], feed_conc[0])
    return out[None]


def solution(mesh):
    in_specs = (
        P("col", None, "axial", None, "trans"),
        P("col", None, "trans"),
        P(),
        P(),
        P(),
        P(),
        P("col", None),
        P("col", None, None),
    )
    out_specs = P("col", None, "axial", None, "trans")
    return jax.shard_map(body, mesh=mesh, in_specs=in_specs, out_specs=out_specs, check_vma=False)
```

```python
import functools

import jax
import jax.numpy as jnp
from jax import lax
from jax.experimental import pallas as pl
from jax.experimental.pallas import tpu as pltpu
from jax.sharding import PartitionSpec as P


def swapped(array, axis, distance):
    return lax.ppermute(array, axis, [(i, i ^ 1 << distance) for i in range(lax.axis_size(axis))])


def from_behind(value, axis, steps):
    count = lax.axis_size(axis)
    initial, last = (max(0, -steps), min(count, count - steps))
    return lax.ppermute(value, axis, [(source, source + steps) for source in range(initial, last)])


def void_map(zone_map, porosity):
    voids = jnp.zeros(zone_map.shape, porosity.dtype)
    for number in range(porosity.shape[0]):
        voids = voids + jnp.where(zone_map == number, porosity[number], 0.0)
    return voids


def _vmem():
    return pl.BlockSpec(memory_space=pltpu.VMEM)


ROUNDS = (1, 2, 4, 8)
MESH = pl.DeviceIdType.MESH


def porosity_of(zone, por_ref):
    voids = jnp.zeros(zone.shape, jnp.float32)
    for number in range(por_ref.shape[0]):
        voids = voids + jnp.where(zone == number, por_ref[number], 0.0)
    return voids


def stencil_weights(voids, voids_lo, voids_hi, tr_ref, w_ref):
    wide, tall = voids.shape
    sublane = lax.broadcasted_iota(jnp.int32, (wide, tall), 0)
    lane = lax.broadcasted_iota(jnp.int32, (wide, tall), 1)
    p_xm = jnp.where(sublane == 0, 0.0, pltpu.roll(voids, 1, 0))
    p_xp = jnp.where(sublane == wide - 1, 0.0, pltpu.roll(voids, wide - 1, 0))
    p_ym = jnp.where(lane == 0, jnp.broadcast_to(voids_lo, (wide, tall)), pltpu.roll(voids, 1, 1))
    p_yp = jnp.where(lane == tall - 1, jnp.broadcast_to(voids_hi, (wide, tall)), pltpu.roll(voids, tall - 1, 1))
    faces = [2.0 * p / (voids + p) for p in (p_xm, p_xp, p_ym, p_yp)]
    for s in range(w_ref.shape[1]):
        scaled = [tr_ref[s] * face for face in faces]
        for direction in range(4):
            w_ref[1 + direction, s] = scaled[direction]
        w_ref[0, s] = 1.0 - (scaled[0] + scaled[1] + scaled[2] + scaled[3])


def setup(count, voids, ax_ref, cour_ref, cp_ref, ip_ref, l_ref, r_ref, co_ref, sub_ref, sup_ref,
          qf_ref, qb_ref, mf_ref, mb_ref, cprev_ref, hnext_ref, exf_ref, exb_ref):
    species, depth, wide, tall = cp_ref.shape
    position = lax.axis_index("axial")
    rounds = len(ROUNDS)
    at_outlet = position == count - 1
    for s in range(species):
        dispersion = ax_ref[s] + jnp.zeros((wide, tall), jnp.float32)
        flow_rate = cour_ref[s] / voids
        sub = -(dispersion + flow_rate)
        sup = -dispersion
        mi = 1.0 + 2.0 * dispersion + flow_rate
        me = 1.0 + dispersion + flow_rate
        sub_ref[s] = sub
        sup_ref[s] = sup
        coef = None
        for z in range(depth - 1):
            pivot = mi if z == 0 else mi - sub * coef
            inv = 1.0 / pivot
            coef = sup * inv
            ip_ref[s, z] = inv
            cp_ref[s, z] = coef

        def ends(last):
            inv_last = 1.0 / (last - sub * cp_ref[s, depth - 2])
            down = ip_ref[s, 0]
            downs = [down]
            for z in range(1, depth - 1):
                down = -sub * down * ip_ref[s, z]
                downs.append(down)
            left = -sub * down * inv_last
            left_last = left
            for z in range(depth - 2, -1, -1):
                left = downs[z] - cp_ref[s, z] * left
            right = inv_last
            for z in range(depth - 2, -1, -1):
                right = -cp_ref[s, z] * right
            return left, left_last, right, inv_last

        l0i, l1i, r0i, r1i = ends(mi)
        l0o, l1o, r0o, r1o = ends(me)

        own_last = jnp.where(at_outlet, me, mi)
        inv_last = 1.0 / (own_last - sub * cp_ref[s, depth - 2])
        ip_ref[s, depth - 1] = inv_last
        cp_ref[s, depth - 1] = sup * inv_last
        down = ip_ref[s, 0]
        l_ref[s, 0] = down
        for z in range(1, depth):
            down = -sub * down * ip_ref[s, z]
            l_ref[s, z] = down
        left = down
        right = inv_last
        r_ref[s, depth - 1] = right
        for z in range(depth - 2, -1, -1):
            left = l_ref[s, z] - cp_ref[s, z] * left
            l_ref[s, z] = left
            right = -cp_ref[s, z] * right
            r_ref[s, z] = right

        zero = jnp.zeros_like(sub)
        one = jnp.ones_like(sub)
        inner = (-sub * l0i, -sub * l1i, -sup * r0i, -sup * r1i)
        first = (zero, zero, inner[2], inner[3])
        outlet = (-sub * l0o, -sub * l1o, zero, zero)

        def couplings(j):
            return first if j == 0 else outlet if j == count - 1 else inner

        c_prev = zero
        for j in range(count):
            p0, p1, q0, q1 = couplings(j)
            inv = one if j == 0 else 1.0 / (1.0 - p0 * c_prev)
            qf_ref[j] = p1 * inv
            mf_ref[j] = p1 * c_prev * inv
            cprev_ref[j] = c_prev
            c_prev = q1 + p1 * c_prev * q0 * inv
        h_next = zero
        for j in range(count - 1, -1, -1):
            p0, p1, q0, q1 = couplings(j)
            inv = one if j == count - 1 else 1.0 / (1.0 - q1 * h_next)
            qb_ref[j] = q0 * inv
            mb_ref[j] = q0 * h_next * inv
            hnext_ref[j] = h_next
            h_next = p0 + q0 * h_next * p1 * inv

        for kk in range(count):
            exf_ref[0, kk] = one
            exb_ref[0, kk] = one
        for r in range(rounds - 1):
            d = ROUNDS[r]
            for kk in range(count):
                if kk - d >= 0:
                    exf_ref[r + 1, kk] = exf_ref[r, kk] * qf_ref[kk - d] * exf_ref[r, kk - d]
                else:
                    exf_ref[r + 1, kk] = one
                if kk + d < count:
                    exb_ref[r + 1, kk] = exb_ref[r, kk] * qb_ref[kk + d] * exb_ref[r, kk + d]
                else:
                    exb_ref[r + 1, kk] = one

        co_ref[0, s] = mf_ref[position]
        co_ref[1, s] = mb_ref[position]
        qf_own = qf_ref[position]
        qb_own = qb_ref[position]
        for r in range(rounds):
            wef = exf_ref[r, position]
            web = exb_ref[r, position]
            co_ref[2 + r, s] = wef
            co_ref[2 + rounds + r, s] = qf_own * wef
            co_ref[2 + 2 * rounds + r, s] = web
            co_ref[2 + 3 * rounds + r, s] = qb_own * web
        at_first = position == 0
        at_last = position == count - 1
        p0 = jnp.where(at_first, zero, jnp.where(at_last, outlet[0], inner[0]))
        p1 = jnp.where(at_first, zero, jnp.where(at_last, outlet[1], inner[1]))
        q0 = jnp.where(at_last, zero, inner[2])
        q1 = jnp.where(at_last, zero, inner[3])
        c_own = cprev_ref[position]
        h_own = hnext_ref[position]
        a11 = 1.0 - p0 * c_own
        a12 = -q0 * h_own
        a21 = -p1 * c_own
        a22 = 1.0 - q1 * h_own
        inv_det = 1.0 / (a11 * a22 - a12 * a21)
        base = 2 + 4 * rounds
        for i, value in enumerate(
            (p0, p1, q0, q1, c_own, h_own, a22 * inv_det, -a12 * inv_det, -a21 * inv_det, a11 * inv_det)
        ):
            co_ref[base + i, s] = value


def fused_kernel(count, v_ref, zone_ref, por_ref, ax_ref, cour_ref, tr_ref, plan_ref, feed_ref,
                 o_ref,
                 cp_ref, ip_ref, l_ref, r_ref, co_ref, w_ref, sub_ref, sup_ref,
                 qf_ref, qb_ref, mf_ref, mb_ref, cprev_ref, hnext_ref, exf_ref, exb_ref,
                 vs_ref, vr_ref, vsem_s, vsem_r,
                 y_ref, hs_lo, hs_hi, hr_lo, hr_hi, face_in, g_ref, sf, sb, ef, eb,
                 snd_f, snd_b, rcv_f, rcv_b, send_sem, recv_sem):
    species, depth, wide, tall = v_ref.shape
    steps = plan_ref.shape[0]
    rounds = len(ROUNDS)
    position = lax.axis_index("axial")
    trans = lax.axis_index("trans")
    col = lax.axis_index("col")
    n_trans = lax.axis_size("trans")
    at_inlet = position == 0
    has_lo = trans > 0
    has_hi = trans < n_trans - 1
    lo_dev = (position, jnp.maximum(trans - 1, 0), col)
    hi_dev = (position, jnp.minimum(trans + 1, n_trans - 1), col)
    col_dev = (position, trans, 1 - col)
    lane = lax.broadcasted_iota(jnp.int32, (wide, tall), 1)
    base = 2 + 4 * rounds

    barrier = pltpu.get_barrier_semaphore()

    def greet(cond, device):
        @pl.when(cond)
        def _():
            pl.semaphore_signal(barrier, 1, device_id=device, device_id_type=MESH)

    greet(has_lo, lo_dev)
    greet(has_hi, hi_dev)
    greet(at_inlet, col_dev)
    partners = has_lo.astype(jnp.int32) + has_hi.astype(jnp.int32) + at_inlet.astype(jnp.int32)
    for d in ROUNDS:
        has_right = position + d < count
        has_left = position - d >= 0
        greet(has_right, (jnp.minimum(position + d, count - 1), trans, col))
        greet(has_left, (jnp.maximum(position - d, 0), trans, col))
        partners = partners + has_right.astype(jnp.int32) + has_left.astype(jnp.int32)
    voids = porosity_of(zone_ref[...], por_ref)
    vs_ref[...] = voids

    def run_setup():
        setup(count, voids, ax_ref, cour_ref, cp_ref, ip_ref, l_ref, r_ref, co_ref, sub_ref, sup_ref,
              qf_ref, qb_ref, mf_ref, mb_ref, cprev_ref, hnext_ref, exf_ref, exb_ref)

    pl.when(col == 0)(run_setup)
    pl.semaphore_wait(barrier, partners)

    zero_rows = jnp.zeros((species, wide, tall), jnp.float32)
    for h in range(steps):
        @pl.when(jnp.logical_not(has_lo))
        def _():
            hr_lo[h] = jnp.zeros((wide, tall), jnp.float32)

        @pl.when(jnp.logical_not(has_hi))
        def _():
            hr_hi[h] = jnp.zeros((wide, tall), jnp.float32)

        @pl.when(jnp.logical_not(at_inlet))
        def _():
            face_in[h] = zero_rows

    @pl.when(jnp.logical_not(has_lo))
    def _():
        vr_ref[0] = jnp.zeros((wide, tall), jnp.float32)

    @pl.when(jnp.logical_not(has_hi))
    def _():
        vr_ref[1] = jnp.zeros((wide, tall), jnp.float32)

    voids_up = pltpu.make_async_remote_copy(
        src_ref=vs_ref, dst_ref=vr_ref.at[0], send_sem=vsem_s.at[0], recv_sem=vsem_r.at[0],
        device_id=hi_dev, device_id_type=MESH,
    )
    voids_down = pltpu.make_async_remote_copy(
        src_ref=vs_ref, dst_ref=vr_ref.at[1], send_sem=vsem_s.at[1], recv_sem=vsem_r.at[1],
        device_id=lo_dev, device_id_type=MESH,
    )
    pl.when(has_hi)(voids_up.start)
    pl.when(has_lo)(voids_down.start)

    def exchange_start(h):
        src = v_ref if h == 0 else o_ref
        acc_lo = jnp.zeros((wide, tall), jnp.float32)
        acc_hi = jnp.zeros((wide, tall), jnp.float32)

        def column(s, z, c):
            if h == 0:
                return src[s, z, :, c : c + 1]
            cut = slice(c, c + 1)
            return (y_ref[s, z, :, cut] - ef[s, :, cut] * l_ref[s, z, :, cut]
                    - eb[s, :, cut] * r_ref[s, z, :, cut])

        for s in range(species):
            for z in range(depth):
                at = s * depth + z
                acc_lo = jnp.where(lane == at, jnp.broadcast_to(column(s, z, tall - 1), (wide, tall)), acc_lo)
                acc_hi = jnp.where(lane == at, jnp.broadcast_to(column(s, z, 0), (wide, tall)), acc_hi)
        hs_lo[h] = acc_lo
        hs_hi[h] = acc_hi
        copy_lo = pltpu.make_async_remote_copy(
            src_ref=hs_lo.at[h], dst_ref=hr_lo.at[h], send_sem=send_sem.at[h, 0], recv_sem=recv_sem.at[h, 0],
            device_id=hi_dev, device_id_type=MESH,
        )
        copy_hi = pltpu.make_async_remote_copy(
            src_ref=hs_hi.at[h], dst_ref=hr_hi.at[h], send_sem=send_sem.at[h, 1], recv_sem=recv_sem.at[h, 1],
            device_id=lo_dev, device_id_type=MESH,
        )
        copy_face = pltpu.make_async_remote_copy(
            src_ref=src.at[:, 0], dst_ref=face_in.at[h], send_sem=send_sem.at[h, 2], recv_sem=recv_sem.at[h, 2],
            device_id=col_dev, device_id_type=MESH,
        )
        pl.when(has_hi)(copy_lo.start)
        pl.when(has_lo)(copy_hi.start)
        pl.when(at_inlet)(copy_face.start)
        return copy_lo, copy_hi, copy_face

    def exchange_wait(copy_lo, copy_hi, copy_face):
        pl.when(has_lo)(copy_lo.wait_recv)
        pl.when(has_hi)(copy_hi.wait_recv)
        pl.when(has_hi)(copy_lo.wait_send)
        pl.when(has_lo)(copy_hi.wait_send)

    pending = exchange_start(0)
    pl.when(col != 0)(run_setup)
    pl.when(has_lo)(voids_up.wait_recv)
    pl.when(has_hi)(voids_down.wait_recv)
    pl.when(has_hi)(voids_up.wait_send)
    pl.when(has_lo)(voids_down.wait_send)
    voids_lo = jnp.where(has_lo, vr_ref[0, :, tall - 1 : tall], 0.0)
    voids_hi = jnp.where(has_hi, vr_ref[1, :, 0:1], 0.0)
    stencil_weights(voids, voids_lo, voids_hi, tr_ref, w_ref)

    for h in range(steps):
        src = v_ref if h == 0 else o_ref
        copy_lo, copy_hi, copy_face = pending
        exchange_wait(copy_lo, copy_hi, copy_face)

        for s in range(species):
            w0 = w_ref[0, s]
            wxm = w_ref[1, s]
            wxp = w_ref[2, s]
            wym = w_ref[3, s]
            wyp = w_ref[4, s]
            sub = sub_ref[s]
            down = None
            for z in range(depth):
                v = src[s, z]
                xm = pltpu.roll(v, 1, 0)
                xp = pltpu.roll(v, wide - 1, 0)
                at = s * depth + z
                ym = jnp.where(lane == 0, hr_lo[h, :, at : at + 1], pltpu.roll(v, 1, 1))
                yp = jnp.where(lane == tall - 1, hr_hi[h, :, at : at + 1], pltpu.roll(v, tall - 1, 1))
                moved = w0 * v + ((wxp * xp + wxm * xm) + (wyp * yp + wym * ym))
                if z == 0:
                    down = moved * ip_ref[s, 0]
                else:
                    down = (moved - sub * down) * ip_ref[s, z]
                y_ref[s, z] = down
            solved = down
            g_ref[1, s] = solved
            for z in range(depth - 2, -1, -1):
                solved = y_ref[s, z] - cp_ref[s, z] * solved
                y_ref[s, z] = solved
            g_ref[0, s] = solved

        pl.when(at_inlet)(copy_face.wait_recv)
        pl.when(at_inlet)(copy_face.wait_send)
        for s in range(species):
            recycled = (plan_ref[h, s].astype(jnp.float32) + 1.0) * 0.25
            inlet = (1.0 - recycled) * feed_ref[s] + recycled * face_in[h, s]
            entry = jnp.where(at_inlet, -sub_ref[s] * inlet, 0.0)
            g_ref[2, s] = entry
            g_ref[0, s] = g_ref[0, s] + entry * l_ref[s, 0]
            g_ref[1, s] = g_ref[1, s] + entry * l_ref[s, depth - 1]
        g0 = g_ref[0]
        g1 = g_ref[1]
        sf[...] = g1 + co_ref[0] * g0
        sb[...] = g0 + co_ref[1] * g1
        ef[...] = zero_rows
        eb[...] = zero_rows
        for r in range(rounds):
            snd_f[h, r] = sf[...]
            snd_b[h, r] = sb[...]
            rank = jnp.where(col == 0, r, rounds - 1 - r)
            d = jnp.where(col == 0, ROUNDS[r], ROUNDS[rounds - 1 - r])
            has_right = position + d < count
            has_left = position - d >= 0
            right = jnp.minimum(position + d, count - 1)
            left = jnp.maximum(position - d, 0)
            copy_f = pltpu.make_async_remote_copy(
                src_ref=snd_f.at[h, r], dst_ref=rcv_f.at[h, r],
                send_sem=send_sem.at[h, 3 + r], recv_sem=recv_sem.at[h, 3 + r],
                device_id=(right, trans, col), device_id_type=MESH,
            )
            copy_b = pltpu.make_async_remote_copy(
                src_ref=snd_b.at[h, r], dst_ref=rcv_b.at[h, r],
                send_sem=send_sem.at[h, 3 + rounds + r], recv_sem=recv_sem.at[h, 3 + rounds + r],
                device_id=(left, trans, col), device_id_type=MESH,
            )
            pl.when(has_right)(copy_f.start)
            pl.when(has_left)(copy_b.start)
            last_round = r == rounds - 1

            @pl.when(has_left)
            def _():
                copy_f.wait_recv()
                got = rcv_f[h, r]
                ef[...] += co_ref[2 + rank] * got
                if not last_round:
                    sf[...] += co_ref[2 + rounds + rank] * got

            @pl.when(has_right)
            def _():
                copy_b.wait_recv()
                got = rcv_b[h, r]
                eb[...] += co_ref[2 + 2 * rounds + rank] * got
                if not last_round:
                    sb[...] += co_ref[2 + 3 * rounds + rank] * got

            pl.when(has_right)(copy_f.wait_send)
            pl.when(has_left)(copy_b.wait_send)

        before = ef[...]
        after = eb[...]
        r1 = g0 + co_ref[base + 0] * before + co_ref[base + 2] * after
        r2 = g1 + co_ref[base + 1] * before + co_ref[base + 3] * after
        top = r1 * co_ref[base + 6] + r2 * co_ref[base + 7]
        bottom = r1 * co_ref[base + 8] + r2 * co_ref[base + 9]
        ef[...] = sub_ref[...] * (before + co_ref[base + 4] * top)
        eb[...] = sup_ref[...] * (after + co_ref[base + 5] * bottom)
        for s in range(species):
            ef[s] = ef[s] - g_ref[2, s]
        rows = range(depth)
        if h + 1 < steps:
            for s in range(species):
                o_ref[s, 0] = y_ref[s, 0] - ef[s] * l_ref[s, 0] - eb[s] * r_ref[s, 0]
            pending = exchange_start(h + 1)
            rows = range(1, depth)
        for s in range(species):
            left_coef = ef[s]
            right_coef = eb[s]
            for z in rows:
                o_ref[s, z] = y_ref[s, z] - left_coef * l_ref[s, z] - right_coef * r_ref[s, z]


def body(concentration, zone_map, porosity, axial_number, courant, transverse, feed_conc, plan):
    f32 = jnp.float32
    count = lax.axis_size("axial")
    values = concentration[0]
    species, depth, wide, tall = values.shape
    steps = plan.shape[1]
    zone = zone_map[0]
    assert species * depth <= tall
    rounds = len(ROUNDS)
    n_co = 2 + 4 * rounds + 10
    slab = (wide, tall)
    block = (species, depth) + slab
    smem = pl.BlockSpec(memory_space=pltpu.SMEM)

    n_slot = 3 + 2 * rounds
    out = pl.pallas_call(
        functools.partial(fused_kernel, count),
        out_shape=jax.ShapeDtypeStruct(block, f32),
        in_specs=[_vmem()] * 2 + [smem] * 6,
        out_specs=_vmem(),
        scratch_shapes=[pltpu.VMEM(block, f32)] * 4
        + [pltpu.VMEM((n_co, species) + slab, f32), pltpu.VMEM((5, species) + slab, f32)]
        + [pltpu.VMEM((species,) + slab, f32)] * 2
        + [pltpu.VMEM((count,) + slab, f32)] * 6
        + [pltpu.VMEM((rounds, count) + slab, f32)] * 2
        + [pltpu.VMEM(slab, f32), pltpu.VMEM((2,) + slab, f32)]
        + [pltpu.SemaphoreType.DMA((2,))] * 2
        + [pltpu.VMEM(block, f32)]
        + [pltpu.VMEM((steps,) + slab, f32)] * 4
        + [pltpu.VMEM((steps, species) + slab, f32)]
        + [pltpu.VMEM((3, species) + slab, f32)]
        + [pltpu.VMEM((species,) + slab, f32)] * 4
        + [pltpu.VMEM((steps, rounds, species) + slab, f32)] * 4
        + [pltpu.SemaphoreType.DMA((steps, n_slot))] * 2,
        compiler_params=pltpu.CompilerParams(collective_id=0, has_side_effects=True),
        cost_estimate=pl.CostEstimate(
            flops=100 * steps * species * depth * wide * tall, transcendentals=0,
            bytes_accessed=3 * 4 * species * depth * wide * tall,
        ),
    )(values, zone, porosity, axial_number, courant, transverse, plan[0], feed_conc[0])
    return out[None]


def solution(mesh):
    in_specs = (
        P("col", None, "axial", None, "trans"),
        P("col", None, "trans"),
        P(),
        P(),
        P(),
        P(),
        P("col", None),
        P("col", None, None),
    )
    out_specs = P("col", None, "axial", None, "trans")
    return jax.shard_map(body, mesh=mesh, in_specs=in_specs, out_specs=out_specs, check_vma=False)
```

```python
import functools

import jax
import jax.numpy as jnp
from jax import lax
from jax.experimental import pallas as pl
from jax.experimental.pallas import tpu as pltpu
from jax.sharding import PartitionSpec as P


def swapped(array, axis, distance):
    return lax.ppermute(array, axis, [(i, i ^ 1 << distance) for i in range(lax.axis_size(axis))])


def from_behind(value, axis, steps):
    count = lax.axis_size(axis)
    initial, last = (max(0, -steps), min(count, count - steps))
    return lax.ppermute(value, axis, [(source, source + steps) for source in range(initial, last)])


def void_map(zone_map, porosity):
    voids = jnp.zeros(zone_map.shape, porosity.dtype)
    for number in range(porosity.shape[0]):
        voids = voids + jnp.where(zone_map == number, porosity[number], 0.0)
    return voids


def _vmem():
    return pl.BlockSpec(memory_space=pltpu.VMEM)


ROUNDS = (1, 2, 4, 8)
MESH = pl.DeviceIdType.MESH


def porosity_of(zone, por_ref):
    voids = jnp.zeros(zone.shape, jnp.float32)
    for number in range(por_ref.shape[0]):
        voids = voids + jnp.where(zone == number, por_ref[number], 0.0)
    return voids


def stencil_weights(voids, voids_lo, voids_hi, tr_ref, w_ref):
    wide, tall = voids.shape
    sublane = lax.broadcasted_iota(jnp.int32, (wide, tall), 0)
    lane = lax.broadcasted_iota(jnp.int32, (wide, tall), 1)
    p_xm = jnp.where(sublane == 0, 0.0, pltpu.roll(voids, 1, 0))
    p_xp = jnp.where(sublane == wide - 1, 0.0, pltpu.roll(voids, wide - 1, 0))
    p_ym = jnp.where(lane == 0, jnp.broadcast_to(voids_lo, (wide, tall)), pltpu.roll(voids, 1, 1))
    p_yp = jnp.where(lane == tall - 1, jnp.broadcast_to(voids_hi, (wide, tall)), pltpu.roll(voids, tall - 1, 1))
    faces = [2.0 * p / (voids + p) for p in (p_xm, p_xp, p_ym, p_yp)]
    for s in range(w_ref.shape[1]):
        scaled = [tr_ref[s] * face for face in faces]
        for direction in range(4):
            w_ref[1 + direction, s] = scaled[direction]
        w_ref[0, s] = 1.0 - (scaled[0] + scaled[1] + scaled[2] + scaled[3])


def setup(count, voids, ax_ref, cour_ref, cp_ref, ip_ref, l_ref, r_ref, co_ref, sub_ref, sup_ref,
          qf_ref, qb_ref, mf_ref, mb_ref, cprev_ref, hnext_ref, exf_ref, exb_ref):
    species, depth, wide, tall = cp_ref.shape
    position = lax.axis_index("axial")
    rounds = len(ROUNDS)
    at_outlet = position == count - 1
    for s in range(species):
        dispersion = ax_ref[s] + jnp.zeros((wide, tall), jnp.float32)
        flow_rate = cour_ref[s] / voids
        sub = -(dispersion + flow_rate)
        sup = -dispersion
        mi = 1.0 + 2.0 * dispersion + flow_rate
        me = 1.0 + dispersion + flow_rate
        sub_ref[s] = sub
        sup_ref[s] = sup
        coef = None
        for z in range(depth - 1):
            pivot = mi if z == 0 else mi - sub * coef
            inv = 1.0 / pivot
            coef = sup * inv
            ip_ref[s, z] = inv
            cp_ref[s, z] = coef

        def ends(last):
            inv_last = 1.0 / (last - sub * cp_ref[s, depth - 2])
            down = ip_ref[s, 0]
            downs = [down]
            for z in range(1, depth - 1):
                down = -sub * down * ip_ref[s, z]
                downs.append(down)
            left = -sub * down * inv_last
            left_last = left
            for z in range(depth - 2, -1, -1):
                left = downs[z] - cp_ref[s, z] * left
            right = inv_last
            for z in range(depth - 2, -1, -1):
                right = -cp_ref[s, z] * right
            return left, left_last, right, inv_last

        l0i, l1i, r0i, r1i = ends(mi)
        l0o, l1o, r0o, r1o = ends(me)

        own_last = jnp.where(at_outlet, me, mi)
        inv_last = 1.0 / (own_last - sub * cp_ref[s, depth - 2])
        ip_ref[s, depth - 1] = inv_last
        cp_ref[s, depth - 1] = sup * inv_last
        down = ip_ref[s, 0]
        l_ref[s, 0] = down
        for z in range(1, depth):
            down = -sub * down * ip_ref[s, z]
            l_ref[s, z] = down
        left = down
        right = inv_last
        r_ref[s, depth - 1] = right
        for z in range(depth - 2, -1, -1):
            left = l_ref[s, z] - cp_ref[s, z] * left
            l_ref[s, z] = left
            right = -cp_ref[s, z] * right
            r_ref[s, z] = right

        zero = jnp.zeros_like(sub)
        one = jnp.ones_like(sub)
        inner = (-sub * l0i, -sub * l1i, -sup * r0i, -sup * r1i)
        first = (zero, zero, inner[2], inner[3])
        outlet = (-sub * l0o, -sub * l1o, zero, zero)

        def couplings(j):
            return first if j == 0 else outlet if j == count - 1 else inner

        c_prev = zero
        for j in range(count):
            p0, p1, q0, q1 = couplings(j)
            inv = one if j == 0 else 1.0 / (1.0 - p0 * c_prev)
            qf_ref[j] = p1 * inv
            mf_ref[j] = p1 * c_prev * inv
            cprev_ref[j] = c_prev
            c_prev = q1 + p1 * c_prev * q0 * inv
        h_next = zero
        for j in range(count - 1, -1, -1):
            p0, p1, q0, q1 = couplings(j)
            inv = one if j == count - 1 else 1.0 / (1.0 - q1 * h_next)
            qb_ref[j] = q0 * inv
            mb_ref[j] = q0 * h_next * inv
            hnext_ref[j] = h_next
            h_next = p0 + q0 * h_next * p1 * inv

        for kk in range(count):
            exf_ref[0, kk] = one
            exb_ref[0, kk] = one
        for r in range(rounds - 1):
            d = ROUNDS[r]
            for kk in range(count):
                if kk - d >= 0:
                    exf_ref[r + 1, kk] = exf_ref[r, kk] * qf_ref[kk - d] * exf_ref[r, kk - d]
                else:
                    exf_ref[r + 1, kk] = one
                if kk + d < count:
                    exb_ref[r + 1, kk] = exb_ref[r, kk] * qb_ref[kk + d] * exb_ref[r, kk + d]
                else:
                    exb_ref[r + 1, kk] = one

        co_ref[0, s] = mf_ref[position]
        co_ref[1, s] = mb_ref[position]
        qf_own = qf_ref[position]
        qb_own = qb_ref[position]
        for r in range(rounds):
            wef = exf_ref[r, position]
            web = exb_ref[r, position]
            co_ref[2 + r, s] = wef
            co_ref[2 + rounds + r, s] = qf_own * wef
            co_ref[2 + 2 * rounds + r, s] = web
            co_ref[2 + 3 * rounds + r, s] = qb_own * web
        at_first = position == 0
        at_last = position == count - 1
        p0 = jnp.where(at_first, zero, jnp.where(at_last, outlet[0], inner[0]))
        p1 = jnp.where(at_first, zero, jnp.where(at_last, outlet[1], inner[1]))
        q0 = jnp.where(at_last, zero, inner[2])
        q1 = jnp.where(at_last, zero, inner[3])
        c_own = cprev_ref[position]
        h_own = hnext_ref[position]
        a11 = 1.0 - p0 * c_own
        a12 = -q0 * h_own
        a21 = -p1 * c_own
        a22 = 1.0 - q1 * h_own
        inv_det = 1.0 / (a11 * a22 - a12 * a21)
        base = 2 + 4 * rounds
        for i, value in enumerate(
            (p0, p1, q0, q1, c_own, h_own, a22 * inv_det, -a12 * inv_det, -a21 * inv_det, a11 * inv_det)
        ):
            co_ref[base + i, s] = value


def fused_kernel(count, v_ref, zone_ref, por_ref, ax_ref, cour_ref, tr_ref, plan_ref, feed_ref,
                 o_ref,
                 cp_ref, ip_ref, l_ref, r_ref, co_ref, w_ref, sub_ref, sup_ref,
                 qf_ref, qb_ref, mf_ref, mb_ref, cprev_ref, hnext_ref, exf_ref, exb_ref,
                 vs_ref, vr_ref, vsem_s, vsem_r,
                 y_ref, hs_lo, hs_hi, hr_lo, hr_hi, face_in, g_ref, sf, sb, ef, eb,
                 snd_f, snd_b, rcv_f, rcv_b, send_sem, recv_sem):
    species, depth, wide, tall = v_ref.shape
    steps = plan_ref.shape[0]
    rounds = len(ROUNDS)
    position = lax.axis_index("axial")
    trans = lax.axis_index("trans")
    col = lax.axis_index("col")
    n_trans = lax.axis_size("trans")
    at_inlet = position == 0
    has_lo = trans > 0
    has_hi = trans < n_trans - 1
    lo_dev = (position, jnp.maximum(trans - 1, 0), col)
    hi_dev = (position, jnp.minimum(trans + 1, n_trans - 1), col)
    col_dev = (position, trans, 1 - col)
    lane = lax.broadcasted_iota(jnp.int32, (wide, tall), 1)
    base = 2 + 4 * rounds

    barrier = pltpu.get_barrier_semaphore()

    def greet(cond, device):
        @pl.when(cond)
        def _():
            pl.semaphore_signal(barrier, 1, device_id=device, device_id_type=MESH)

    greet(has_lo, lo_dev)
    greet(has_hi, hi_dev)
    greet(at_inlet, col_dev)
    partners = has_lo.astype(jnp.int32) + has_hi.astype(jnp.int32) + at_inlet.astype(jnp.int32)
    for d in ROUNDS:
        has_right = position + d < count
        has_left = position - d >= 0
        greet(has_right, (jnp.minimum(position + d, count - 1), trans, col))
        greet(has_left, (jnp.maximum(position - d, 0), trans, col))
        partners = partners + has_right.astype(jnp.int32) + has_left.astype(jnp.int32)
    voids = porosity_of(zone_ref[...], por_ref)
    vs_ref[...] = voids

    def run_setup():
        setup(count, voids, ax_ref, cour_ref, cp_ref, ip_ref, l_ref, r_ref, co_ref, sub_ref, sup_ref,
              qf_ref, qb_ref, mf_ref, mb_ref, cprev_ref, hnext_ref, exf_ref, exb_ref)

    pl.when(col == 0)(run_setup)
    pl.semaphore_wait(barrier, partners)

    zero_rows = jnp.zeros((species, wide, tall), jnp.float32)
    for h in range(steps):
        @pl.when(jnp.logical_not(has_lo))
        def _():
            hr_lo[h] = jnp.zeros((wide, tall), jnp.float32)

        @pl.when(jnp.logical_not(has_hi))
        def _():
            hr_hi[h] = jnp.zeros((wide, tall), jnp.float32)

        @pl.when(jnp.logical_not(at_inlet))
        def _():
            face_in[h] = zero_rows

    @pl.when(jnp.logical_not(has_lo))
    def _():
        vr_ref[0] = jnp.zeros((wide, tall), jnp.float32)

    @pl.when(jnp.logical_not(has_hi))
    def _():
        vr_ref[1] = jnp.zeros((wide, tall), jnp.float32)

    voids_up = pltpu.make_async_remote_copy(
        src_ref=vs_ref, dst_ref=vr_ref.at[0], send_sem=vsem_s.at[0], recv_sem=vsem_r.at[0],
        device_id=hi_dev, device_id_type=MESH,
    )
    voids_down = pltpu.make_async_remote_copy(
        src_ref=vs_ref, dst_ref=vr_ref.at[1], send_sem=vsem_s.at[1], recv_sem=vsem_r.at[1],
        device_id=lo_dev, device_id_type=MESH,
    )
    pl.when(has_hi)(voids_up.start)
    pl.when(has_lo)(voids_down.start)

    def exchange_start(h):
        src = v_ref if h == 0 else o_ref
        acc_lo = jnp.zeros((wide, tall), jnp.float32)
        acc_hi = jnp.zeros((wide, tall), jnp.float32)

        def column(s, z, c):
            if h == 0:
                return src[s, z, :, c : c + 1]
            cut = slice(c, c + 1)
            return (y_ref[s, z, :, cut] - ef[s, :, cut] * l_ref[s, z, :, cut]
                    - eb[s, :, cut] * r_ref[s, z, :, cut])

        for s in range(species):
            for z in range(depth):
                at = s * depth + z
                acc_lo = jnp.where(lane == at, jnp.broadcast_to(column(s, z, tall - 1), (wide, tall)), acc_lo)
                acc_hi = jnp.where(lane == at, jnp.broadcast_to(column(s, z, 0), (wide, tall)), acc_hi)
        hs_lo[h] = acc_lo
        hs_hi[h] = acc_hi
        copy_lo = pltpu.make_async_remote_copy(
            src_ref=hs_lo.at[h], dst_ref=hr_lo.at[h], send_sem=send_sem.at[h, 0], recv_sem=recv_sem.at[h, 0],
            device_id=hi_dev, device_id_type=MESH,
        )
        copy_hi = pltpu.make_async_remote_copy(
            src_ref=hs_hi.at[h], dst_ref=hr_hi.at[h], send_sem=send_sem.at[h, 1], recv_sem=recv_sem.at[h, 1],
            device_id=lo_dev, device_id_type=MESH,
        )
        copy_face = pltpu.make_async_remote_copy(
            src_ref=src.at[:, 0], dst_ref=face_in.at[h], send_sem=send_sem.at[h, 2], recv_sem=recv_sem.at[h, 2],
            device_id=col_dev, device_id_type=MESH,
        )
        pl.when(has_hi)(copy_lo.start)
        pl.when(has_lo)(copy_hi.start)
        pl.when(at_inlet)(copy_face.start)
        return copy_lo, copy_hi, copy_face

    def exchange_wait(copy_lo, copy_hi, copy_face):
        pl.when(has_lo)(copy_lo.wait_recv)
        pl.when(has_hi)(copy_hi.wait_recv)
        pl.when(has_hi)(copy_lo.wait_send)
        pl.when(has_lo)(copy_hi.wait_send)

    pending = exchange_start(0)
    pl.when(col != 0)(run_setup)
    pl.when(has_lo)(voids_up.wait_recv)
    pl.when(has_hi)(voids_down.wait_recv)
    pl.when(has_hi)(voids_up.wait_send)
    pl.when(has_lo)(voids_down.wait_send)
    voids_lo = jnp.where(has_lo, vr_ref[0, :, tall - 1 : tall], 0.0)
    voids_hi = jnp.where(has_hi, vr_ref[1, :, 0:1], 0.0)
    stencil_weights(voids, voids_lo, voids_hi, tr_ref, w_ref)

    for h in range(steps):
        src = v_ref if h == 0 else o_ref
        copy_lo, copy_hi, copy_face = pending
        exchange_wait(copy_lo, copy_hi, copy_face)

        for s in range(species):
            w0 = w_ref[0, s]
            wxm = w_ref[1, s]
            wxp = w_ref[2, s]
            wym = w_ref[3, s]
            wyp = w_ref[4, s]
            sub = sub_ref[s]
            down = None
            for z in range(depth):
                v = src[s, z]
                xm = pltpu.roll(v, 1, 0)
                xp = pltpu.roll(v, wide - 1, 0)
                at = s * depth + z
                ym = jnp.where(lane == 0, hr_lo[h, :, at : at + 1], pltpu.roll(v, 1, 1))
                yp = jnp.where(lane == tall - 1, hr_hi[h, :, at : at + 1], pltpu.roll(v, tall - 1, 1))
                moved = w0 * v + ((wxp * xp + wxm * xm) + (wyp * yp + wym * ym))
                if z == 0:
                    down = moved * ip_ref[s, 0]
                else:
                    down = (moved - sub * down) * ip_ref[s, z]
                y_ref[s, z] = down
            solved = down
            g_ref[1, s] = solved
            for z in range(depth - 2, -1, -1):
                solved = y_ref[s, z] - cp_ref[s, z] * solved
                y_ref[s, z] = solved
            g_ref[0, s] = solved

        pl.when(at_inlet)(copy_face.wait_recv)
        pl.when(at_inlet)(copy_face.wait_send)
        for s in range(species):
            recycled = (plan_ref[h, s].astype(jnp.float32) + 1.0) * 0.25
            inlet = (1.0 - recycled) * feed_ref[s] + recycled * face_in[h, s]
            entry = jnp.where(at_inlet, -sub_ref[s] * inlet, 0.0)
            g_ref[2, s] = entry
            g_ref[0, s] = g_ref[0, s] + entry * l_ref[s, 0]
            g_ref[1, s] = g_ref[1, s] + entry * l_ref[s, depth - 1]
        g0 = g_ref[0]
        g1 = g_ref[1]
        sf[...] = g1 + co_ref[0] * g0
        sb[...] = g0 + co_ref[1] * g1
        ef[...] = zero_rows
        eb[...] = zero_rows
        sent = []
        for r in range(rounds):
            snd_f[h, r] = sf[...]
            snd_b[h, r] = sb[...]
            rank = jnp.where(col == 0, r, rounds - 1 - r)
            d = jnp.where(col == 0, ROUNDS[r], ROUNDS[rounds - 1 - r])
            has_right = position + d < count
            has_left = position - d >= 0
            right = jnp.minimum(position + d, count - 1)
            left = jnp.maximum(position - d, 0)
            copy_f = pltpu.make_async_remote_copy(
                src_ref=snd_f.at[h, r], dst_ref=rcv_f.at[h, r],
                send_sem=send_sem.at[h, 3 + r], recv_sem=recv_sem.at[h, 3 + r],
                device_id=(right, trans, col), device_id_type=MESH,
            )
            copy_b = pltpu.make_async_remote_copy(
                src_ref=snd_b.at[h, r], dst_ref=rcv_b.at[h, r],
                send_sem=send_sem.at[h, 3 + rounds + r], recv_sem=recv_sem.at[h, 3 + rounds + r],
                device_id=(left, trans, col), device_id_type=MESH,
            )
            pl.when(has_right)(copy_f.start)
            pl.when(has_left)(copy_b.start)
            last_round = r == rounds - 1

            @pl.when(has_left)
            def _():
                copy_f.wait_recv()
                got = rcv_f[h, r]
                ef[...] += co_ref[2 + rank] * got
                if not last_round:
                    sf[...] += co_ref[2 + rounds + rank] * got

            @pl.when(has_right)
            def _():
                copy_b.wait_recv()
                got = rcv_b[h, r]
                eb[...] += co_ref[2 + 2 * rounds + rank] * got
                if not last_round:
                    sb[...] += co_ref[2 + 3 * rounds + rank] * got

            sent.append((has_right, copy_f))
            sent.append((has_left, copy_b))

        before = ef[...]
        after = eb[...]
        r1 = g0 + co_ref[base + 0] * before + co_ref[base + 2] * after
        r2 = g1 + co_ref[base + 1] * before + co_ref[base + 3] * after
        top = r1 * co_ref[base + 6] + r2 * co_ref[base + 7]
        bottom = r1 * co_ref[base + 8] + r2 * co_ref[base + 9]
        ef[...] = sub_ref[...] * (before + co_ref[base + 4] * top)
        eb[...] = sup_ref[...] * (after + co_ref[base + 5] * bottom)
        for cond, copy in sent:
            pl.when(cond)(copy.wait_send)
        for s in range(species):
            ef[s] = ef[s] - g_ref[2, s]
        rows = range(depth)
        if h + 1 < steps:
            for s in range(species):
                o_ref[s, 0] = y_ref[s, 0] - ef[s] * l_ref[s, 0] - eb[s] * r_ref[s, 0]
            pending = exchange_start(h + 1)
            rows = range(1, depth)
        for s in range(species):
            left_coef = ef[s]
            right_coef = eb[s]
            for z in rows:
                o_ref[s, z] = y_ref[s, z] - left_coef * l_ref[s, z] - right_coef * r_ref[s, z]


def body(concentration, zone_map, porosity, axial_number, courant, transverse, feed_conc, plan):
    f32 = jnp.float32
    count = lax.axis_size("axial")
    values = concentration[0]
    species, depth, wide, tall = values.shape
    steps = plan.shape[1]
    zone = zone_map[0]
    assert species * depth <= tall
    rounds = len(ROUNDS)
    n_co = 2 + 4 * rounds + 10
    slab = (wide, tall)
    block = (species, depth) + slab
    smem = pl.BlockSpec(memory_space=pltpu.SMEM)

    n_slot = 3 + 2 * rounds
    out = pl.pallas_call(
        functools.partial(fused_kernel, count),
        out_shape=jax.ShapeDtypeStruct(block, f32),
        in_specs=[_vmem()] * 2 + [smem] * 6,
        out_specs=_vmem(),
        scratch_shapes=[pltpu.VMEM(block, f32)] * 4
        + [pltpu.VMEM((n_co, species) + slab, f32), pltpu.VMEM((5, species) + slab, f32)]
        + [pltpu.VMEM((species,) + slab, f32)] * 2
        + [pltpu.VMEM((count,) + slab, f32)] * 6
        + [pltpu.VMEM((rounds, count) + slab, f32)] * 2
        + [pltpu.VMEM(slab, f32), pltpu.VMEM((2,) + slab, f32)]
        + [pltpu.SemaphoreType.DMA((2,))] * 2
        + [pltpu.VMEM(block, f32)]
        + [pltpu.VMEM((steps,) + slab, f32)] * 4
        + [pltpu.VMEM((steps, species) + slab, f32)]
        + [pltpu.VMEM((3, species) + slab, f32)]
        + [pltpu.VMEM((species,) + slab, f32)] * 4
        + [pltpu.VMEM((steps, rounds, species) + slab, f32)] * 4
        + [pltpu.SemaphoreType.DMA((steps, n_slot))] * 2,
        compiler_params=pltpu.CompilerParams(collective_id=0, has_side_effects=True),
        cost_estimate=pl.CostEstimate(
            flops=100 * steps * species * depth * wide * tall, transcendentals=0,
            bytes_accessed=3 * 4 * species * depth * wide * tall,
        ),
    )(values, zone, porosity, axial_number, courant, transverse, plan[0], feed_conc[0])
    return out[None]


def solution(mesh):
    in_specs = (
        P("col", None, "axial", None, "trans"),
        P("col", None, "trans"),
        P(),
        P(),
        P(),
        P(),
        P("col", None),
        P("col", None, None),
    )
    out_specs = P("col", None, "axial", None, "trans")
    return jax.shard_map(body, mesh=mesh, in_specs=in_specs, out_specs=out_specs, check_vma=False)
```

```python
import functools

import jax
import jax.numpy as jnp
from jax import lax
from jax.experimental import pallas as pl
from jax.experimental.pallas import tpu as pltpu
from jax.sharding import PartitionSpec as P


def swapped(array, axis, distance):
    return lax.ppermute(array, axis, [(i, i ^ 1 << distance) for i in range(lax.axis_size(axis))])


def from_behind(value, axis, steps):
    count = lax.axis_size(axis)
    initial, last = (max(0, -steps), min(count, count - steps))
    return lax.ppermute(value, axis, [(source, source + steps) for source in range(initial, last)])


def void_map(zone_map, porosity):
    voids = jnp.zeros(zone_map.shape, porosity.dtype)
    for number in range(porosity.shape[0]):
        voids = voids + jnp.where(zone_map == number, porosity[number], 0.0)
    return voids


def _vmem():
    return pl.BlockSpec(memory_space=pltpu.VMEM)


ROUNDS = (1, 2, 4, 8)
MESH = pl.DeviceIdType.MESH


def porosity_of(zone, por_ref):
    voids = jnp.zeros(zone.shape, jnp.float32)
    for number in range(por_ref.shape[0]):
        voids = voids + jnp.where(zone == number, por_ref[number], 0.0)
    return voids


def stencil_weights(voids, voids_lo, voids_hi, tr_ref, w_ref):
    wide, tall = voids.shape
    sublane = lax.broadcasted_iota(jnp.int32, (wide, tall), 0)
    lane = lax.broadcasted_iota(jnp.int32, (wide, tall), 1)
    p_xm = jnp.where(sublane == 0, 0.0, pltpu.roll(voids, 1, 0))
    p_xp = jnp.where(sublane == wide - 1, 0.0, pltpu.roll(voids, wide - 1, 0))
    p_ym = jnp.where(lane == 0, jnp.broadcast_to(voids_lo, (wide, tall)), pltpu.roll(voids, 1, 1))
    p_yp = jnp.where(lane == tall - 1, jnp.broadcast_to(voids_hi, (wide, tall)), pltpu.roll(voids, tall - 1, 1))
    faces = [2.0 * p / (voids + p) for p in (p_xm, p_xp, p_ym, p_yp)]
    for s in range(w_ref.shape[1]):
        scaled = [tr_ref[s] * face for face in faces]
        for direction in range(4):
            w_ref[1 + direction, s] = scaled[direction]
        w_ref[0, s] = 1.0 - (scaled[0] + scaled[1] + scaled[2] + scaled[3])


def setup(count, voids, ax_ref, cour_ref, cp_ref, ip_ref, l_ref, r_ref, co_ref, sub_ref, sup_ref,
          qf_ref, qb_ref, mf_ref, mb_ref, cprev_ref, hnext_ref, exf_ref, exb_ref):
    species, depth, wide, tall = cp_ref.shape
    position = lax.axis_index("axial")
    rounds = len(ROUNDS)
    at_outlet = position == count - 1
    for s in range(species):
        dispersion = ax_ref[s] + jnp.zeros((wide, tall), jnp.float32)
        flow_rate = cour_ref[s] / voids
        sub = -(dispersion + flow_rate)
        sup = -dispersion
        mi = 1.0 + 2.0 * dispersion + flow_rate
        me = 1.0 + dispersion + flow_rate
        sub_ref[s] = sub
        sup_ref[s] = sup
        coef = None
        for z in range(depth - 1):
            pivot = mi if z == 0 else mi - sub * coef
            inv = 1.0 / pivot
            coef = sup * inv
            ip_ref[s, z] = inv
            cp_ref[s, z] = coef

        def ends(last):
            inv_last = 1.0 / (last - sub * cp_ref[s, depth - 2])
            down = ip_ref[s, 0]
            downs = [down]
            for z in range(1, depth - 1):
                down = -sub * down * ip_ref[s, z]
                downs.append(down)
            left = -sub * down * inv_last
            left_last = left
            for z in range(depth - 2, -1, -1):
                left = downs[z] - cp_ref[s, z] * left
            right = inv_last
            for z in range(depth - 2, -1, -1):
                right = -cp_ref[s, z] * right
            return left, left_last, right, inv_last

        l0i, l1i, r0i, r1i = ends(mi)
        l0o, l1o, r0o, r1o = ends(me)

        own_last = jnp.where(at_outlet, me, mi)
        inv_last = 1.0 / (own_last - sub * cp_ref[s, depth - 2])
        ip_ref[s, depth - 1] = inv_last
        cp_ref[s, depth - 1] = sup * inv_last
        down = ip_ref[s, 0]
        l_ref[s, 0] = down
        for z in range(1, depth):
            down = -sub * down * ip_ref[s, z]
            l_ref[s, z] = down
        left = down
        right = inv_last
        r_ref[s, depth - 1] = right
        for z in range(depth - 2, -1, -1):
            left = l_ref[s, z] - cp_ref[s, z] * left
            l_ref[s, z] = left
            right = -cp_ref[s, z] * right
            r_ref[s, z] = right

        zero = jnp.zeros_like(sub)
        one = jnp.ones_like(sub)
        inner = (-sub * l0i, -sub * l1i, -sup * r0i, -sup * r1i)
        first = (zero, zero, inner[2], inner[3])
        outlet = (-sub * l0o, -sub * l1o, zero, zero)

        def couplings(j):
            return first if j == 0 else outlet if j == count - 1 else inner

        c_prev = zero
        for j in range(count):
            p0, p1, q0, q1 = couplings(j)
            inv = one if j == 0 else 1.0 / (1.0 - p0 * c_prev)
            qf_ref[j] = p1 * inv
            mf_ref[j] = p1 * c_prev * inv
            cprev_ref[j] = c_prev
            c_prev = q1 + p1 * c_prev * q0 * inv
        h_next = zero
        for j in range(count - 1, -1, -1):
            p0, p1, q0, q1 = couplings(j)
            inv = one if j == count - 1 else 1.0 / (1.0 - q1 * h_next)
            qb_ref[j] = q0 * inv
            mb_ref[j] = q0 * h_next * inv
            hnext_ref[j] = h_next
            h_next = p0 + q0 * h_next * p1 * inv

        for kk in range(count):
            exf_ref[0, kk] = one
            exb_ref[0, kk] = one
        for r in range(rounds - 1):
            d = ROUNDS[r]
            for kk in range(count):
                if kk - d >= 0:
                    exf_ref[r + 1, kk] = exf_ref[r, kk] * qf_ref[kk - d] * exf_ref[r, kk - d]
                else:
                    exf_ref[r + 1, kk] = one
                if kk + d < count:
                    exb_ref[r + 1, kk] = exb_ref[r, kk] * qb_ref[kk + d] * exb_ref[r, kk + d]
                else:
                    exb_ref[r + 1, kk] = one

        co_ref[0, s] = mf_ref[position]
        co_ref[1, s] = mb_ref[position]
        qf_own = qf_ref[position]
        qb_own = qb_ref[position]
        for r in range(rounds):
            wef = exf_ref[r, position]
            web = exb_ref[r, position]
            co_ref[2 + r, s] = wef
            co_ref[2 + rounds + r, s] = qf_own * wef
            co_ref[2 + 2 * rounds + r, s] = web
            co_ref[2 + 3 * rounds + r, s] = qb_own * web
        at_first = position == 0
        at_last = position == count - 1
        p0 = jnp.where(at_first, zero, jnp.where(at_last, outlet[0], inner[0]))
        p1 = jnp.where(at_first, zero, jnp.where(at_last, outlet[1], inner[1]))
        q0 = jnp.where(at_last, zero, inner[2])
        q1 = jnp.where(at_last, zero, inner[3])
        c_own = cprev_ref[position]
        h_own = hnext_ref[position]
        a11 = 1.0 - p0 * c_own
        a12 = -q0 * h_own
        a21 = -p1 * c_own
        a22 = 1.0 - q1 * h_own
        inv_det = 1.0 / (a11 * a22 - a12 * a21)
        base = 2 + 4 * rounds
        for i, value in enumerate(
            (p0, p1, q0, q1, c_own, h_own, a22 * inv_det, -a12 * inv_det, -a21 * inv_det, a11 * inv_det)
        ):
            co_ref[base + i, s] = value


def fused_kernel(count, v_ref, zone_ref, por_ref, ax_ref, cour_ref, tr_ref, plan_ref, feed_ref,
                 o_ref,
                 cp_ref, ip_ref, l_ref, r_ref, co_ref, w_ref, sub_ref, sup_ref,
                 qf_ref, qb_ref, mf_ref, mb_ref, cprev_ref, hnext_ref, exf_ref, exb_ref,
                 vs_ref, vr_ref, vsem_s, vsem_r,
                 y_ref, hs_lo, hs_hi, hr_lo, hr_hi, face_in, g_ref, sf, sb, ef, eb,
                 snd_f, snd_b, rcv_f, rcv_b, send_sem, recv_sem):
    species, depth, wide, tall = v_ref.shape
    steps = plan_ref.shape[0]
    rounds = len(ROUNDS)
    position = lax.axis_index("axial")
    trans = lax.axis_index("trans")
    col = lax.axis_index("col")
    n_trans = lax.axis_size("trans")
    at_inlet = position == 0
    has_lo = trans > 0
    has_hi = trans < n_trans - 1
    lo_dev = (position, jnp.maximum(trans - 1, 0), col)
    hi_dev = (position, jnp.minimum(trans + 1, n_trans - 1), col)
    col_dev = (position, trans, 1 - col)
    lane = lax.broadcasted_iota(jnp.int32, (wide, tall), 1)
    base = 2 + 4 * rounds

    barrier = pltpu.get_barrier_semaphore()

    def greet(cond, device):
        @pl.when(cond)
        def _():
            pl.semaphore_signal(barrier, 1, device_id=device, device_id_type=MESH)

    greet(has_lo, lo_dev)
    greet(has_hi, hi_dev)
    greet(at_inlet, col_dev)
    partners = has_lo.astype(jnp.int32) + has_hi.astype(jnp.int32) + at_inlet.astype(jnp.int32)
    for d in ROUNDS:
        has_right = position + d < count
        has_left = position - d >= 0
        greet(has_right, (jnp.minimum(position + d, count - 1), trans, col))
        greet(has_left, (jnp.maximum(position - d, 0), trans, col))
        partners = partners + has_right.astype(jnp.int32) + has_left.astype(jnp.int32)
    voids = porosity_of(zone_ref[...], por_ref)
    vs_ref[...] = voids

    def run_setup():
        setup(count, voids, ax_ref, cour_ref, cp_ref, ip_ref, l_ref, r_ref, co_ref, sub_ref, sup_ref,
              qf_ref, qb_ref, mf_ref, mb_ref, cprev_ref, hnext_ref, exf_ref, exb_ref)

    pl.when(col == 0)(run_setup)
    pl.semaphore_wait(barrier, partners)

    zero_rows = jnp.zeros((species, wide, tall), jnp.float32)
    for h in range(steps):
        @pl.when(jnp.logical_not(has_lo))
        def _():
            hr_lo[h] = jnp.zeros((wide, tall), jnp.float32)

        @pl.when(jnp.logical_not(has_hi))
        def _():
            hr_hi[h] = jnp.zeros((wide, tall), jnp.float32)

        @pl.when(jnp.logical_not(at_inlet))
        def _():
            face_in[h] = zero_rows

    @pl.when(jnp.logical_not(has_lo))
    def _():
        vr_ref[0] = jnp.zeros((wide, tall), jnp.float32)

    @pl.when(jnp.logical_not(has_hi))
    def _():
        vr_ref[1] = jnp.zeros((wide, tall), jnp.float32)

    voids_up = pltpu.make_async_remote_copy(
        src_ref=vs_ref, dst_ref=vr_ref.at[0], send_sem=vsem_s.at[0], recv_sem=vsem_r.at[0],
        device_id=hi_dev, device_id_type=MESH,
    )
    voids_down = pltpu.make_async_remote_copy(
        src_ref=vs_ref, dst_ref=vr_ref.at[1], send_sem=vsem_s.at[1], recv_sem=vsem_r.at[1],
        device_id=lo_dev, device_id_type=MESH,
    )
    pl.when(has_hi)(voids_up.start)
    pl.when(has_lo)(voids_down.start)

    def exchange_start(h):
        src = v_ref if h == 0 else o_ref
        acc_lo = jnp.zeros((wide, tall), jnp.float32)
        acc_hi = jnp.zeros((wide, tall), jnp.float32)

        def column(s, z, c):
            if h == 0:
                return src[s, z, :, c : c + 1]
            cut = slice(c, c + 1)
            return (y_ref[s, z, :, cut] - ef[s, :, cut] * l_ref[s, z, :, cut]
                    - eb[s, :, cut] * r_ref[s, z, :, cut])

        for s in range(species):
            for z in range(depth):
                at = s * depth + z
                acc_lo = jnp.where(lane == at, jnp.broadcast_to(column(s, z, tall - 1), (wide, tall)), acc_lo)
                acc_hi = jnp.where(lane == at, jnp.broadcast_to(column(s, z, 0), (wide, tall)), acc_hi)
        hs_lo[h] = acc_lo
        hs_hi[h] = acc_hi
        copy_lo = pltpu.make_async_remote_copy(
            src_ref=hs_lo.at[h], dst_ref=hr_lo.at[h], send_sem=send_sem.at[h, 0], recv_sem=recv_sem.at[h, 0],
            device_id=hi_dev, device_id_type=MESH,
        )
        copy_hi = pltpu.make_async_remote_copy(
            src_ref=hs_hi.at[h], dst_ref=hr_hi.at[h], send_sem=send_sem.at[h, 1], recv_sem=recv_sem.at[h, 1],
            device_id=lo_dev, device_id_type=MESH,
        )
        copy_face = pltpu.make_async_remote_copy(
            src_ref=src.at[:, 0], dst_ref=face_in.at[h], send_sem=send_sem.at[h, 2], recv_sem=recv_sem.at[h, 2],
            device_id=col_dev, device_id_type=MESH,
        )
        pl.when(has_hi)(copy_lo.start)
        pl.when(has_lo)(copy_hi.start)
        pl.when(at_inlet)(copy_face.start)
        return copy_lo, copy_hi, copy_face

    def exchange_wait(copy_lo, copy_hi, copy_face):
        pl.when(has_lo)(copy_lo.wait_recv)
        pl.when(has_hi)(copy_hi.wait_recv)
        pl.when(has_hi)(copy_lo.wait_send)
        pl.when(has_lo)(copy_hi.wait_send)

    pending = exchange_start(0)
    pl.when(col != 0)(run_setup)
    pl.when(has_lo)(voids_up.wait_recv)
    pl.when(has_hi)(voids_down.wait_recv)
    pl.when(has_hi)(voids_up.wait_send)
    pl.when(has_lo)(voids_down.wait_send)
    voids_lo = jnp.where(has_lo, vr_ref[0, :, tall - 1 : tall], 0.0)
    voids_hi = jnp.where(has_hi, vr_ref[1, :, 0:1], 0.0)
    stencil_weights(voids, voids_lo, voids_hi, tr_ref, w_ref)

    for h in range(steps):
        src = v_ref if h == 0 else o_ref
        copy_lo, copy_hi, copy_face = pending
        exchange_wait(copy_lo, copy_hi, copy_face)

        for s in range(species):
            w0 = w_ref[0, s]
            wxm = w_ref[1, s]
            wxp = w_ref[2, s]
            wym = w_ref[3, s]
            wyp = w_ref[4, s]
            sub = sub_ref[s]
            down = None
            for z in range(depth):
                v = src[s, z]
                xm = pltpu.roll(v, 1, 0)
                xp = pltpu.roll(v, wide - 1, 0)
                at = s * depth + z
                ym = jnp.where(lane == 0, hr_lo[h, :, at : at + 1], pltpu.roll(v, 1, 1))
                yp = jnp.where(lane == tall - 1, hr_hi[h, :, at : at + 1], pltpu.roll(v, tall - 1, 1))
                moved = w0 * v + ((wxp * xp + wxm * xm) + (wyp * yp + wym * ym))
                if z == 0:
                    down = moved * ip_ref[s, 0]
                else:
                    down = (moved - sub * down) * ip_ref[s, z]
                y_ref[s, z] = down
            solved = down
            g_ref[1, s] = solved
            for z in range(depth - 2, -1, -1):
                solved = y_ref[s, z] - cp_ref[s, z] * solved
                y_ref[s, z] = solved
            g_ref[0, s] = solved

        pl.when(at_inlet)(copy_face.wait_recv)
        pl.when(at_inlet)(copy_face.wait_send)
        for s in range(species):
            recycled = (plan_ref[h, s].astype(jnp.float32) + 1.0) * 0.25
            inlet = (1.0 - recycled) * feed_ref[s] + recycled * face_in[h, s]
            entry = jnp.where(at_inlet, -sub_ref[s] * inlet, 0.0)
            g_ref[2, s] = entry
            g_ref[0, s] = g_ref[0, s] + entry * l_ref[s, 0]
            g_ref[1, s] = g_ref[1, s] + entry * l_ref[s, depth - 1]
        g0 = g_ref[0]
        g1 = g_ref[1]
        sf[...] = g1 + co_ref[0] * g0
        sb[...] = g0 + co_ref[1] * g1
        ef[...] = zero_rows
        eb[...] = zero_rows
        sent = []
        for r in range(rounds):
            snd_f[h, r] = sf[...]
            snd_b[h, r] = sb[...]
            rank = r
            d = ROUNDS[r]
            has_right = position + d < count
            has_left = position - d >= 0
            right = jnp.minimum(position + d, count - 1)
            left = jnp.maximum(position - d, 0)
            copy_f = pltpu.make_async_remote_copy(
                src_ref=snd_f.at[h, r], dst_ref=rcv_f.at[h, r],
                send_sem=send_sem.at[h, 3 + r], recv_sem=recv_sem.at[h, 3 + r],
                device_id=(right, trans, col), device_id_type=MESH,
            )
            copy_b = pltpu.make_async_remote_copy(
                src_ref=snd_b.at[h, r], dst_ref=rcv_b.at[h, r],
                send_sem=send_sem.at[h, 3 + rounds + r], recv_sem=recv_sem.at[h, 3 + rounds + r],
                device_id=(left, trans, col), device_id_type=MESH,
            )
            pl.when(has_right)(copy_f.start)
            pl.when(has_left)(copy_b.start)
            last_round = r == rounds - 1

            @pl.when(has_left)
            def _():
                copy_f.wait_recv()
                got = rcv_f[h, r]
                ef[...] += co_ref[2 + rank] * got
                if not last_round:
                    sf[...] += co_ref[2 + rounds + rank] * got

            @pl.when(has_right)
            def _():
                copy_b.wait_recv()
                got = rcv_b[h, r]
                eb[...] += co_ref[2 + 2 * rounds + rank] * got
                if not last_round:
                    sb[...] += co_ref[2 + 3 * rounds + rank] * got

            sent.append((has_right, copy_f))
            sent.append((has_left, copy_b))

        before = ef[...]
        after = eb[...]
        r1 = g0 + co_ref[base + 0] * before + co_ref[base + 2] * after
        r2 = g1 + co_ref[base + 1] * before + co_ref[base + 3] * after
        top = r1 * co_ref[base + 6] + r2 * co_ref[base + 7]
        bottom = r1 * co_ref[base + 8] + r2 * co_ref[base + 9]
        ef[...] = sub_ref[...] * (before + co_ref[base + 4] * top)
        eb[...] = sup_ref[...] * (after + co_ref[base + 5] * bottom)
        for cond, copy in sent:
            pl.when(cond)(copy.wait_send)
        for s in range(species):
            ef[s] = ef[s] - g_ref[2, s]
        rows = range(depth)
        if h + 1 < steps:
            for s in range(species):
                o_ref[s, 0] = y_ref[s, 0] - ef[s] * l_ref[s, 0] - eb[s] * r_ref[s, 0]
            pending = exchange_start(h + 1)
            rows = range(1, depth)
        for s in range(species):
            left_coef = ef[s]
            right_coef = eb[s]
            for z in rows:
                o_ref[s, z] = y_ref[s, z] - left_coef * l_ref[s, z] - right_coef * r_ref[s, z]


def body(concentration, zone_map, porosity, axial_number, courant, transverse, feed_conc, plan):
    f32 = jnp.float32
    count = lax.axis_size("axial")
    values = concentration[0]
    species, depth, wide, tall = values.shape
    steps = plan.shape[1]
    zone = zone_map[0]
    assert species * depth <= tall
    rounds = len(ROUNDS)
    n_co = 2 + 4 * rounds + 10
    slab = (wide, tall)
    block = (species, depth) + slab
    smem = pl.BlockSpec(memory_space=pltpu.SMEM)

    n_slot = 3 + 2 * rounds
    out = pl.pallas_call(
        functools.partial(fused_kernel, count),
        out_shape=jax.ShapeDtypeStruct(block, f32),
        in_specs=[_vmem()] * 2 + [smem] * 6,
        out_specs=_vmem(),
        scratch_shapes=[pltpu.VMEM(block, f32)] * 4
        + [pltpu.VMEM((n_co, species) + slab, f32), pltpu.VMEM((5, species) + slab, f32)]
        + [pltpu.VMEM((species,) + slab, f32)] * 2
        + [pltpu.VMEM((count,) + slab, f32)] * 6
        + [pltpu.VMEM((rounds, count) + slab, f32)] * 2
        + [pltpu.VMEM(slab, f32), pltpu.VMEM((2,) + slab, f32)]
        + [pltpu.SemaphoreType.DMA((2,))] * 2
        + [pltpu.VMEM(block, f32)]
        + [pltpu.VMEM((steps,) + slab, f32)] * 4
        + [pltpu.VMEM((steps, species) + slab, f32)]
        + [pltpu.VMEM((3, species) + slab, f32)]
        + [pltpu.VMEM((species,) + slab, f32)] * 4
        + [pltpu.VMEM((steps, rounds, species) + slab, f32)] * 4
        + [pltpu.SemaphoreType.DMA((steps, n_slot))] * 2,
        compiler_params=pltpu.CompilerParams(collective_id=0, has_side_effects=True),
        cost_estimate=pl.CostEstimate(
            flops=100 * steps * species * depth * wide * tall, transcendentals=0,
            bytes_accessed=3 * 4 * species * depth * wide * tall,
        ),
    )(values, zone, porosity, axial_number, courant, transverse, plan[0], feed_conc[0])
    return out[None]


def solution(mesh):
    in_specs = (
        P("col", None, "axial", None, "trans"),
        P("col", None, "trans"),
        P(),
        P(),
        P(),
        P(),
        P("col", None),
        P("col", None, None),
    )
    out_specs = P("col", None, "axial", None, "trans")
    return jax.shard_map(body, mesh=mesh, in_specs=in_specs, out_specs=out_specs, check_vma=False)
```

```python
import functools

import jax
import jax.numpy as jnp
from jax import lax
from jax.experimental import pallas as pl
from jax.experimental.pallas import tpu as pltpu
from jax.sharding import PartitionSpec as P


def swapped(array, axis, distance):
    return lax.ppermute(array, axis, [(i, i ^ 1 << distance) for i in range(lax.axis_size(axis))])


def from_behind(value, axis, steps):
    count = lax.axis_size(axis)
    initial, last = (max(0, -steps), min(count, count - steps))
    return lax.ppermute(value, axis, [(source, source + steps) for source in range(initial, last)])


def void_map(zone_map, porosity):
    voids = jnp.zeros(zone_map.shape, porosity.dtype)
    for number in range(porosity.shape[0]):
        voids = voids + jnp.where(zone_map == number, porosity[number], 0.0)
    return voids


def _vmem():
    return pl.BlockSpec(memory_space=pltpu.VMEM)


ROUNDS = (1, 2, 4, 8)
MESH = pl.DeviceIdType.MESH


def porosity_of(zone, por_ref):
    voids = jnp.zeros(zone.shape, jnp.float32)
    for number in range(por_ref.shape[0]):
        voids = voids + jnp.where(zone == number, por_ref[number], 0.0)
    return voids


def stencil_weights(voids, voids_lo, voids_hi, tr_ref, w_ref):
    wide, tall = voids.shape
    sublane = lax.broadcasted_iota(jnp.int32, (wide, tall), 0)
    lane = lax.broadcasted_iota(jnp.int32, (wide, tall), 1)
    p_xm = jnp.where(sublane == 0, 0.0, pltpu.roll(voids, 1, 0))
    p_xp = jnp.where(sublane == wide - 1, 0.0, pltpu.roll(voids, wide - 1, 0))
    p_ym = jnp.where(lane == 0, jnp.broadcast_to(voids_lo, (wide, tall)), pltpu.roll(voids, 1, 1))
    p_yp = jnp.where(lane == tall - 1, jnp.broadcast_to(voids_hi, (wide, tall)), pltpu.roll(voids, tall - 1, 1))
    faces = [2.0 * p / (voids + p) for p in (p_xm, p_xp, p_ym, p_yp)]
    for s in range(w_ref.shape[1]):
        scaled = [tr_ref[s] * face for face in faces]
        for direction in range(4):
            w_ref[1 + direction, s] = scaled[direction]
        w_ref[0, s] = 1.0 - (scaled[0] + scaled[1] + scaled[2] + scaled[3])


def setup(count, voids, ax_ref, cour_ref, cp_ref, ip_ref, l_ref, r_ref, co_ref, sub_ref, sup_ref,
          qf_ref, qb_ref, mf_ref, mb_ref, cprev_ref, hnext_ref, exf_ref, exb_ref):
    species, depth, wide, tall = cp_ref.shape
    position = lax.axis_index("axial")
    rounds = len(ROUNDS)
    at_outlet = position == count - 1
    for s in range(species):
        dispersion = ax_ref[s] + jnp.zeros((wide, tall), jnp.float32)
        flow_rate = cour_ref[s] / voids
        sub = -(dispersion + flow_rate)
        sup = -dispersion
        mi = 1.0 + 2.0 * dispersion + flow_rate
        me = 1.0 + dispersion + flow_rate
        sub_ref[s] = sub
        sup_ref[s] = sup
        coef = None
        for z in range(depth - 1):
            pivot = mi if z == 0 else mi - sub * coef
            inv = 1.0 / pivot
            coef = sup * inv
            ip_ref[s, z] = inv
            cp_ref[s, z] = coef

        def ends(last):
            inv_last = 1.0 / (last - sub * cp_ref[s, depth - 2])
            down = ip_ref[s, 0]
            downs = [down]
            for z in range(1, depth - 1):
                down = -sub * down * ip_ref[s, z]
                downs.append(down)
            left = -sub * down * inv_last
            left_last = left
            for z in range(depth - 2, -1, -1):
                left = downs[z] - cp_ref[s, z] * left
            right = inv_last
            for z in range(depth - 2, -1, -1):
                right = -cp_ref[s, z] * right
            return left, left_last, right, inv_last

        l0i, l1i, r0i, r1i = ends(mi)
        l0o, l1o, r0o, r1o = ends(me)

        own_last = jnp.where(at_outlet, me, mi)
        inv_last = 1.0 / (own_last - sub * cp_ref[s, depth - 2])
        ip_ref[s, depth - 1] = inv_last
        cp_ref[s, depth - 1] = sup * inv_last
        down = ip_ref[s, 0]
        l_ref[s, 0] = down
        for z in range(1, depth):
            down = -sub * down * ip_ref[s, z]
            l_ref[s, z] = down
        left = down
        right = inv_last
        r_ref[s, depth - 1] = right
        for z in range(depth - 2, -1, -1):
            left = l_ref[s, z] - cp_ref[s, z] * left
            l_ref[s, z] = left
            right = -cp_ref[s, z] * right
            r_ref[s, z] = right

        zero = jnp.zeros_like(sub)
        one = jnp.ones_like(sub)
        inner = (-sub * l0i, -sub * l1i, -sup * r0i, -sup * r1i)
        first = (zero, zero, inner[2], inner[3])
        outlet = (-sub * l0o, -sub * l1o, zero, zero)

        def couplings(j):
            return first if j == 0 else outlet if j == count - 1 else inner

        c_prev = zero
        for j in range(count):
            p0, p1, q0, q1 = couplings(j)
            inv = one if j == 0 else 1.0 / (1.0 - p0 * c_prev)
            qf_ref[j] = p1 * inv
            mf_ref[j] = p1 * c_prev * inv
            cprev_ref[j] = c_prev
            c_prev = q1 + p1 * c_prev * q0 * inv
        h_next = zero
        for j in range(count - 1, -1, -1):
            p0, p1, q0, q1 = couplings(j)
            inv = one if j == count - 1 else 1.0 / (1.0 - q1 * h_next)
            qb_ref[j] = q0 * inv
            mb_ref[j] = q0 * h_next * inv
            hnext_ref[j] = h_next
            h_next = p0 + q0 * h_next * p1 * inv

        for kk in range(count):
            exf_ref[0, kk] = one
            exb_ref[0, kk] = one
        for r in range(rounds - 1):
            d = ROUNDS[r]
            for kk in range(count):
                if kk - d >= 0:
                    exf_ref[r + 1, kk] = exf_ref[r, kk] * qf_ref[kk - d] * exf_ref[r, kk - d]
                else:
                    exf_ref[r + 1, kk] = one
                if kk + d < count:
                    exb_ref[r + 1, kk] = exb_ref[r, kk] * qb_ref[kk + d] * exb_ref[r, kk + d]
                else:
                    exb_ref[r + 1, kk] = one

        co_ref[0, s] = mf_ref[position]
        co_ref[1, s] = mb_ref[position]
        qf_own = qf_ref[position]
        qb_own = qb_ref[position]
        for r in range(rounds):
            wef = exf_ref[r, position]
            web = exb_ref[r, position]
            co_ref[2 + r, s] = wef
            co_ref[2 + rounds + r, s] = qf_own * wef
            co_ref[2 + 2 * rounds + r, s] = web
            co_ref[2 + 3 * rounds + r, s] = qb_own * web
        at_first = position == 0
        at_last = position == count - 1
        p0 = jnp.where(at_first, zero, jnp.where(at_last, outlet[0], inner[0]))
        p1 = jnp.where(at_first, zero, jnp.where(at_last, outlet[1], inner[1]))
        q0 = jnp.where(at_last, zero, inner[2])
        q1 = jnp.where(at_last, zero, inner[3])
        c_own = cprev_ref[position]
        h_own = hnext_ref[position]
        a11 = 1.0 - p0 * c_own
        a12 = -q0 * h_own
        a21 = -p1 * c_own
        a22 = 1.0 - q1 * h_own
        inv_det = 1.0 / (a11 * a22 - a12 * a21)
        base = 2 + 4 * rounds
        for i, value in enumerate(
            (p0, p1, q0, q1, c_own, h_own, a22 * inv_det, -a12 * inv_det, -a21 * inv_det, a11 * inv_det)
        ):
            co_ref[base + i, s] = value


def fused_kernel(count, v_ref, zone_ref, por_ref, ax_ref, cour_ref, tr_ref, plan_ref, feed_ref,
                 o_ref,
                 cp_ref, ip_ref, l_ref, r_ref, co_ref, w_ref, sub_ref, sup_ref,
                 qf_ref, qb_ref, mf_ref, mb_ref, cprev_ref, hnext_ref, exf_ref, exb_ref,
                 vs_ref, vr_ref, vsem_s, vsem_r,
                 y_ref, hs_lo, hs_hi, hr_lo, hr_hi, face_in, g_ref, sf, sb, ef, eb,
                 snd_f, snd_b, rcv_f, rcv_b, send_sem, recv_sem):
    species, depth, wide, tall = v_ref.shape
    steps = plan_ref.shape[0]
    rounds = len(ROUNDS)
    position = lax.axis_index("axial")
    trans = lax.axis_index("trans")
    col = lax.axis_index("col")
    n_trans = lax.axis_size("trans")
    at_inlet = position == 0
    has_lo = trans > 0
    has_hi = trans < n_trans - 1
    lo_dev = (position, jnp.maximum(trans - 1, 0), col)
    hi_dev = (position, jnp.minimum(trans + 1, n_trans - 1), col)
    col_dev = (position, trans, 1 - col)
    lane = lax.broadcasted_iota(jnp.int32, (wide, tall), 1)
    base = 2 + 4 * rounds

    barrier = pltpu.get_barrier_semaphore()

    def greet(cond, device):
        @pl.when(cond)
        def _():
            pl.semaphore_signal(barrier, 1, device_id=device, device_id_type=MESH)

    greet(has_lo, lo_dev)
    greet(has_hi, hi_dev)
    greet(at_inlet, col_dev)
    partners = has_lo.astype(jnp.int32) + has_hi.astype(jnp.int32) + at_inlet.astype(jnp.int32)
    for d in ROUNDS:
        has_right = position + d < count
        has_left = position - d >= 0
        greet(has_right, (jnp.minimum(position + d, count - 1), trans, col))
        greet(has_left, (jnp.maximum(position - d, 0), trans, col))
        partners = partners + has_right.astype(jnp.int32) + has_left.astype(jnp.int32)
    voids = porosity_of(zone_ref[...], por_ref)
    vs_ref[...] = voids

    def run_setup():
        setup(count, voids, ax_ref, cour_ref, cp_ref, ip_ref, l_ref, r_ref, co_ref, sub_ref, sup_ref,
              qf_ref, qb_ref, mf_ref, mb_ref, cprev_ref, hnext_ref, exf_ref, exb_ref)

    pl.semaphore_wait(barrier, partners)

    zero_rows = jnp.zeros((species, wide, tall), jnp.float32)
    for h in range(steps):
        @pl.when(jnp.logical_not(has_lo))
        def _():
            hr_lo[h] = jnp.zeros((wide, tall), jnp.float32)

        @pl.when(jnp.logical_not(has_hi))
        def _():
            hr_hi[h] = jnp.zeros((wide, tall), jnp.float32)

        @pl.when(jnp.logical_not(at_inlet))
        def _():
            face_in[h] = zero_rows

    @pl.when(jnp.logical_not(has_lo))
    def _():
        vr_ref[0] = jnp.zeros((wide, tall), jnp.float32)

    @pl.when(jnp.logical_not(has_hi))
    def _():
        vr_ref[1] = jnp.zeros((wide, tall), jnp.float32)

    voids_up = pltpu.make_async_remote_copy(
        src_ref=vs_ref, dst_ref=vr_ref.at[0], send_sem=vsem_s.at[0], recv_sem=vsem_r.at[0],
        device_id=hi_dev, device_id_type=MESH,
    )
    voids_down = pltpu.make_async_remote_copy(
        src_ref=vs_ref, dst_ref=vr_ref.at[1], send_sem=vsem_s.at[1], recv_sem=vsem_r.at[1],
        device_id=lo_dev, device_id_type=MESH,
    )
    pl.when(has_hi)(voids_up.start)
    pl.when(has_lo)(voids_down.start)

    def exchange_start(h):
        src = v_ref if h == 0 else o_ref
        acc_lo = jnp.zeros((wide, tall), jnp.float32)
        acc_hi = jnp.zeros((wide, tall), jnp.float32)

        def column(s, z, c):
            if h == 0:
                return src[s, z, :, c : c + 1]
            cut = slice(c, c + 1)
            return (y_ref[s, z, :, cut] - ef[s, :, cut] * l_ref[s, z, :, cut]
                    - eb[s, :, cut] * r_ref[s, z, :, cut])

        for s in range(species):
            for z in range(depth):
                at = s * depth + z
                acc_lo = jnp.where(lane == at, jnp.broadcast_to(column(s, z, tall - 1), (wide, tall)), acc_lo)
                acc_hi = jnp.where(lane == at, jnp.broadcast_to(column(s, z, 0), (wide, tall)), acc_hi)
        hs_lo[h] = acc_lo
        hs_hi[h] = acc_hi
        copy_lo = pltpu.make_async_remote_copy(
            src_ref=hs_lo.at[h], dst_ref=hr_lo.at[h], send_sem=send_sem.at[h, 0], recv_sem=recv_sem.at[h, 0],
            device_id=hi_dev, device_id_type=MESH,
        )
        copy_hi = pltpu.make_async_remote_copy(
            src_ref=hs_hi.at[h], dst_ref=hr_hi.at[h], send_sem=send_sem.at[h, 1], recv_sem=recv_sem.at[h, 1],
            device_id=lo_dev, device_id_type=MESH,
        )
        copy_face = pltpu.make_async_remote_copy(
            src_ref=src.at[:, 0], dst_ref=face_in.at[h], send_sem=send_sem.at[h, 2], recv_sem=recv_sem.at[h, 2],
            device_id=col_dev, device_id_type=MESH,
        )
        pl.when(has_hi)(copy_lo.start)
        pl.when(has_lo)(copy_hi.start)
        pl.when(at_inlet)(copy_face.start)
        return copy_lo, copy_hi, copy_face

    def exchange_wait(copy_lo, copy_hi, copy_face):
        pl.when(has_lo)(copy_lo.wait_recv)
        pl.when(has_hi)(copy_hi.wait_recv)
        pl.when(has_hi)(copy_lo.wait_send)
        pl.when(has_lo)(copy_hi.wait_send)

    pending = exchange_start(0)
    run_setup()
    pl.when(has_lo)(voids_up.wait_recv)
    pl.when(has_hi)(voids_down.wait_recv)
    pl.when(has_hi)(voids_up.wait_send)
    pl.when(has_lo)(voids_down.wait_send)
    voids_lo = jnp.where(has_lo, vr_ref[0, :, tall - 1 : tall], 0.0)
    voids_hi = jnp.where(has_hi, vr_ref[1, :, 0:1], 0.0)
    stencil_weights(voids, voids_lo, voids_hi, tr_ref, w_ref)

    for h in range(steps):
        src = v_ref if h == 0 else o_ref
        copy_lo, copy_hi, copy_face = pending
        exchange_wait(copy_lo, copy_hi, copy_face)

        for s in range(species):
            w0 = w_ref[0, s]
            wxm = w_ref[1, s]
            wxp = w_ref[2, s]
            wym = w_ref[3, s]
            wyp = w_ref[4, s]
            sub = sub_ref[s]
            down = None
            for z in range(depth):
                v = src[s, z]
                xm = pltpu.roll(v, 1, 0)
                xp = pltpu.roll(v, wide - 1, 0)
                at = s * depth + z
                ym = jnp.where(lane == 0, hr_lo[h, :, at : at + 1], pltpu.roll(v, 1, 1))
                yp = jnp.where(lane == tall - 1, hr_hi[h, :, at : at + 1], pltpu.roll(v, tall - 1, 1))
                moved = w0 * v + ((wxp * xp + wxm * xm) + (wyp * yp + wym * ym))
                if z == 0:
                    down = moved * ip_ref[s, 0]
                else:
                    down = (moved - sub * down) * ip_ref[s, z]
                y_ref[s, z] = down
            solved = down
            g_ref[1, s] = solved
            for z in range(depth - 2, -1, -1):
                solved = y_ref[s, z] - cp_ref[s, z] * solved
                y_ref[s, z] = solved
            g_ref[0, s] = solved

        pl.when(at_inlet)(copy_face.wait_recv)
        pl.when(at_inlet)(copy_face.wait_send)
        for s in range(species):
            recycled = (plan_ref[h, s].astype(jnp.float32) + 1.0) * 0.25
            inlet = (1.0 - recycled) * feed_ref[s] + recycled * face_in[h, s]
            entry = jnp.where(at_inlet, -sub_ref[s] * inlet, 0.0)
            g_ref[2, s] = entry
            g_ref[0, s] = g_ref[0, s] + entry * l_ref[s, 0]
            g_ref[1, s] = g_ref[1, s] + entry * l_ref[s, depth - 1]
        g0 = g_ref[0]
        g1 = g_ref[1]
        sf[...] = g1 + co_ref[0] * g0
        sb[...] = g0 + co_ref[1] * g1
        ef[...] = zero_rows
        eb[...] = zero_rows
        sent = []
        for r in range(rounds):
            snd_f[h, r] = sf[...]
            snd_b[h, r] = sb[...]
            rank = r
            d = ROUNDS[r]
            has_right = position + d < count
            has_left = position - d >= 0
            right = jnp.minimum(position + d, count - 1)
            left = jnp.maximum(position - d, 0)
            copy_f = pltpu.make_async_remote_copy(
                src_ref=snd_f.at[h, r], dst_ref=rcv_f.at[h, r],
                send_sem=send_sem.at[h, 3 + r], recv_sem=recv_sem.at[h, 3 + r],
                device_id=(right, trans, col), device_id_type=MESH,
            )
            copy_b = pltpu.make_async_remote_copy(
                src_ref=snd_b.at[h, r], dst_ref=rcv_b.at[h, r],
                send_sem=send_sem.at[h, 3 + rounds + r], recv_sem=recv_sem.at[h, 3 + rounds + r],
                device_id=(left, trans, col), device_id_type=MESH,
            )
            pl.when(has_right)(copy_f.start)
            pl.when(has_left)(copy_b.start)
            last_round = r == rounds - 1

            @pl.when(has_left)
            def _():
                copy_f.wait_recv()
                got = rcv_f[h, r]
                ef[...] += co_ref[2 + rank] * got
                if not last_round:
                    sf[...] += co_ref[2 + rounds + rank] * got

            @pl.when(has_right)
            def _():
                copy_b.wait_recv()
                got = rcv_b[h, r]
                eb[...] += co_ref[2 + 2 * rounds + rank] * got
                if not last_round:
                    sb[...] += co_ref[2 + 3 * rounds + rank] * got

            sent.append((has_right, copy_f))
            sent.append((has_left, copy_b))

        before = ef[...]
        after = eb[...]
        r1 = g0 + co_ref[base + 0] * before + co_ref[base + 2] * after
        r2 = g1 + co_ref[base + 1] * before + co_ref[base + 3] * after
        top = r1 * co_ref[base + 6] + r2 * co_ref[base + 7]
        bottom = r1 * co_ref[base + 8] + r2 * co_ref[base + 9]
        ef[...] = sub_ref[...] * (before + co_ref[base + 4] * top)
        eb[...] = sup_ref[...] * (after + co_ref[base + 5] * bottom)
        for cond, copy in sent:
            pl.when(cond)(copy.wait_send)
        for s in range(species):
            ef[s] = ef[s] - g_ref[2, s]
        rows = range(depth)
        if h + 1 < steps:
            for s in range(species):
                o_ref[s, 0] = y_ref[s, 0] - ef[s] * l_ref[s, 0] - eb[s] * r_ref[s, 0]
            pending = exchange_start(h + 1)
            rows = range(1, depth)
        for s in range(species):
            left_coef = ef[s]
            right_coef = eb[s]
            for z in rows:
                o_ref[s, z] = y_ref[s, z] - left_coef * l_ref[s, z] - right_coef * r_ref[s, z]


def body(concentration, zone_map, porosity, axial_number, courant, transverse, feed_conc, plan):
    f32 = jnp.float32
    count = lax.axis_size("axial")
    values = concentration[0]
    species, depth, wide, tall = values.shape
    steps = plan.shape[1]
    zone = zone_map[0]
    assert species * depth <= tall
    rounds = len(ROUNDS)
    n_co = 2 + 4 * rounds + 10
    slab = (wide, tall)
    block = (species, depth) + slab
    smem = pl.BlockSpec(memory_space=pltpu.SMEM)

    n_slot = 3 + 2 * rounds
    out = pl.pallas_call(
        functools.partial(fused_kernel, count),
        out_shape=jax.ShapeDtypeStruct(block, f32),
        in_specs=[_vmem()] * 2 + [smem] * 6,
        out_specs=_vmem(),
        scratch_shapes=[pltpu.VMEM(block, f32)] * 4
        + [pltpu.VMEM((n_co, species) + slab, f32), pltpu.VMEM((5, species) + slab, f32)]
        + [pltpu.VMEM((species,) + slab, f32)] * 2
        + [pltpu.VMEM((count,) + slab, f32)] * 6
        + [pltpu.VMEM((rounds, count) + slab, f32)] * 2
        + [pltpu.VMEM(slab, f32), pltpu.VMEM((2,) + slab, f32)]
        + [pltpu.SemaphoreType.DMA((2,))] * 2
        + [pltpu.VMEM(block, f32)]
        + [pltpu.VMEM((steps,) + slab, f32)] * 4
        + [pltpu.VMEM((steps, species) + slab, f32)]
        + [pltpu.VMEM((3, species) + slab, f32)]
        + [pltpu.VMEM((species,) + slab, f32)] * 4
        + [pltpu.VMEM((steps, rounds, species) + slab, f32)] * 4
        + [pltpu.SemaphoreType.DMA((steps, n_slot))] * 2,
        compiler_params=pltpu.CompilerParams(collective_id=0, has_side_effects=True),
        cost_estimate=pl.CostEstimate(
            flops=100 * steps * species * depth * wide * tall, transcendentals=0,
            bytes_accessed=3 * 4 * species * depth * wide * tall,
        ),
    )(values, zone, porosity, axial_number, courant, transverse, plan[0], feed_conc[0])
    return out[None]


def solution(mesh):
    in_specs = (
        P("col", None, "axial", None, "trans"),
        P("col", None, "trans"),
        P(),
        P(),
        P(),
        P(),
        P("col", None),
        P("col", None, None),
    )
    out_specs = P("col", None, "axial", None, "trans")
    return jax.shard_map(body, mesh=mesh, in_specs=in_specs, out_specs=out_specs, check_vma=False)
```

```python
import functools

import jax
import jax.numpy as jnp
from jax import lax
from jax.experimental import pallas as pl
from jax.experimental.pallas import tpu as pltpu
from jax.sharding import PartitionSpec as P


def swapped(array, axis, distance):
    return lax.ppermute(array, axis, [(i, i ^ 1 << distance) for i in range(lax.axis_size(axis))])


def from_behind(value, axis, steps):
    count = lax.axis_size(axis)
    initial, last = (max(0, -steps), min(count, count - steps))
    return lax.ppermute(value, axis, [(source, source + steps) for source in range(initial, last)])


def void_map(zone_map, porosity):
    voids = jnp.zeros(zone_map.shape, porosity.dtype)
    for number in range(porosity.shape[0]):
        voids = voids + jnp.where(zone_map == number, porosity[number], 0.0)
    return voids


def _vmem():
    return pl.BlockSpec(memory_space=pltpu.VMEM)


ROUNDS = (1, 2, 4, 8)
MESH = pl.DeviceIdType.MESH


def porosity_of(zone, por_ref):
    voids = jnp.zeros(zone.shape, jnp.float32)
    for number in range(por_ref.shape[0]):
        voids = voids + jnp.where(zone == number, por_ref[number], 0.0)
    return voids


def stencil_weights(voids, voids_lo, voids_hi, tr_ref, w_ref):
    wide, tall = voids.shape
    sublane = lax.broadcasted_iota(jnp.int32, (wide, tall), 0)
    lane = lax.broadcasted_iota(jnp.int32, (wide, tall), 1)
    p_xm = jnp.where(sublane == 0, 0.0, pltpu.roll(voids, 1, 0))
    p_xp = jnp.where(sublane == wide - 1, 0.0, pltpu.roll(voids, wide - 1, 0))
    p_ym = jnp.where(lane == 0, jnp.broadcast_to(voids_lo, (wide, tall)), pltpu.roll(voids, 1, 1))
    p_yp = jnp.where(lane == tall - 1, jnp.broadcast_to(voids_hi, (wide, tall)), pltpu.roll(voids, tall - 1, 1))
    faces = [2.0 * p / (voids + p) for p in (p_xm, p_xp, p_ym, p_yp)]
    for s in range(w_ref.shape[1]):
        scaled = [tr_ref[s] * face for face in faces]
        for direction in range(4):
            w_ref[1 + direction, s] = scaled[direction]
        w_ref[0, s] = 1.0 - (scaled[0] + scaled[1] + scaled[2] + scaled[3])


def setup(count, voids, ax_ref, cour_ref, cp_ref, ip_ref, l_ref, r_ref, co_ref, sub_ref, sup_ref,
          qf_ref, qb_ref, mf_ref, mb_ref, cprev_ref, hnext_ref, exf_ref, exb_ref):
    species, depth, wide, tall = cp_ref.shape
    position = lax.axis_index("axial")
    rounds = len(ROUNDS)
    at_outlet = position == count - 1
    for s in range(species):
        dispersion = ax_ref[s] + jnp.zeros((wide, tall), jnp.float32)
        flow_rate = cour_ref[s] / voids
        sub = -(dispersion + flow_rate)
        sup = -dispersion
        mi = 1.0 + 2.0 * dispersion + flow_rate
        me = 1.0 + dispersion + flow_rate
        sub_ref[s] = sub
        sup_ref[s] = sup
        coef = None
        for z in range(depth - 1):
            pivot = mi if z == 0 else mi - sub * coef
            inv = 1.0 / pivot
            coef = sup * inv
            ip_ref[s, z] = inv
            cp_ref[s, z] = coef

        down = ip_ref[s, 0]
        l_ref[s, 0] = down
        for z in range(1, depth - 1):
            down = -sub * down * ip_ref[s, z]
            l_ref[s, z] = down
        alpha = down
        beta = -cp_ref[s, depth - 2]
        for z in range(depth - 3, -1, -1):
            alpha = l_ref[s, z] - cp_ref[s, z] * alpha
            beta = -cp_ref[s, z] * beta

        def ends(last):
            inv_last = 1.0 / (last - sub * cp_ref[s, depth - 2])
            left_last = -sub * down * inv_last
            return alpha + beta * left_last, left_last, beta * inv_last, inv_last

        l0i, l1i, r0i, r1i = ends(mi)
        l0o, l1o, r0o, r1o = ends(me)

        own_last = jnp.where(at_outlet, me, mi)
        inv_last = 1.0 / (own_last - sub * cp_ref[s, depth - 2])
        ip_ref[s, depth - 1] = inv_last
        cp_ref[s, depth - 1] = sup * inv_last
        left = -sub * down * inv_last
        l_ref[s, depth - 1] = left
        right = inv_last
        r_ref[s, depth - 1] = right
        for z in range(depth - 2, -1, -1):
            left = l_ref[s, z] - cp_ref[s, z] * left
            l_ref[s, z] = left
            right = -cp_ref[s, z] * right
            r_ref[s, z] = right

        zero = jnp.zeros_like(sub)
        one = jnp.ones_like(sub)
        inner = (-sub * l0i, -sub * l1i, -sup * r0i, -sup * r1i)
        first = (zero, zero, inner[2], inner[3])
        outlet = (-sub * l0o, -sub * l1o, zero, zero)

        def couplings(j):
            return first if j == 0 else outlet if j == count - 1 else inner

        c_prev = zero
        for j in range(count):
            p0, p1, q0, q1 = couplings(j)
            inv = one if j == 0 else 1.0 / (1.0 - p0 * c_prev)
            qf_ref[j] = p1 * inv
            mf_ref[j] = p1 * c_prev * inv
            cprev_ref[j] = c_prev
            c_prev = q1 + p1 * c_prev * q0 * inv
        h_next = zero
        for j in range(count - 1, -1, -1):
            p0, p1, q0, q1 = couplings(j)
            inv = one if j == count - 1 else 1.0 / (1.0 - q1 * h_next)
            qb_ref[j] = q0 * inv
            mb_ref[j] = q0 * h_next * inv
            hnext_ref[j] = h_next
            h_next = p0 + q0 * h_next * p1 * inv

        for kk in range(count):
            exf_ref[0, kk] = one
            exb_ref[0, kk] = one
        for r in range(rounds - 1):
            d = ROUNDS[r]
            for kk in range(count):
                if kk - d >= 0:
                    exf_ref[r + 1, kk] = exf_ref[r, kk] * qf_ref[kk - d] * exf_ref[r, kk - d]
                else:
                    exf_ref[r + 1, kk] = one
                if kk + d < count:
                    exb_ref[r + 1, kk] = exb_ref[r, kk] * qb_ref[kk + d] * exb_ref[r, kk + d]
                else:
                    exb_ref[r + 1, kk] = one

        co_ref[0, s] = mf_ref[position]
        co_ref[1, s] = mb_ref[position]
        qf_own = qf_ref[position]
        qb_own = qb_ref[position]
        for r in range(rounds):
            wef = exf_ref[r, position]
            web = exb_ref[r, position]
            co_ref[2 + r, s] = wef
            co_ref[2 + rounds + r, s] = qf_own * wef
            co_ref[2 + 2 * rounds + r, s] = web
            co_ref[2 + 3 * rounds + r, s] = qb_own * web
        at_first = position == 0
        at_last = position == count - 1
        p0 = jnp.where(at_first, zero, jnp.where(at_last, outlet[0], inner[0]))
        p1 = jnp.where(at_first, zero, jnp.where(at_last, outlet[1], inner[1]))
        q0 = jnp.where(at_last, zero, inner[2])
        q1 = jnp.where(at_last, zero, inner[3])
        c_own = cprev_ref[position]
        h_own = hnext_ref[position]
        a11 = 1.0 - p0 * c_own
        a12 = -q0 * h_own
        a21 = -p1 * c_own
        a22 = 1.0 - q1 * h_own
        inv_det = 1.0 / (a11 * a22 - a12 * a21)
        base = 2 + 4 * rounds
        for i, value in enumerate(
            (p0, p1, q0, q1, c_own, h_own, a22 * inv_det, -a12 * inv_det, -a21 * inv_det, a11 * inv_det)
        ):
            co_ref[base + i, s] = value


def fused_kernel(count, v_ref, zone_ref, por_ref, ax_ref, cour_ref, tr_ref, plan_ref, feed_ref,
                 o_ref,
                 cp_ref, ip_ref, l_ref, r_ref, co_ref, w_ref, sub_ref, sup_ref,
                 qf_ref, qb_ref, mf_ref, mb_ref, cprev_ref, hnext_ref, exf_ref, exb_ref,
                 vs_ref, vr_ref, vsem_s, vsem_r,
                 y_ref, hs_lo, hs_hi, hr_lo, hr_hi, face_in, g_ref, sf, sb, ef, eb,
                 snd_f, snd_b, rcv_f, rcv_b, send_sem, recv_sem):
    species, depth, wide, tall = v_ref.shape
    steps = plan_ref.shape[0]
    rounds = len(ROUNDS)
    position = lax.axis_index("axial")
    trans = lax.axis_index("trans")
    col = lax.axis_index("col")
    n_trans = lax.axis_size("trans")
    at_inlet = position == 0
    has_lo = trans > 0
    has_hi = trans < n_trans - 1
    lo_dev = (position, jnp.maximum(trans - 1, 0), col)
    hi_dev = (position, jnp.minimum(trans + 1, n_trans - 1), col)
    col_dev = (position, trans, 1 - col)
    lane = lax.broadcasted_iota(jnp.int32, (wide, tall), 1)
    base = 2 + 4 * rounds

    barrier = pltpu.get_barrier_semaphore()

    def greet(cond, device):
        @pl.when(cond)
        def _():
            pl.semaphore_signal(barrier, 1, device_id=device, device_id_type=MESH)

    greet(has_lo, lo_dev)
    greet(has_hi, hi_dev)
    greet(at_inlet, col_dev)
    partners = has_lo.astype(jnp.int32) + has_hi.astype(jnp.int32) + at_inlet.astype(jnp.int32)
    for d in ROUNDS:
        has_right = position + d < count
        has_left = position - d >= 0
        greet(has_right, (jnp.minimum(position + d, count - 1), trans, col))
        greet(has_left, (jnp.maximum(position - d, 0), trans, col))
        partners = partners + has_right.astype(jnp.int32) + has_left.astype(jnp.int32)
    voids = porosity_of(zone_ref[...], por_ref)
    vs_ref[...] = voids

    def run_setup():
        setup(count, voids, ax_ref, cour_ref, cp_ref, ip_ref, l_ref, r_ref, co_ref, sub_ref, sup_ref,
              qf_ref, qb_ref, mf_ref, mb_ref, cprev_ref, hnext_ref, exf_ref, exb_ref)

    pl.semaphore_wait(barrier, partners)

    zero_rows = jnp.zeros((species, wide, tall), jnp.float32)
    for h in range(steps):
        @pl.when(jnp.logical_not(has_lo))
        def _():
            hr_lo[h] = jnp.zeros((wide, tall), jnp.float32)

        @pl.when(jnp.logical_not(has_hi))
        def _():
            hr_hi[h] = jnp.zeros((wide, tall), jnp.float32)

        @pl.when(jnp.logical_not(at_inlet))
        def _():
            face_in[h] = zero_rows

    @pl.when(jnp.logical_not(has_lo))
    def _():
        vr_ref[0] = jnp.zeros((wide, tall), jnp.float32)

    @pl.when(jnp.logical_not(has_hi))
    def _():
        vr_ref[1] = jnp.zeros((wide, tall), jnp.float32)

    voids_up = pltpu.make_async_remote_copy(
        src_ref=vs_ref, dst_ref=vr_ref.at[0], send_sem=vsem_s.at[0], recv_sem=vsem_r.at[0],
        device_id=hi_dev, device_id_type=MESH,
    )
    voids_down = pltpu.make_async_remote_copy(
        src_ref=vs_ref, dst_ref=vr_ref.at[1], send_sem=vsem_s.at[1], recv_sem=vsem_r.at[1],
        device_id=lo_dev, device_id_type=MESH,
    )
    pl.when(has_hi)(voids_up.start)
    pl.when(has_lo)(voids_down.start)

    def exchange_start(h):
        src = v_ref if h == 0 else o_ref
        acc_lo = jnp.zeros((wide, tall), jnp.float32)
        acc_hi = jnp.zeros((wide, tall), jnp.float32)

        def column(s, z, c):
            if h == 0:
                return src[s, z, :, c : c + 1]
            cut = slice(c, c + 1)
            return (y_ref[s, z, :, cut] - ef[s, :, cut] * l_ref[s, z, :, cut]
                    - eb[s, :, cut] * r_ref[s, z, :, cut])

        for s in range(species):
            for z in range(depth):
                at = s * depth + z
                acc_lo = jnp.where(lane == at, jnp.broadcast_to(column(s, z, tall - 1), (wide, tall)), acc_lo)
                acc_hi = jnp.where(lane == at, jnp.broadcast_to(column(s, z, 0), (wide, tall)), acc_hi)
        hs_lo[h] = acc_lo
        hs_hi[h] = acc_hi
        copy_lo = pltpu.make_async_remote_copy(
            src_ref=hs_lo.at[h], dst_ref=hr_lo.at[h], send_sem=send_sem.at[h, 0], recv_sem=recv_sem.at[h, 0],
            device_id=hi_dev, device_id_type=MESH,
        )
        copy_hi = pltpu.make_async_remote_copy(
            src_ref=hs_hi.at[h], dst_ref=hr_hi.at[h], send_sem=send_sem.at[h, 1], recv_sem=recv_sem.at[h, 1],
            device_id=lo_dev, device_id_type=MESH,
        )
        copy_face = pltpu.make_async_remote_copy(
            src_ref=src.at[:, 0], dst_ref=face_in.at[h], send_sem=send_sem.at[h, 2], recv_sem=recv_sem.at[h, 2],
            device_id=col_dev, device_id_type=MESH,
        )
        pl.when(has_hi)(copy_lo.start)
        pl.when(has_lo)(copy_hi.start)
        pl.when(at_inlet)(copy_face.start)
        return copy_lo, copy_hi, copy_face

    def exchange_wait(copy_lo, copy_hi, copy_face):
        pl.when(has_lo)(copy_lo.wait_recv)
        pl.when(has_hi)(copy_hi.wait_recv)
        pl.when(has_hi)(copy_lo.wait_send)
        pl.when(has_lo)(copy_hi.wait_send)

    pending = exchange_start(0)
    run_setup()
    pl.when(has_lo)(voids_up.wait_recv)
    pl.when(has_hi)(voids_down.wait_recv)
    pl.when(has_hi)(voids_up.wait_send)
    pl.when(has_lo)(voids_down.wait_send)
    voids_lo = jnp.where(has_lo, vr_ref[0, :, tall - 1 : tall], 0.0)
    voids_hi = jnp.where(has_hi, vr_ref[1, :, 0:1], 0.0)
    stencil_weights(voids, voids_lo, voids_hi, tr_ref, w_ref)

    for h in range(steps):
        src = v_ref if h == 0 else o_ref
        copy_lo, copy_hi, copy_face = pending
        exchange_wait(copy_lo, copy_hi, copy_face)

        for s in range(species):
            w0 = w_ref[0, s]
            wxm = w_ref[1, s]
            wxp = w_ref[2, s]
            wym = w_ref[3, s]
            wyp = w_ref[4, s]
            sub = sub_ref[s]
            down = None
            for z in range(depth):
                v = src[s, z]
                xm = pltpu.roll(v, 1, 0)
                xp = pltpu.roll(v, wide - 1, 0)
                at = s * depth + z
                ym = jnp.where(lane == 0, hr_lo[h, :, at : at + 1], pltpu.roll(v, 1, 1))
                yp = jnp.where(lane == tall - 1, hr_hi[h, :, at : at + 1], pltpu.roll(v, tall - 1, 1))
                moved = w0 * v + ((wxp * xp + wxm * xm) + (wyp * yp + wym * ym))
                if z == 0:
                    down = moved * ip_ref[s, 0]
                else:
                    down = (moved - sub * down) * ip_ref[s, z]
                y_ref[s, z] = down
            solved = down
            g_ref[1, s] = solved
            for z in range(depth - 2, -1, -1):
                solved = y_ref[s, z] - cp_ref[s, z] * solved
                y_ref[s, z] = solved
            g_ref[0, s] = solved

        pl.when(at_inlet)(copy_face.wait_recv)
        pl.when(at_inlet)(copy_face.wait_send)
        for s in range(species):
            recycled = (plan_ref[h, s].astype(jnp.float32) + 1.0) * 0.25
            inlet = (1.0 - recycled) * feed_ref[s] + recycled * face_in[h, s]
            entry = jnp.where(at_inlet, -sub_ref[s] * inlet, 0.0)
            g_ref[2, s] = entry
            g_ref[0, s] = g_ref[0, s] + entry * l_ref[s, 0]
            g_ref[1, s] = g_ref[1, s] + entry * l_ref[s, depth - 1]
        g0 = g_ref[0]
        g1 = g_ref[1]
        sf[...] = g1 + co_ref[0] * g0
        sb[...] = g0 + co_ref[1] * g1
        ef[...] = zero_rows
        eb[...] = zero_rows
        sent = []
        for r in range(rounds):
            snd_f[h, r] = sf[...]
            snd_b[h, r] = sb[...]
            rank = r
            d = ROUNDS[r]
            has_right = position + d < count
            has_left = position - d >= 0
            right = jnp.minimum(position + d, count - 1)
            left = jnp.maximum(position - d, 0)
            copy_f = pltpu.make_async_remote_copy(
                src_ref=snd_f.at[h, r], dst_ref=rcv_f.at[h, r],
                send_sem=send_sem.at[h, 3 + r], recv_sem=recv_sem.at[h, 3 + r],
                device_id=(right, trans, col), device_id_type=MESH,
            )
            copy_b = pltpu.make_async_remote_copy(
                src_ref=snd_b.at[h, r], dst_ref=rcv_b.at[h, r],
                send_sem=send_sem.at[h, 3 + rounds + r], recv_sem=recv_sem.at[h, 3 + rounds + r],
                device_id=(left, trans, col), device_id_type=MESH,
            )
            pl.when(has_right)(copy_f.start)
            pl.when(has_left)(copy_b.start)
            last_round = r == rounds - 1

            @pl.when(has_left)
            def _():
                copy_f.wait_recv()
                got = rcv_f[h, r]
                ef[...] += co_ref[2 + rank] * got
                if not last_round:
                    sf[...] += co_ref[2 + rounds + rank] * got

            @pl.when(has_right)
            def _():
                copy_b.wait_recv()
                got = rcv_b[h, r]
                eb[...] += co_ref[2 + 2 * rounds + rank] * got
                if not last_round:
                    sb[...] += co_ref[2 + 3 * rounds + rank] * got

            sent.append((has_right, copy_f))
            sent.append((has_left, copy_b))

        before = ef[...]
        after = eb[...]
        r1 = g0 + co_ref[base + 0] * before + co_ref[base + 2] * after
        r2 = g1 + co_ref[base + 1] * before + co_ref[base + 3] * after
        top = r1 * co_ref[base + 6] + r2 * co_ref[base + 7]
        bottom = r1 * co_ref[base + 8] + r2 * co_ref[base + 9]
        ef[...] = sub_ref[...] * (before + co_ref[base + 4] * top)
        eb[...] = sup_ref[...] * (after + co_ref[base + 5] * bottom)
        for cond, copy in sent:
            pl.when(cond)(copy.wait_send)
        for s in range(species):
            ef[s] = ef[s] - g_ref[2, s]
        rows = range(depth)
        if h + 1 < steps:
            for s in range(species):
                o_ref[s, 0] = y_ref[s, 0] - ef[s] * l_ref[s, 0] - eb[s] * r_ref[s, 0]
            pending = exchange_start(h + 1)
            rows = range(1, depth)
        for s in range(species):
            left_coef = ef[s]
            right_coef = eb[s]
            for z in rows:
                o_ref[s, z] = y_ref[s, z] - left_coef * l_ref[s, z] - right_coef * r_ref[s, z]


def body(concentration, zone_map, porosity, axial_number, courant, transverse, feed_conc, plan):
    f32 = jnp.float32
    count = lax.axis_size("axial")
    values = concentration[0]
    species, depth, wide, tall = values.shape
    steps = plan.shape[1]
    zone = zone_map[0]
    assert species * depth <= tall
    rounds = len(ROUNDS)
    n_co = 2 + 4 * rounds + 10
    slab = (wide, tall)
    block = (species, depth) + slab
    smem = pl.BlockSpec(memory_space=pltpu.SMEM)

    n_slot = 3 + 2 * rounds
    out = pl.pallas_call(
        functools.partial(fused_kernel, count),
        out_shape=jax.ShapeDtypeStruct(block, f32),
        in_specs=[_vmem()] * 2 + [smem] * 6,
        out_specs=_vmem(),
        scratch_shapes=[pltpu.VMEM(block, f32)] * 4
        + [pltpu.VMEM((n_co, species) + slab, f32), pltpu.VMEM((5, species) + slab, f32)]
        + [pltpu.VMEM((species,) + slab, f32)] * 2
        + [pltpu.VMEM((count,) + slab, f32)] * 6
        + [pltpu.VMEM((rounds, count) + slab, f32)] * 2
        + [pltpu.VMEM(slab, f32), pltpu.VMEM((2,) + slab, f32)]
        + [pltpu.SemaphoreType.DMA((2,))] * 2
        + [pltpu.VMEM(block, f32)]
        + [pltpu.VMEM((steps,) + slab, f32)] * 4
        + [pltpu.VMEM((steps, species) + slab, f32)]
        + [pltpu.VMEM((3, species) + slab, f32)]
        + [pltpu.VMEM((species,) + slab, f32)] * 4
        + [pltpu.VMEM((steps, rounds, species) + slab, f32)] * 4
        + [pltpu.SemaphoreType.DMA((steps, n_slot))] * 2,
        compiler_params=pltpu.CompilerParams(collective_id=0, has_side_effects=True),
        cost_estimate=pl.CostEstimate(
            flops=100 * steps * species * depth * wide * tall, transcendentals=0,
            bytes_accessed=3 * 4 * species * depth * wide * tall,
        ),
    )(values, zone, porosity, axial_number, courant, transverse, plan[0], feed_conc[0])
    return out[None]


def solution(mesh):
    in_specs = (
        P("col", None, "axial", None, "trans"),
        P("col", None, "trans"),
        P(),
        P(),
        P(),
        P(),
        P("col", None),
        P("col", None, None),
    )
    out_specs = P("col", None, "axial", None, "trans")
    return jax.shard_map(body, mesh=mesh, in_specs=in_specs, out_specs=out_specs, check_vma=False)
```

```python
import functools

import jax
import jax.numpy as jnp
from jax import lax
from jax.experimental import pallas as pl
from jax.experimental.pallas import tpu as pltpu
from jax.sharding import PartitionSpec as P


def swapped(array, axis, distance):
    return lax.ppermute(array, axis, [(i, i ^ 1 << distance) for i in range(lax.axis_size(axis))])


def from_behind(value, axis, steps):
    count = lax.axis_size(axis)
    initial, last = (max(0, -steps), min(count, count - steps))
    return lax.ppermute(value, axis, [(source, source + steps) for source in range(initial, last)])


def void_map(zone_map, porosity):
    voids = jnp.zeros(zone_map.shape, porosity.dtype)
    for number in range(porosity.shape[0]):
        voids = voids + jnp.where(zone_map == number, porosity[number], 0.0)
    return voids


def _vmem():
    return pl.BlockSpec(memory_space=pltpu.VMEM)


ROUNDS = (1, 2, 4, 8)
MESH = pl.DeviceIdType.MESH


def porosity_of(zone, por_ref):
    voids = jnp.zeros(zone.shape, jnp.float32)
    for number in range(por_ref.shape[0]):
        voids = voids + jnp.where(zone == number, por_ref[number], 0.0)
    return voids


def stencil_weights(voids, voids_lo, voids_hi, tr_ref, w_ref):
    wide, tall = voids.shape
    sublane = lax.broadcasted_iota(jnp.int32, (wide, tall), 0)
    lane = lax.broadcasted_iota(jnp.int32, (wide, tall), 1)
    p_xm = jnp.where(sublane == 0, 0.0, pltpu.roll(voids, 1, 0))
    p_xp = jnp.where(sublane == wide - 1, 0.0, pltpu.roll(voids, wide - 1, 0))
    p_ym = jnp.where(lane == 0, jnp.broadcast_to(voids_lo, (wide, tall)), pltpu.roll(voids, 1, 1))
    p_yp = jnp.where(lane == tall - 1, jnp.broadcast_to(voids_hi, (wide, tall)), pltpu.roll(voids, tall - 1, 1))
    faces = [2.0 * p / (voids + p) for p in (p_xm, p_xp, p_ym, p_yp)]
    for s in range(w_ref.shape[1]):
        scaled = [tr_ref[s] * face for face in faces]
        for direction in range(4):
            w_ref[1 + direction, s] = scaled[direction]
        w_ref[0, s] = 1.0 - (scaled[0] + scaled[1] + scaled[2] + scaled[3])


def setup(count, voids, ax_ref, cour_ref, cp_ref, ip_ref, l_ref, r_ref, co_ref, sub_ref, sup_ref,
          qf_ref, qb_ref, mf_ref, mb_ref, cprev_ref, hnext_ref, exf_ref, exb_ref):
    species, depth, wide, tall = cp_ref.shape
    position = lax.axis_index("axial")
    rounds = len(ROUNDS)
    at_outlet = position == count - 1
    for s in range(species):
        dispersion = ax_ref[s] + jnp.zeros((wide, tall), jnp.float32)
        flow_rate = cour_ref[s] / voids
        sub = -(dispersion + flow_rate)
        sup = -dispersion
        mi = 1.0 + 2.0 * dispersion + flow_rate
        me = 1.0 + dispersion + flow_rate
        sub_ref[s] = sub
        sup_ref[s] = sup
        coef = None
        for z in range(depth - 1):
            pivot = mi if z == 0 else mi - sub * coef
            inv = 1.0 / pivot
            coef = sup * inv
            ip_ref[s, z] = inv
            cp_ref[s, z] = coef

        down = ip_ref[s, 0]
        l_ref[s, 0] = down
        for z in range(1, depth - 1):
            down = -sub * down * ip_ref[s, z]
            l_ref[s, z] = down
        alpha = down
        beta = -cp_ref[s, depth - 2]
        for z in range(depth - 3, -1, -1):
            alpha = l_ref[s, z] - cp_ref[s, z] * alpha
            beta = -cp_ref[s, z] * beta

        def ends(last):
            inv_last = 1.0 / (last - sub * cp_ref[s, depth - 2])
            left_last = -sub * down * inv_last
            return alpha + beta * left_last, left_last, beta * inv_last, inv_last

        l0i, l1i, r0i, r1i = ends(mi)
        l0o, l1o, r0o, r1o = ends(me)

        own_last = jnp.where(at_outlet, me, mi)
        inv_last = 1.0 / (own_last - sub * cp_ref[s, depth - 2])
        ip_ref[s, depth - 1] = inv_last
        cp_ref[s, depth - 1] = sup * inv_last
        left = -sub * down * inv_last
        l_ref[s, depth - 1] = left
        l_ref[s, 0] = alpha + beta * left

        zero = jnp.zeros_like(sub)
        one = jnp.ones_like(sub)
        inner = (-sub * l0i, -sub * l1i, -sup * r0i, -sup * r1i)
        first = (zero, zero, inner[2], inner[3])
        outlet = (-sub * l0o, -sub * l1o, zero, zero)

        def couplings(j):
            return first if j == 0 else outlet if j == count - 1 else inner

        c_prev = zero
        for j in range(count):
            p0, p1, q0, q1 = couplings(j)
            inv = one if j == 0 else 1.0 / (1.0 - p0 * c_prev)
            qf_ref[j] = p1 * inv
            mf_ref[j] = p1 * c_prev * inv
            cprev_ref[j] = c_prev
            c_prev = q1 + p1 * c_prev * q0 * inv
        h_next = zero
        for j in range(count - 1, -1, -1):
            p0, p1, q0, q1 = couplings(j)
            inv = one if j == count - 1 else 1.0 / (1.0 - q1 * h_next)
            qb_ref[j] = q0 * inv
            mb_ref[j] = q0 * h_next * inv
            hnext_ref[j] = h_next
            h_next = p0 + q0 * h_next * p1 * inv

        for kk in range(count):
            exf_ref[0, kk] = one
            exb_ref[0, kk] = one
        for r in range(rounds - 1):
            d = ROUNDS[r]
            for kk in range(count):
                if kk - d >= 0:
                    exf_ref[r + 1, kk] = exf_ref[r, kk] * qf_ref[kk - d] * exf_ref[r, kk - d]
                else:
                    exf_ref[r + 1, kk] = one
                if kk + d < count:
                    exb_ref[r + 1, kk] = exb_ref[r, kk] * qb_ref[kk + d] * exb_ref[r, kk + d]
                else:
                    exb_ref[r + 1, kk] = one

        co_ref[0, s] = mf_ref[position]
        co_ref[1, s] = mb_ref[position]
        qf_own = qf_ref[position]
        qb_own = qb_ref[position]
        for r in range(rounds):
            wef = exf_ref[r, position]
            web = exb_ref[r, position]
            co_ref[2 + r, s] = wef
            co_ref[2 + rounds + r, s] = qf_own * wef
            co_ref[2 + 2 * rounds + r, s] = web
            co_ref[2 + 3 * rounds + r, s] = qb_own * web
        at_first = position == 0
        at_last = position == count - 1
        p0 = jnp.where(at_first, zero, jnp.where(at_last, outlet[0], inner[0]))
        p1 = jnp.where(at_first, zero, jnp.where(at_last, outlet[1], inner[1]))
        q0 = jnp.where(at_last, zero, inner[2])
        q1 = jnp.where(at_last, zero, inner[3])
        c_own = cprev_ref[position]
        h_own = hnext_ref[position]
        a11 = 1.0 - p0 * c_own
        a12 = -q0 * h_own
        a21 = -p1 * c_own
        a22 = 1.0 - q1 * h_own
        inv_det = 1.0 / (a11 * a22 - a12 * a21)
        base = 2 + 4 * rounds
        for i, value in enumerate(
            (p0, p1, q0, q1, c_own, h_own, a22 * inv_det, -a12 * inv_det, -a21 * inv_det, a11 * inv_det)
        ):
            co_ref[base + i, s] = value


def spike_rows(cp_ref, ip_ref, l_ref, r_ref):
    species, depth = cp_ref.shape[0], cp_ref.shape[1]
    for s in range(species):
        left = l_ref[s, depth - 1]
        right = ip_ref[s, depth - 1]
        r_ref[s, depth - 1] = right
        for z in range(depth - 2, 0, -1):
            left = l_ref[s, z] - cp_ref[s, z] * left
            l_ref[s, z] = left
            right = -cp_ref[s, z] * right
            r_ref[s, z] = right
        r_ref[s, 0] = -cp_ref[s, 0] * right


def fused_kernel(count, v_ref, zone_ref, por_ref, ax_ref, cour_ref, tr_ref, plan_ref, feed_ref,
                 o_ref,
                 cp_ref, ip_ref, l_ref, r_ref, co_ref, w_ref, sub_ref, sup_ref,
                 qf_ref, qb_ref, mf_ref, mb_ref, cprev_ref, hnext_ref, exf_ref, exb_ref,
                 vs_ref, vr_ref, vsem_s, vsem_r,
                 y_ref, hs_lo, hs_hi, hr_lo, hr_hi, face_in, g_ref, sf, sb, ef, eb,
                 snd_f, snd_b, rcv_f, rcv_b, send_sem, recv_sem):
    species, depth, wide, tall = v_ref.shape
    steps = plan_ref.shape[0]
    rounds = len(ROUNDS)
    position = lax.axis_index("axial")
    trans = lax.axis_index("trans")
    col = lax.axis_index("col")
    n_trans = lax.axis_size("trans")
    at_inlet = position == 0
    has_lo = trans > 0
    has_hi = trans < n_trans - 1
    lo_dev = (position, jnp.maximum(trans - 1, 0), col)
    hi_dev = (position, jnp.minimum(trans + 1, n_trans - 1), col)
    col_dev = (position, trans, 1 - col)
    lane = lax.broadcasted_iota(jnp.int32, (wide, tall), 1)
    base = 2 + 4 * rounds

    barrier = pltpu.get_barrier_semaphore()

    def greet(cond, device):
        @pl.when(cond)
        def _():
            pl.semaphore_signal(barrier, 1, device_id=device, device_id_type=MESH)

    greet(has_lo, lo_dev)
    greet(has_hi, hi_dev)
    greet(at_inlet, col_dev)
    partners = has_lo.astype(jnp.int32) + has_hi.astype(jnp.int32) + at_inlet.astype(jnp.int32)
    for d in ROUNDS:
        has_right = position + d < count
        has_left = position - d >= 0
        greet(has_right, (jnp.minimum(position + d, count - 1), trans, col))
        greet(has_left, (jnp.maximum(position - d, 0), trans, col))
        partners = partners + has_right.astype(jnp.int32) + has_left.astype(jnp.int32)
    voids = porosity_of(zone_ref[...], por_ref)
    vs_ref[...] = voids

    def run_setup():
        setup(count, voids, ax_ref, cour_ref, cp_ref, ip_ref, l_ref, r_ref, co_ref, sub_ref, sup_ref,
              qf_ref, qb_ref, mf_ref, mb_ref, cprev_ref, hnext_ref, exf_ref, exb_ref)

    pl.semaphore_wait(barrier, partners)

    zero_rows = jnp.zeros((species, wide, tall), jnp.float32)
    for h in range(steps):
        @pl.when(jnp.logical_not(has_lo))
        def _():
            hr_lo[h] = jnp.zeros((wide, tall), jnp.float32)

        @pl.when(jnp.logical_not(has_hi))
        def _():
            hr_hi[h] = jnp.zeros((wide, tall), jnp.float32)

        @pl.when(jnp.logical_not(at_inlet))
        def _():
            face_in[h] = zero_rows

    @pl.when(jnp.logical_not(has_lo))
    def _():
        vr_ref[0] = jnp.zeros((wide, tall), jnp.float32)

    @pl.when(jnp.logical_not(has_hi))
    def _():
        vr_ref[1] = jnp.zeros((wide, tall), jnp.float32)

    voids_up = pltpu.make_async_remote_copy(
        src_ref=vs_ref, dst_ref=vr_ref.at[0], send_sem=vsem_s.at[0], recv_sem=vsem_r.at[0],
        device_id=hi_dev, device_id_type=MESH,
    )
    voids_down = pltpu.make_async_remote_copy(
        src_ref=vs_ref, dst_ref=vr_ref.at[1], send_sem=vsem_s.at[1], recv_sem=vsem_r.at[1],
        device_id=lo_dev, device_id_type=MESH,
    )
    pl.when(has_hi)(voids_up.start)
    pl.when(has_lo)(voids_down.start)

    def exchange_start(h):
        src = v_ref if h == 0 else o_ref
        acc_lo = jnp.zeros((wide, tall), jnp.float32)
        acc_hi = jnp.zeros((wide, tall), jnp.float32)

        def column(s, z, c):
            if h == 0:
                return src[s, z, :, c : c + 1]
            cut = slice(c, c + 1)
            return (y_ref[s, z, :, cut] - ef[s, :, cut] * l_ref[s, z, :, cut]
                    - eb[s, :, cut] * r_ref[s, z, :, cut])

        for s in range(species):
            for z in range(depth):
                at = s * depth + z
                acc_lo = jnp.where(lane == at, jnp.broadcast_to(column(s, z, tall - 1), (wide, tall)), acc_lo)
                acc_hi = jnp.where(lane == at, jnp.broadcast_to(column(s, z, 0), (wide, tall)), acc_hi)
        hs_lo[h] = acc_lo
        hs_hi[h] = acc_hi
        copy_lo = pltpu.make_async_remote_copy(
            src_ref=hs_lo.at[h], dst_ref=hr_lo.at[h], send_sem=send_sem.at[h, 0], recv_sem=recv_sem.at[h, 0],
            device_id=hi_dev, device_id_type=MESH,
        )
        copy_hi = pltpu.make_async_remote_copy(
            src_ref=hs_hi.at[h], dst_ref=hr_hi.at[h], send_sem=send_sem.at[h, 1], recv_sem=recv_sem.at[h, 1],
            device_id=lo_dev, device_id_type=MESH,
        )
        copy_face = pltpu.make_async_remote_copy(
            src_ref=src.at[:, 0], dst_ref=face_in.at[h], send_sem=send_sem.at[h, 2], recv_sem=recv_sem.at[h, 2],
            device_id=col_dev, device_id_type=MESH,
        )
        pl.when(has_hi)(copy_lo.start)
        pl.when(has_lo)(copy_hi.start)
        pl.when(at_inlet)(copy_face.start)
        return copy_lo, copy_hi, copy_face

    def exchange_wait(copy_lo, copy_hi, copy_face):
        pl.when(has_lo)(copy_lo.wait_recv)
        pl.when(has_hi)(copy_hi.wait_recv)
        pl.when(has_hi)(copy_lo.wait_send)
        pl.when(has_lo)(copy_hi.wait_send)

    pending = exchange_start(0)
    run_setup()
    pl.when(has_lo)(voids_up.wait_recv)
    pl.when(has_hi)(voids_down.wait_recv)
    pl.when(has_hi)(voids_up.wait_send)
    pl.when(has_lo)(voids_down.wait_send)
    voids_lo = jnp.where(has_lo, vr_ref[0, :, tall - 1 : tall], 0.0)
    voids_hi = jnp.where(has_hi, vr_ref[1, :, 0:1], 0.0)
    stencil_weights(voids, voids_lo, voids_hi, tr_ref, w_ref)

    for h in range(steps):
        src = v_ref if h == 0 else o_ref
        copy_lo, copy_hi, copy_face = pending
        exchange_wait(copy_lo, copy_hi, copy_face)

        for s in range(species):
            w0 = w_ref[0, s]
            wxm = w_ref[1, s]
            wxp = w_ref[2, s]
            wym = w_ref[3, s]
            wyp = w_ref[4, s]
            sub = sub_ref[s]
            down = None
            for z in range(depth):
                v = src[s, z]
                xm = pltpu.roll(v, 1, 0)
                xp = pltpu.roll(v, wide - 1, 0)
                at = s * depth + z
                ym = jnp.where(lane == 0, hr_lo[h, :, at : at + 1], pltpu.roll(v, 1, 1))
                yp = jnp.where(lane == tall - 1, hr_hi[h, :, at : at + 1], pltpu.roll(v, tall - 1, 1))
                moved = w0 * v + ((wxp * xp + wxm * xm) + (wyp * yp + wym * ym))
                if z == 0:
                    down = moved * ip_ref[s, 0]
                else:
                    down = (moved - sub * down) * ip_ref[s, z]
                y_ref[s, z] = down
            solved = down
            g_ref[1, s] = solved
            for z in range(depth - 2, -1, -1):
                solved = y_ref[s, z] - cp_ref[s, z] * solved
                y_ref[s, z] = solved
            g_ref[0, s] = solved

        pl.when(at_inlet)(copy_face.wait_recv)
        pl.when(at_inlet)(copy_face.wait_send)
        for s in range(species):
            recycled = (plan_ref[h, s].astype(jnp.float32) + 1.0) * 0.25
            inlet = (1.0 - recycled) * feed_ref[s] + recycled * face_in[h, s]
            entry = jnp.where(at_inlet, -sub_ref[s] * inlet, 0.0)
            g_ref[2, s] = entry
            g_ref[0, s] = g_ref[0, s] + entry * l_ref[s, 0]
            g_ref[1, s] = g_ref[1, s] + entry * l_ref[s, depth - 1]
        g0 = g_ref[0]
        g1 = g_ref[1]
        sf[...] = g1 + co_ref[0] * g0
        sb[...] = g0 + co_ref[1] * g1
        ef[...] = zero_rows
        eb[...] = zero_rows
        sent = []
        for r in range(rounds):
            snd_f[h, r] = sf[...]
            snd_b[h, r] = sb[...]
            rank = r
            d = ROUNDS[r]
            has_right = position + d < count
            has_left = position - d >= 0
            right = jnp.minimum(position + d, count - 1)
            left = jnp.maximum(position - d, 0)
            copy_f = pltpu.make_async_remote_copy(
                src_ref=snd_f.at[h, r], dst_ref=rcv_f.at[h, r],
                send_sem=send_sem.at[h, 3 + r], recv_sem=recv_sem.at[h, 3 + r],
                device_id=(right, trans, col), device_id_type=MESH,
            )
            copy_b = pltpu.make_async_remote_copy(
                src_ref=snd_b.at[h, r], dst_ref=rcv_b.at[h, r],
                send_sem=send_sem.at[h, 3 + rounds + r], recv_sem=recv_sem.at[h, 3 + rounds + r],
                device_id=(left, trans, col), device_id_type=MESH,
            )
            pl.when(has_right)(copy_f.start)
            pl.when(has_left)(copy_b.start)
            last_round = r == rounds - 1
            if h == 0 and r == 0:
                spike_rows(cp_ref, ip_ref, l_ref, r_ref)

            @pl.when(has_left)
            def _():
                copy_f.wait_recv()
                got = rcv_f[h, r]
                ef[...] += co_ref[2 + rank] * got
                if not last_round:
                    sf[...] += co_ref[2 + rounds + rank] * got

            @pl.when(has_right)
            def _():
                copy_b.wait_recv()
                got = rcv_b[h, r]
                eb[...] += co_ref[2 + 2 * rounds + rank] * got
                if not last_round:
                    sb[...] += co_ref[2 + 3 * rounds + rank] * got

            sent.append((has_right, copy_f))
            sent.append((has_left, copy_b))

        before = ef[...]
        after = eb[...]
        r1 = g0 + co_ref[base + 0] * before + co_ref[base + 2] * after
        r2 = g1 + co_ref[base + 1] * before + co_ref[base + 3] * after
        top = r1 * co_ref[base + 6] + r2 * co_ref[base + 7]
        bottom = r1 * co_ref[base + 8] + r2 * co_ref[base + 9]
        ef[...] = sub_ref[...] * (before + co_ref[base + 4] * top)
        eb[...] = sup_ref[...] * (after + co_ref[base + 5] * bottom)
        for cond, copy in sent:
            pl.when(cond)(copy.wait_send)
        for s in range(species):
            ef[s] = ef[s] - g_ref[2, s]
        rows = range(depth)
        if h + 1 < steps:
            for s in range(species):
                o_ref[s, 0] = y_ref[s, 0] - ef[s] * l_ref[s, 0] - eb[s] * r_ref[s, 0]
            pending = exchange_start(h + 1)
            rows = range(1, depth)
        for s in range(species):
            left_coef = ef[s]
            right_coef = eb[s]
            for z in rows:
                o_ref[s, z] = y_ref[s, z] - left_coef * l_ref[s, z] - right_coef * r_ref[s, z]


def body(concentration, zone_map, porosity, axial_number, courant, transverse, feed_conc, plan):
    f32 = jnp.float32
    count = lax.axis_size("axial")
    values = concentration[0]
    species, depth, wide, tall = values.shape
    steps = plan.shape[1]
    zone = zone_map[0]
    assert species * depth <= tall
    rounds = len(ROUNDS)
    n_co = 2 + 4 * rounds + 10
    slab = (wide, tall)
    block = (species, depth) + slab
    smem = pl.BlockSpec(memory_space=pltpu.SMEM)

    n_slot = 3 + 2 * rounds
    out = pl.pallas_call(
        functools.partial(fused_kernel, count),
        out_shape=jax.ShapeDtypeStruct(block, f32),
        in_specs=[_vmem()] * 2 + [smem] * 6,
        out_specs=_vmem(),
        scratch_shapes=[pltpu.VMEM(block, f32)] * 4
        + [pltpu.VMEM((n_co, species) + slab, f32), pltpu.VMEM((5, species) + slab, f32)]
        + [pltpu.VMEM((species,) + slab, f32)] * 2
        + [pltpu.VMEM((count,) + slab, f32)] * 6
        + [pltpu.VMEM((rounds, count) + slab, f32)] * 2
        + [pltpu.VMEM(slab, f32), pltpu.VMEM((2,) + slab, f32)]
        + [pltpu.SemaphoreType.DMA((2,))] * 2
        + [pltpu.VMEM(block, f32)]
        + [pltpu.VMEM((steps,) + slab, f32)] * 4
        + [pltpu.VMEM((steps, species) + slab, f32)]
        + [pltpu.VMEM((3, species) + slab, f32)]
        + [pltpu.VMEM((species,) + slab, f32)] * 4
        + [pltpu.VMEM((steps, rounds, species) + slab, f32)] * 4
        + [pltpu.SemaphoreType.DMA((steps, n_slot))] * 2,
        compiler_params=pltpu.CompilerParams(collective_id=0, has_side_effects=True),
        cost_estimate=pl.CostEstimate(
            flops=100 * steps * species * depth * wide * tall, transcendentals=0,
            bytes_accessed=3 * 4 * species * depth * wide * tall,
        ),
    )(values, zone, porosity, axial_number, courant, transverse, plan[0], feed_conc[0])
    return out[None]


def solution(mesh):
    in_specs = (
        P("col", None, "axial", None, "trans"),
        P("col", None, "trans"),
        P(),
        P(),
        P(),
        P(),
        P("col", None),
        P("col", None, None),
    )
    out_specs = P("col", None, "axial", None, "trans")
    return jax.shard_map(body, mesh=mesh, in_specs=in_specs, out_specs=out_specs, check_vma=False)
```

```python
import functools

import jax
import jax.numpy as jnp
from jax import lax
from jax.experimental import pallas as pl
from jax.experimental.pallas import tpu as pltpu
from jax.sharding import PartitionSpec as P


def swapped(array, axis, distance):
    return lax.ppermute(array, axis, [(i, i ^ 1 << distance) for i in range(lax.axis_size(axis))])


def from_behind(value, axis, steps):
    count = lax.axis_size(axis)
    initial, last = (max(0, -steps), min(count, count - steps))
    return lax.ppermute(value, axis, [(source, source + steps) for source in range(initial, last)])


def void_map(zone_map, porosity):
    voids = jnp.zeros(zone_map.shape, porosity.dtype)
    for number in range(porosity.shape[0]):
        voids = voids + jnp.where(zone_map == number, porosity[number], 0.0)
    return voids


def _vmem():
    return pl.BlockSpec(memory_space=pltpu.VMEM)


ROUNDS = (1, 2, 4, 8)
MESH = pl.DeviceIdType.MESH


def porosity_of(zone, por_ref):
    voids = jnp.zeros(zone.shape, jnp.float32)
    for number in range(por_ref.shape[0]):
        voids = voids + jnp.where(zone == number, por_ref[number], 0.0)
    return voids


def stencil_weights(voids, voids_lo, voids_hi, tr_ref, w_ref):
    wide, tall = voids.shape
    sublane = lax.broadcasted_iota(jnp.int32, (wide, tall), 0)
    lane = lax.broadcasted_iota(jnp.int32, (wide, tall), 1)
    p_xm = jnp.where(sublane == 0, 0.0, pltpu.roll(voids, 1, 0))
    p_xp = jnp.where(sublane == wide - 1, 0.0, pltpu.roll(voids, wide - 1, 0))
    p_ym = jnp.where(lane == 0, jnp.broadcast_to(voids_lo, (wide, tall)), pltpu.roll(voids, 1, 1))
    p_yp = jnp.where(lane == tall - 1, jnp.broadcast_to(voids_hi, (wide, tall)), pltpu.roll(voids, tall - 1, 1))
    faces = [2.0 * p / (voids + p) for p in (p_xm, p_xp, p_ym, p_yp)]
    for s in range(w_ref.shape[1]):
        scaled = [tr_ref[s] * face for face in faces]
        for direction in range(4):
            w_ref[1 + direction, s] = scaled[direction]
        w_ref[0, s] = 1.0 - (scaled[0] + scaled[1] + scaled[2] + scaled[3])


def setup(count, voids, ax_ref, cour_ref, cp_ref, ip_ref, l_ref, r_ref, co_ref, sub_ref, sup_ref,
          qf_ref, qb_ref, mf_ref, mb_ref, cprev_ref, hnext_ref, exf_ref, exb_ref):
    species, depth, wide, tall = cp_ref.shape
    position = lax.axis_index("axial")
    rounds = len(ROUNDS)
    at_outlet = position == count - 1
    for s in range(species):
        dispersion = ax_ref[s] + jnp.zeros((wide, tall), jnp.float32)
        flow_rate = cour_ref[s] / voids
        sub = -(dispersion + flow_rate)
        sup = -dispersion
        mi = 1.0 + 2.0 * dispersion + flow_rate
        me = 1.0 + dispersion + flow_rate
        sub_ref[s] = sub
        sup_ref[s] = sup
        coef = None
        for z in range(depth - 1):
            pivot = mi if z == 0 else mi - sub * coef
            inv = 1.0 / pivot
            coef = sup * inv
            ip_ref[s, z] = inv
            cp_ref[s, z] = coef

        down = ip_ref[s, 0]
        l_ref[s, 0] = down
        for z in range(1, depth - 1):
            down = -sub * down * ip_ref[s, z]
            l_ref[s, z] = down
        alpha = down
        beta = -cp_ref[s, depth - 2]
        for z in range(depth - 3, -1, -1):
            alpha = l_ref[s, z] - cp_ref[s, z] * alpha
            beta = -cp_ref[s, z] * beta

        def ends(last):
            inv_last = 1.0 / (last - sub * cp_ref[s, depth - 2])
            left_last = -sub * down * inv_last
            return alpha + beta * left_last, left_last, beta * inv_last, inv_last

        l0i, l1i, r0i, r1i = ends(mi)
        l0o, l1o, r0o, r1o = ends(me)

        own_last = jnp.where(at_outlet, me, mi)
        inv_last = 1.0 / (own_last - sub * cp_ref[s, depth - 2])
        ip_ref[s, depth - 1] = inv_last
        cp_ref[s, depth - 1] = sup * inv_last
        left = -sub * down * inv_last
        l_ref[s, depth - 1] = left
        l_ref[s, 0] = alpha + beta * left

        zero = jnp.zeros_like(sub)
        one = jnp.ones_like(sub)
        inner = (-sub * l0i, -sub * l1i, -sup * r0i, -sup * r1i)
        first = (zero, zero, inner[2], inner[3])
        outlet = (-sub * l0o, -sub * l1o, zero, zero)

        def couplings(j):
            return first if j == 0 else outlet if j == count - 1 else inner

        c_prev = zero
        for j in range(count):
            p0, p1, q0, q1 = couplings(j)
            inv = one if j == 0 else 1.0 / (1.0 - p0 * c_prev)
            qf_ref[j] = p1 * inv
            mf_ref[j] = p1 * c_prev * inv
            cprev_ref[j] = c_prev
            c_prev = q1 + p1 * c_prev * q0 * inv
        h_next = zero
        for j in range(count - 1, -1, -1):
            p0, p1, q0, q1 = couplings(j)
            inv = one if j == count - 1 else 1.0 / (1.0 - q1 * h_next)
            qb_ref[j] = q0 * inv
            mb_ref[j] = q0 * h_next * inv
            hnext_ref[j] = h_next
            h_next = p0 + q0 * h_next * p1 * inv

        co_ref[0, s] = mf_ref[position]
        co_ref[1, s] = mb_ref[position]
        qf_own = qf_ref[position]
        qb_own = qb_ref[position]
        for r in range(rounds):
            wef = one
            web = one
            for j in range(1, ROUNDS[r]):
                wef = wef * jnp.where(position - j >= 0, qf_ref[jnp.maximum(position - j, 0)], 1.0)
                web = web * jnp.where(position + j < count, qb_ref[jnp.minimum(position + j, count - 1)], 1.0)
            co_ref[2 + r, s] = wef
            co_ref[2 + rounds + r, s] = qf_own * wef
            co_ref[2 + 2 * rounds + r, s] = web
            co_ref[2 + 3 * rounds + r, s] = qb_own * web
        at_first = position == 0
        at_last = position == count - 1
        p0 = jnp.where(at_first, zero, jnp.where(at_last, outlet[0], inner[0]))
        p1 = jnp.where(at_first, zero, jnp.where(at_last, outlet[1], inner[1]))
        q0 = jnp.where(at_last, zero, inner[2])
        q1 = jnp.where(at_last, zero, inner[3])
        c_own = cprev_ref[position]
        h_own = hnext_ref[position]
        a11 = 1.0 - p0 * c_own
        a12 = -q0 * h_own
        a21 = -p1 * c_own
        a22 = 1.0 - q1 * h_own
        inv_det = 1.0 / (a11 * a22 - a12 * a21)
        base = 2 + 4 * rounds
        for i, value in enumerate(
            (p0, p1, q0, q1, c_own, h_own, a22 * inv_det, -a12 * inv_det, -a21 * inv_det, a11 * inv_det)
        ):
            co_ref[base + i, s] = value


def spike_rows(cp_ref, ip_ref, l_ref, r_ref):
    species, depth = cp_ref.shape[0], cp_ref.shape[1]
    for s in range(species):
        left = l_ref[s, depth - 1]
        right = ip_ref[s, depth - 1]
        r_ref[s, depth - 1] = right
        for z in range(depth - 2, 0, -1):
            left = l_ref[s, z] - cp_ref[s, z] * left
            l_ref[s, z] = left
            right = -cp_ref[s, z] * right
            r_ref[s, z] = right
        r_ref[s, 0] = -cp_ref[s, 0] * right


def fused_kernel(count, v_ref, zone_ref, por_ref, ax_ref, cour_ref, tr_ref, plan_ref, feed_ref,
                 o_ref,
                 cp_ref, ip_ref, l_ref, r_ref, co_ref, w_ref, sub_ref, sup_ref,
                 qf_ref, qb_ref, mf_ref, mb_ref, cprev_ref, hnext_ref, exf_ref, exb_ref,
                 vs_ref, vr_ref, vsem_s, vsem_r,
                 y_ref, hs_lo, hs_hi, hr_lo, hr_hi, face_in, g_ref, sf, sb, ef, eb,
                 snd_f, snd_b, rcv_f, rcv_b, send_sem, recv_sem):
    species, depth, wide, tall = v_ref.shape
    steps = plan_ref.shape[0]
    rounds = len(ROUNDS)
    position = lax.axis_index("axial")
    trans = lax.axis_index("trans")
    col = lax.axis_index("col")
    n_trans = lax.axis_size("trans")
    at_inlet = position == 0
    has_lo = trans > 0
    has_hi = trans < n_trans - 1
    lo_dev = (position, jnp.maximum(trans - 1, 0), col)
    hi_dev = (position, jnp.minimum(trans + 1, n_trans - 1), col)
    col_dev = (position, trans, 1 - col)
    lane = lax.broadcasted_iota(jnp.int32, (wide, tall), 1)
    base = 2 + 4 * rounds

    barrier = pltpu.get_barrier_semaphore()

    def greet(cond, device):
        @pl.when(cond)
        def _():
            pl.semaphore_signal(barrier, 1, device_id=device, device_id_type=MESH)

    greet(has_lo, lo_dev)
    greet(has_hi, hi_dev)
    greet(at_inlet, col_dev)
    partners = has_lo.astype(jnp.int32) + has_hi.astype(jnp.int32) + at_inlet.astype(jnp.int32)
    for d in ROUNDS:
        has_right = position + d < count
        has_left = position - d >= 0
        greet(has_right, (jnp.minimum(position + d, count - 1), trans, col))
        greet(has_left, (jnp.maximum(position - d, 0), trans, col))
        partners = partners + has_right.astype(jnp.int32) + has_left.astype(jnp.int32)
    voids = porosity_of(zone_ref[...], por_ref)
    vs_ref[...] = voids

    def run_setup():
        setup(count, voids, ax_ref, cour_ref, cp_ref, ip_ref, l_ref, r_ref, co_ref, sub_ref, sup_ref,
              qf_ref, qb_ref, mf_ref, mb_ref, cprev_ref, hnext_ref, exf_ref, exb_ref)

    pl.semaphore_wait(barrier, partners)

    zero_rows = jnp.zeros((species, wide, tall), jnp.float32)
    for h in range(steps):
        @pl.when(jnp.logical_not(has_lo))
        def _():
            hr_lo[h] = jnp.zeros((wide, tall), jnp.float32)

        @pl.when(jnp.logical_not(has_hi))
        def _():
            hr_hi[h] = jnp.zeros((wide, tall), jnp.float32)

        @pl.when(jnp.logical_not(at_inlet))
        def _():
            face_in[h] = zero_rows

    @pl.when(jnp.logical_not(has_lo))
    def _():
        vr_ref[0] = jnp.zeros((wide, tall), jnp.float32)

    @pl.when(jnp.logical_not(has_hi))
    def _():
        vr_ref[1] = jnp.zeros((wide, tall), jnp.float32)

    voids_up = pltpu.make_async_remote_copy(
        src_ref=vs_ref, dst_ref=vr_ref.at[0], send_sem=vsem_s.at[0], recv_sem=vsem_r.at[0],
        device_id=hi_dev, device_id_type=MESH,
    )
    voids_down = pltpu.make_async_remote_copy(
        src_ref=vs_ref, dst_ref=vr_ref.at[1], send_sem=vsem_s.at[1], recv_sem=vsem_r.at[1],
        device_id=lo_dev, device_id_type=MESH,
    )
    pl.when(has_hi)(voids_up.start)
    pl.when(has_lo)(voids_down.start)

    def exchange_start(h):
        src = v_ref if h == 0 else o_ref
        acc_lo = jnp.zeros((wide, tall), jnp.float32)
        acc_hi = jnp.zeros((wide, tall), jnp.float32)

        def column(s, z, c):
            if h == 0:
                return src[s, z, :, c : c + 1]
            cut = slice(c, c + 1)
            return (y_ref[s, z, :, cut] - ef[s, :, cut] * l_ref[s, z, :, cut]
                    - eb[s, :, cut] * r_ref[s, z, :, cut])

        for s in range(species):
            for z in range(depth):
                at = s * depth + z
                acc_lo = jnp.where(lane == at, jnp.broadcast_to(column(s, z, tall - 1), (wide, tall)), acc_lo)
                acc_hi = jnp.where(lane == at, jnp.broadcast_to(column(s, z, 0), (wide, tall)), acc_hi)
        hs_lo[h] = acc_lo
        hs_hi[h] = acc_hi
        copy_lo = pltpu.make_async_remote_copy(
            src_ref=hs_lo.at[h], dst_ref=hr_lo.at[h], send_sem=send_sem.at[h, 0], recv_sem=recv_sem.at[h, 0],
            device_id=hi_dev, device_id_type=MESH,
        )
        copy_hi = pltpu.make_async_remote_copy(
            src_ref=hs_hi.at[h], dst_ref=hr_hi.at[h], send_sem=send_sem.at[h, 1], recv_sem=recv_sem.at[h, 1],
            device_id=lo_dev, device_id_type=MESH,
        )
        copy_face = pltpu.make_async_remote_copy(
            src_ref=src.at[:, 0], dst_ref=face_in.at[h], send_sem=send_sem.at[h, 2], recv_sem=recv_sem.at[h, 2],
            device_id=col_dev, device_id_type=MESH,
        )
        pl.when(has_hi)(copy_lo.start)
        pl.when(has_lo)(copy_hi.start)
        pl.when(at_inlet)(copy_face.start)
        return copy_lo, copy_hi, copy_face

    def exchange_wait(copy_lo, copy_hi, copy_face):
        pl.when(has_lo)(copy_lo.wait_recv)
        pl.when(has_hi)(copy_hi.wait_recv)
        pl.when(has_hi)(copy_lo.wait_send)
        pl.when(has_lo)(copy_hi.wait_send)

    pending = exchange_start(0)
    run_setup()
    pl.when(has_lo)(voids_up.wait_recv)
    pl.when(has_hi)(voids_down.wait_recv)
    pl.when(has_hi)(voids_up.wait_send)
    pl.when(has_lo)(voids_down.wait_send)
    voids_lo = jnp.where(has_lo, vr_ref[0, :, tall - 1 : tall], 0.0)
    voids_hi = jnp.where(has_hi, vr_ref[1, :, 0:1], 0.0)
    stencil_weights(voids, voids_lo, voids_hi, tr_ref, w_ref)

    for h in range(steps):
        src = v_ref if h == 0 else o_ref
        copy_lo, copy_hi, copy_face = pending
        exchange_wait(copy_lo, copy_hi, copy_face)

        for s in range(species):
            w0 = w_ref[0, s]
            wxm = w_ref[1, s]
            wxp = w_ref[2, s]
            wym = w_ref[3, s]
            wyp = w_ref[4, s]
            sub = sub_ref[s]
            down = None
            for z in range(depth):
                v = src[s, z]
                xm = pltpu.roll(v, 1, 0)
                xp = pltpu.roll(v, wide - 1, 0)
                at = s * depth + z
                ym = jnp.where(lane == 0, hr_lo[h, :, at : at + 1], pltpu.roll(v, 1, 1))
                yp = jnp.where(lane == tall - 1, hr_hi[h, :, at : at + 1], pltpu.roll(v, tall - 1, 1))
                moved = w0 * v + ((wxp * xp + wxm * xm) + (wyp * yp + wym * ym))
                if z == 0:
                    down = moved * ip_ref[s, 0]
                else:
                    down = (moved - sub * down) * ip_ref[s, z]
                y_ref[s, z] = down
            solved = down
            g_ref[1, s] = solved
            for z in range(depth - 2, -1, -1):
                solved = y_ref[s, z] - cp_ref[s, z] * solved
                y_ref[s, z] = solved
            g_ref[0, s] = solved

        pl.when(at_inlet)(copy_face.wait_recv)
        pl.when(at_inlet)(copy_face.wait_send)
        for s in range(species):
            recycled = (plan_ref[h, s].astype(jnp.float32) + 1.0) * 0.25
            inlet = (1.0 - recycled) * feed_ref[s] + recycled * face_in[h, s]
            entry = jnp.where(at_inlet, -sub_ref[s] * inlet, 0.0)
            g_ref[2, s] = entry
            g_ref[0, s] = g_ref[0, s] + entry * l_ref[s, 0]
            g_ref[1, s] = g_ref[1, s] + entry * l_ref[s, depth - 1]
        g0 = g_ref[0]
        g1 = g_ref[1]
        sf[...] = g1 + co_ref[0] * g0
        sb[...] = g0 + co_ref[1] * g1
        ef[...] = zero_rows
        eb[...] = zero_rows
        sent = []
        for r in range(rounds):
            snd_f[h, r] = sf[...]
            snd_b[h, r] = sb[...]
            rank = r
            d = ROUNDS[r]
            has_right = position + d < count
            has_left = position - d >= 0
            right = jnp.minimum(position + d, count - 1)
            left = jnp.maximum(position - d, 0)
            copy_f = pltpu.make_async_remote_copy(
                src_ref=snd_f.at[h, r], dst_ref=rcv_f.at[h, r],
                send_sem=send_sem.at[h, 3 + r], recv_sem=recv_sem.at[h, 3 + r],
                device_id=(right, trans, col), device_id_type=MESH,
            )
            copy_b = pltpu.make_async_remote_copy(
                src_ref=snd_b.at[h, r], dst_ref=rcv_b.at[h, r],
                send_sem=send_sem.at[h, 3 + rounds + r], recv_sem=recv_sem.at[h, 3 + rounds + r],
                device_id=(left, trans, col), device_id_type=MESH,
            )
            pl.when(has_right)(copy_f.start)
            pl.when(has_left)(copy_b.start)
            last_round = r == rounds - 1
            if h == 0 and r == 0:
                spike_rows(cp_ref, ip_ref, l_ref, r_ref)

            @pl.when(has_left)
            def _():
                copy_f.wait_recv()
                got = rcv_f[h, r]
                ef[...] += co_ref[2 + rank] * got
                if not last_round:
                    sf[...] += co_ref[2 + rounds + rank] * got

            @pl.when(has_right)
            def _():
                copy_b.wait_recv()
                got = rcv_b[h, r]
                eb[...] += co_ref[2 + 2 * rounds + rank] * got
                if not last_round:
                    sb[...] += co_ref[2 + 3 * rounds + rank] * got

            sent.append((has_right, copy_f))
            sent.append((has_left, copy_b))

        before = ef[...]
        after = eb[...]
        r1 = g0 + co_ref[base + 0] * before + co_ref[base + 2] * after
        r2 = g1 + co_ref[base + 1] * before + co_ref[base + 3] * after
        top = r1 * co_ref[base + 6] + r2 * co_ref[base + 7]
        bottom = r1 * co_ref[base + 8] + r2 * co_ref[base + 9]
        ef[...] = sub_ref[...] * (before + co_ref[base + 4] * top)
        eb[...] = sup_ref[...] * (after + co_ref[base + 5] * bottom)
        for cond, copy in sent:
            pl.when(cond)(copy.wait_send)
        for s in range(species):
            ef[s] = ef[s] - g_ref[2, s]
        rows = range(depth)
        if h + 1 < steps:
            for s in range(species):
                o_ref[s, 0] = y_ref[s, 0] - ef[s] * l_ref[s, 0] - eb[s] * r_ref[s, 0]
            pending = exchange_start(h + 1)
            rows = range(1, depth)
        for s in range(species):
            left_coef = ef[s]
            right_coef = eb[s]
            for z in rows:
                o_ref[s, z] = y_ref[s, z] - left_coef * l_ref[s, z] - right_coef * r_ref[s, z]


def body(concentration, zone_map, porosity, axial_number, courant, transverse, feed_conc, plan):
    f32 = jnp.float32
    count = lax.axis_size("axial")
    values = concentration[0]
    species, depth, wide, tall = values.shape
    steps = plan.shape[1]
    zone = zone_map[0]
    assert species * depth <= tall
    rounds = len(ROUNDS)
    n_co = 2 + 4 * rounds + 10
    slab = (wide, tall)
    block = (species, depth) + slab
    smem = pl.BlockSpec(memory_space=pltpu.SMEM)

    n_slot = 3 + 2 * rounds
    out = pl.pallas_call(
        functools.partial(fused_kernel, count),
        out_shape=jax.ShapeDtypeStruct(block, f32),
        in_specs=[_vmem()] * 2 + [smem] * 6,
        out_specs=_vmem(),
        scratch_shapes=[pltpu.VMEM(block, f32)] * 4
        + [pltpu.VMEM((n_co, species) + slab, f32), pltpu.VMEM((5, species) + slab, f32)]
        + [pltpu.VMEM((species,) + slab, f32)] * 2
        + [pltpu.VMEM((count,) + slab, f32)] * 6
        + [pltpu.VMEM((rounds, count) + slab, f32)] * 2
        + [pltpu.VMEM(slab, f32), pltpu.VMEM((2,) + slab, f32)]
        + [pltpu.SemaphoreType.DMA((2,))] * 2
        + [pltpu.VMEM(block, f32)]
        + [pltpu.VMEM((steps,) + slab, f32)] * 4
        + [pltpu.VMEM((steps, species) + slab, f32)]
        + [pltpu.VMEM((3, species) + slab, f32)]
        + [pltpu.VMEM((species,) + slab, f32)] * 4
        + [pltpu.VMEM((steps, rounds, species) + slab, f32)] * 4
        + [pltpu.SemaphoreType.DMA((steps, n_slot))] * 2,
        compiler_params=pltpu.CompilerParams(collective_id=0, has_side_effects=True),
        cost_estimate=pl.CostEstimate(
            flops=100 * steps * species * depth * wide * tall, transcendentals=0,
            bytes_accessed=3 * 4 * species * depth * wide * tall,
        ),
    )(values, zone, porosity, axial_number, courant, transverse, plan[0], feed_conc[0])
    return out[None]


def solution(mesh):
    in_specs = (
        P("col", None, "axial", None, "trans"),
        P("col", None, "trans"),
        P(),
        P(),
        P(),
        P(),
        P("col", None),
        P("col", None, None),
    )
    out_specs = P("col", None, "axial", None, "trans")
    return jax.shard_map(body, mesh=mesh, in_specs=in_specs, out_specs=out_specs, check_vma=False)
```

```python
import functools

import jax
import jax.numpy as jnp
from jax import lax
from jax.experimental import pallas as pl
from jax.experimental.pallas import tpu as pltpu
from jax.sharding import PartitionSpec as P


def swapped(array, axis, distance):
    return lax.ppermute(array, axis, [(i, i ^ 1 << distance) for i in range(lax.axis_size(axis))])


def from_behind(value, axis, steps):
    count = lax.axis_size(axis)
    initial, last = (max(0, -steps), min(count, count - steps))
    return lax.ppermute(value, axis, [(source, source + steps) for source in range(initial, last)])


def void_map(zone_map, porosity):
    voids = jnp.zeros(zone_map.shape, porosity.dtype)
    for number in range(porosity.shape[0]):
        voids = voids + jnp.where(zone_map == number, porosity[number], 0.0)
    return voids


def _vmem():
    return pl.BlockSpec(memory_space=pltpu.VMEM)


ROUNDS = (1, 2, 4, 8)
MESH = pl.DeviceIdType.MESH


def porosity_of(zone, por_ref):
    voids = jnp.zeros(zone.shape, jnp.float32)
    for number in range(por_ref.shape[0]):
        voids = voids + jnp.where(zone == number, por_ref[number], 0.0)
    return voids


def stencil_weights(voids, voids_lo, voids_hi, tr_ref, w_ref):
    wide, tall = voids.shape
    sublane = lax.broadcasted_iota(jnp.int32, (wide, tall), 0)
    lane = lax.broadcasted_iota(jnp.int32, (wide, tall), 1)
    p_xm = jnp.where(sublane == 0, 0.0, pltpu.roll(voids, 1, 0))
    p_xp = jnp.where(sublane == wide - 1, 0.0, pltpu.roll(voids, wide - 1, 0))
    p_ym = jnp.where(lane == 0, jnp.broadcast_to(voids_lo, (wide, tall)), pltpu.roll(voids, 1, 1))
    p_yp = jnp.where(lane == tall - 1, jnp.broadcast_to(voids_hi, (wide, tall)), pltpu.roll(voids, tall - 1, 1))
    faces = [2.0 * p / (voids + p) for p in (p_xm, p_xp, p_ym, p_yp)]
    for s in range(w_ref.shape[1]):
        scaled = [tr_ref[s] * face for face in faces]
        for direction in range(4):
            w_ref[1 + direction, s] = scaled[direction]
        w_ref[0, s] = 1.0 - (scaled[0] + scaled[1] + scaled[2] + scaled[3])


def setup(count, voids, ax_ref, cour_ref, cp_ref, ip_ref, l_ref, r_ref, co_ref, sub_ref, sup_ref,
          qf_ref, qb_ref, mf_ref, mb_ref, cprev_ref, hnext_ref, exf_ref, exb_ref):
    species, depth, wide, tall = cp_ref.shape
    position = lax.axis_index("axial")
    rounds = len(ROUNDS)
    at_outlet = position == count - 1
    entries = []
    for s in range(species):
        dispersion = ax_ref[s] + jnp.zeros((wide, tall), jnp.float32)
        flow_rate = cour_ref[s] / voids
        sub = -(dispersion + flow_rate)
        sup = -dispersion
        sub_ref[s] = sub
        sup_ref[s] = sup
        entries.append((sub, sup, 1.0 + 2.0 * dispersion + flow_rate, 1.0 + dispersion + flow_rate))
    coefs = [None] * species
    for z in range(depth - 1):
        for s in range(species):
            sub, sup, mi, me = entries[s]
            pivot = mi if z == 0 else mi - sub * coefs[s]
            inv = 1.0 / pivot
            coefs[s] = sup * inv
            ip_ref[s, z] = inv
            cp_ref[s, z] = coefs[s]
    for s in range(species):
        sub, sup, mi, me = entries[s]
        down = ip_ref[s, 0]
        l_ref[s, 0] = down
        for z in range(1, depth - 1):
            down = -sub * down * ip_ref[s, z]
            l_ref[s, z] = down
        alpha = down
        beta = -cp_ref[s, depth - 2]
        for z in range(depth - 3, -1, -1):
            alpha = l_ref[s, z] - cp_ref[s, z] * alpha
            beta = -cp_ref[s, z] * beta

        def ends(last):
            inv_last = 1.0 / (last - sub * cp_ref[s, depth - 2])
            left_last = -sub * down * inv_last
            return alpha + beta * left_last, left_last, beta * inv_last, inv_last

        l0i, l1i, r0i, r1i = ends(mi)
        l0o, l1o, r0o, r1o = ends(me)

        own_last = jnp.where(at_outlet, me, mi)
        inv_last = 1.0 / (own_last - sub * cp_ref[s, depth - 2])
        ip_ref[s, depth - 1] = inv_last
        cp_ref[s, depth - 1] = sup * inv_last
        left = -sub * down * inv_last
        l_ref[s, depth - 1] = left
        l_ref[s, 0] = alpha + beta * left

        zero = jnp.zeros_like(sub)
        one = jnp.ones_like(sub)
        inner = (-sub * l0i, -sub * l1i, -sup * r0i, -sup * r1i)
        first = (zero, zero, inner[2], inner[3])
        outlet = (-sub * l0o, -sub * l1o, zero, zero)

        def couplings(j):
            return first if j == 0 else outlet if j == count - 1 else inner

        c_prev = zero
        for j in range(count):
            p0, p1, q0, q1 = couplings(j)
            inv = one if j == 0 else 1.0 / (1.0 - p0 * c_prev)
            qf_ref[j] = p1 * inv
            mf_ref[j] = p1 * c_prev * inv
            cprev_ref[j] = c_prev
            c_prev = q1 + p1 * c_prev * q0 * inv
        h_next = zero
        for j in range(count - 1, -1, -1):
            p0, p1, q0, q1 = couplings(j)
            inv = one if j == count - 1 else 1.0 / (1.0 - q1 * h_next)
            qb_ref[j] = q0 * inv
            mb_ref[j] = q0 * h_next * inv
            hnext_ref[j] = h_next
            h_next = p0 + q0 * h_next * p1 * inv

        for kk in range(count):
            exf_ref[0, kk] = one
            exb_ref[0, kk] = one
        for r in range(rounds - 1):
            d = ROUNDS[r]
            for kk in range(count):
                if kk - d >= 0:
                    exf_ref[r + 1, kk] = exf_ref[r, kk] * qf_ref[kk - d] * exf_ref[r, kk - d]
                else:
                    exf_ref[r + 1, kk] = one
                if kk + d < count:
                    exb_ref[r + 1, kk] = exb_ref[r, kk] * qb_ref[kk + d] * exb_ref[r, kk + d]
                else:
                    exb_ref[r + 1, kk] = one

        co_ref[0, s] = mf_ref[position]
        co_ref[1, s] = mb_ref[position]
        qf_own = qf_ref[position]
        qb_own = qb_ref[position]
        for r in range(rounds):
            wef = exf_ref[r, position]
            web = exb_ref[r, position]
            co_ref[2 + r, s] = wef
            co_ref[2 + rounds + r, s] = qf_own * wef
            co_ref[2 + 2 * rounds + r, s] = web
            co_ref[2 + 3 * rounds + r, s] = qb_own * web
        at_first = position == 0
        at_last = position == count - 1
        p0 = jnp.where(at_first, zero, jnp.where(at_last, outlet[0], inner[0]))
        p1 = jnp.where(at_first, zero, jnp.where(at_last, outlet[1], inner[1]))
        q0 = jnp.where(at_last, zero, inner[2])
        q1 = jnp.where(at_last, zero, inner[3])
        c_own = cprev_ref[position]
        h_own = hnext_ref[position]
        a11 = 1.0 - p0 * c_own
        a12 = -q0 * h_own
        a21 = -p1 * c_own
        a22 = 1.0 - q1 * h_own
        inv_det = 1.0 / (a11 * a22 - a12 * a21)
        base = 2 + 4 * rounds
        for i, value in enumerate(
            (p0, p1, q0, q1, c_own, h_own, a22 * inv_det, -a12 * inv_det, -a21 * inv_det, a11 * inv_det)
        ):
            co_ref[base + i, s] = value


def spike_rows(cp_ref, ip_ref, l_ref, r_ref):
    species, depth = cp_ref.shape[0], cp_ref.shape[1]
    for s in range(species):
        left = l_ref[s, depth - 1]
        right = ip_ref[s, depth - 1]
        r_ref[s, depth - 1] = right
        for z in range(depth - 2, 0, -1):
            left = l_ref[s, z] - cp_ref[s, z] * left
            l_ref[s, z] = left
            right = -cp_ref[s, z] * right
            r_ref[s, z] = right
        r_ref[s, 0] = -cp_ref[s, 0] * right


def fused_kernel(count, v_ref, zone_ref, por_ref, ax_ref, cour_ref, tr_ref, plan_ref, feed_ref,
                 o_ref,
                 cp_ref, ip_ref, l_ref, r_ref, co_ref, w_ref, sub_ref, sup_ref,
                 qf_ref, qb_ref, mf_ref, mb_ref, cprev_ref, hnext_ref, exf_ref, exb_ref,
                 vs_ref, vr_ref, vsem_s, vsem_r,
                 y_ref, hs_lo, hs_hi, hr_lo, hr_hi, face_in, g_ref, sf, sb, ef, eb,
                 snd_f, snd_b, rcv_f, rcv_b, send_sem, recv_sem):
    species, depth, wide, tall = v_ref.shape
    steps = plan_ref.shape[0]
    rounds = len(ROUNDS)
    position = lax.axis_index("axial")
    trans = lax.axis_index("trans")
    col = lax.axis_index("col")
    n_trans = lax.axis_size("trans")
    at_inlet = position == 0
    has_lo = trans > 0
    has_hi = trans < n_trans - 1
    lo_dev = (position, jnp.maximum(trans - 1, 0), col)
    hi_dev = (position, jnp.minimum(trans + 1, n_trans - 1), col)
    col_dev = (position, trans, 1 - col)
    lane = lax.broadcasted_iota(jnp.int32, (wide, tall), 1)
    base = 2 + 4 * rounds

    barrier = pltpu.get_barrier_semaphore()

    def greet(cond, device):
        @pl.when(cond)
        def _():
            pl.semaphore_signal(barrier, 1, device_id=device, device_id_type=MESH)

    greet(has_lo, lo_dev)
    greet(has_hi, hi_dev)
    greet(at_inlet, col_dev)
    partners = has_lo.astype(jnp.int32) + has_hi.astype(jnp.int32) + at_inlet.astype(jnp.int32)
    for d in ROUNDS:
        has_right = position + d < count
        has_left = position - d >= 0
        greet(has_right, (jnp.minimum(position + d, count - 1), trans, col))
        greet(has_left, (jnp.maximum(position - d, 0), trans, col))
        partners = partners + has_right.astype(jnp.int32) + has_left.astype(jnp.int32)
    voids = porosity_of(zone_ref[...], por_ref)
    vs_ref[...] = voids

    def run_setup():
        setup(count, voids, ax_ref, cour_ref, cp_ref, ip_ref, l_ref, r_ref, co_ref, sub_ref, sup_ref,
              qf_ref, qb_ref, mf_ref, mb_ref, cprev_ref, hnext_ref, exf_ref, exb_ref)

    pl.semaphore_wait(barrier, partners)

    zero_rows = jnp.zeros((species, wide, tall), jnp.float32)
    for h in range(steps):
        @pl.when(jnp.logical_not(has_lo))
        def _():
            hr_lo[h] = jnp.zeros((wide, tall), jnp.float32)

        @pl.when(jnp.logical_not(has_hi))
        def _():
            hr_hi[h] = jnp.zeros((wide, tall), jnp.float32)

        @pl.when(jnp.logical_not(at_inlet))
        def _():
            face_in[h] = zero_rows

    @pl.when(jnp.logical_not(has_lo))
    def _():
        vr_ref[0] = jnp.zeros((wide, tall), jnp.float32)

    @pl.when(jnp.logical_not(has_hi))
    def _():
        vr_ref[1] = jnp.zeros((wide, tall), jnp.float32)

    voids_up = pltpu.make_async_remote_copy(
        src_ref=vs_ref, dst_ref=vr_ref.at[0], send_sem=vsem_s.at[0], recv_sem=vsem_r.at[0],
        device_id=hi_dev, device_id_type=MESH,
    )
    voids_down = pltpu.make_async_remote_copy(
        src_ref=vs_ref, dst_ref=vr_ref.at[1], send_sem=vsem_s.at[1], recv_sem=vsem_r.at[1],
        device_id=lo_dev, device_id_type=MESH,
    )
    pl.when(has_hi)(voids_up.start)
    pl.when(has_lo)(voids_down.start)

    def exchange_start(h):
        src = v_ref if h == 0 else o_ref
        acc_lo = jnp.zeros((wide, tall), jnp.float32)
        acc_hi = jnp.zeros((wide, tall), jnp.float32)

        def column(s, z, c):
            if h == 0:
                return src[s, z, :, c : c + 1]
            cut = slice(c, c + 1)
            return (y_ref[s, z, :, cut] - ef[s, :, cut] * l_ref[s, z, :, cut]
                    - eb[s, :, cut] * r_ref[s, z, :, cut])

        for s in range(species):
            for z in range(depth):
                at = s * depth + z
                acc_lo = jnp.where(lane == at, jnp.broadcast_to(column(s, z, tall - 1), (wide, tall)), acc_lo)
                acc_hi = jnp.where(lane == at, jnp.broadcast_to(column(s, z, 0), (wide, tall)), acc_hi)
        hs_lo[h] = acc_lo
        hs_hi[h] = acc_hi
        copy_lo = pltpu.make_async_remote_copy(
            src_ref=hs_lo.at[h], dst_ref=hr_lo.at[h], send_sem=send_sem.at[h, 0], recv_sem=recv_sem.at[h, 0],
            device_id=hi_dev, device_id_type=MESH,
        )
        copy_hi = pltpu.make_async_remote_copy(
            src_ref=hs_hi.at[h], dst_ref=hr_hi.at[h], send_sem=send_sem.at[h, 1], recv_sem=recv_sem.at[h, 1],
            device_id=lo_dev, device_id_type=MESH,
        )
        copy_face = pltpu.make_async_remote_copy(
            src_ref=src.at[:, 0], dst_ref=face_in.at[h], send_sem=send_sem.at[h, 2], recv_sem=recv_sem.at[h, 2],
            device_id=col_dev, device_id_type=MESH,
        )
        pl.when(has_hi)(copy_lo.start)
        pl.when(has_lo)(copy_hi.start)
        pl.when(at_inlet)(copy_face.start)
        return copy_lo, copy_hi, copy_face

    def exchange_wait(copy_lo, copy_hi, copy_face):
        pl.when(has_lo)(copy_lo.wait_recv)
        pl.when(has_hi)(copy_hi.wait_recv)
        pl.when(has_hi)(copy_lo.wait_send)
        pl.when(has_lo)(copy_hi.wait_send)

    pending = exchange_start(0)
    run_setup()
    pl.when(has_lo)(voids_up.wait_recv)
    pl.when(has_hi)(voids_down.wait_recv)
    pl.when(has_hi)(voids_up.wait_send)
    pl.when(has_lo)(voids_down.wait_send)
    voids_lo = jnp.where(has_lo, vr_ref[0, :, tall - 1 : tall], 0.0)
    voids_hi = jnp.where(has_hi, vr_ref[1, :, 0:1], 0.0)
    stencil_weights(voids, voids_lo, voids_hi, tr_ref, w_ref)

    for h in range(steps):
        src = v_ref if h == 0 else o_ref
        copy_lo, copy_hi, copy_face = pending
        exchange_wait(copy_lo, copy_hi, copy_face)

        for s in range(species):
            w0 = w_ref[0, s]
            wxm = w_ref[1, s]
            wxp = w_ref[2, s]
            wym = w_ref[3, s]
            wyp = w_ref[4, s]
            sub = sub_ref[s]
            down = None
            for z in range(depth):
                v = src[s, z]
                xm = pltpu.roll(v, 1, 0)
                xp = pltpu.roll(v, wide - 1, 0)
                at = s * depth + z
                ym = jnp.where(lane == 0, hr_lo[h, :, at : at + 1], pltpu.roll(v, 1, 1))
                yp = jnp.where(lane == tall - 1, hr_hi[h, :, at : at + 1], pltpu.roll(v, tall - 1, 1))
                moved = w0 * v + ((wxp * xp + wxm * xm) + (wyp * yp + wym * ym))
                if z == 0:
                    down = moved * ip_ref[s, 0]
                else:
                    down = (moved - sub * down) * ip_ref[s, z]
                y_ref[s, z] = down
            solved = down
            g_ref[1, s] = solved
            for z in range(depth - 2, -1, -1):
                solved = y_ref[s, z] - cp_ref[s, z] * solved
                y_ref[s, z] = solved
            g_ref[0, s] = solved

        pl.when(at_inlet)(copy_face.wait_recv)
        pl.when(at_inlet)(copy_face.wait_send)
        for s in range(species):
            recycled = (plan_ref[h, s].astype(jnp.float32) + 1.0) * 0.25
            inlet = (1.0 - recycled) * feed_ref[s] + recycled * face_in[h, s]
            entry = jnp.where(at_inlet, -sub_ref[s] * inlet, 0.0)
            g_ref[2, s] = entry
            g_ref[0, s] = g_ref[0, s] + entry * l_ref[s, 0]
            g_ref[1, s] = g_ref[1, s] + entry * l_ref[s, depth - 1]
        g0 = g_ref[0]
        g1 = g_ref[1]
        sf[...] = g1 + co_ref[0] * g0
        sb[...] = g0 + co_ref[1] * g1
        ef[...] = zero_rows
        eb[...] = zero_rows
        sent = []
        for r in range(rounds):
            snd_f[h, r] = sf[...]
            snd_b[h, r] = sb[...]
            rank = r
            d = ROUNDS[r]
            has_right = position + d < count
            has_left = position - d >= 0
            right = jnp.minimum(position + d, count - 1)
            left = jnp.maximum(position - d, 0)
            copy_f = pltpu.make_async_remote_copy(
                src_ref=snd_f.at[h, r], dst_ref=rcv_f.at[h, r],
                send_sem=send_sem.at[h, 3 + r], recv_sem=recv_sem.at[h, 3 + r],
                device_id=(right, trans, col), device_id_type=MESH,
            )
            copy_b = pltpu.make_async_remote_copy(
                src_ref=snd_b.at[h, r], dst_ref=rcv_b.at[h, r],
                send_sem=send_sem.at[h, 3 + rounds + r], recv_sem=recv_sem.at[h, 3 + rounds + r],
                device_id=(left, trans, col), device_id_type=MESH,
            )
            pl.when(has_right)(copy_f.start)
            pl.when(has_left)(copy_b.start)
            last_round = r == rounds - 1
            if h == 0 and r == 0:
                spike_rows(cp_ref, ip_ref, l_ref, r_ref)

            @pl.when(has_left)
            def _():
                copy_f.wait_recv()
                got = rcv_f[h, r]
                ef[...] += co_ref[2 + rank] * got
                if not last_round:
                    sf[...] += co_ref[2 + rounds + rank] * got

            @pl.when(has_right)
            def _():
                copy_b.wait_recv()
                got = rcv_b[h, r]
                eb[...] += co_ref[2 + 2 * rounds + rank] * got
                if not last_round:
                    sb[...] += co_ref[2 + 3 * rounds + rank] * got

            sent.append((has_right, copy_f))
            sent.append((has_left, copy_b))

        before = ef[...]
        after = eb[...]
        r1 = g0 + co_ref[base + 0] * before + co_ref[base + 2] * after
        r2 = g1 + co_ref[base + 1] * before + co_ref[base + 3] * after
        top = r1 * co_ref[base + 6] + r2 * co_ref[base + 7]
        bottom = r1 * co_ref[base + 8] + r2 * co_ref[base + 9]
        ef[...] = sub_ref[...] * (before + co_ref[base + 4] * top)
        eb[...] = sup_ref[...] * (after + co_ref[base + 5] * bottom)
        for cond, copy in sent:
            pl.when(cond)(copy.wait_send)
        for s in range(species):
            ef[s] = ef[s] - g_ref[2, s]
        rows = range(depth)
        if h + 1 < steps:
            for s in range(species):
                o_ref[s, 0] = y_ref[s, 0] - ef[s] * l_ref[s, 0] - eb[s] * r_ref[s, 0]
            pending = exchange_start(h + 1)
            rows = range(1, depth)
        for s in range(species):
            left_coef = ef[s]
            right_coef = eb[s]
            for z in rows:
                o_ref[s, z] = y_ref[s, z] - left_coef * l_ref[s, z] - right_coef * r_ref[s, z]


def body(concentration, zone_map, porosity, axial_number, courant, transverse, feed_conc, plan):
    f32 = jnp.float32
    count = lax.axis_size("axial")
    values = concentration[0]
    species, depth, wide, tall = values.shape
    steps = plan.shape[1]
    zone = zone_map[0]
    assert species * depth <= tall
    rounds = len(ROUNDS)
    n_co = 2 + 4 * rounds + 10
    slab = (wide, tall)
    block = (species, depth) + slab
    smem = pl.BlockSpec(memory_space=pltpu.SMEM)

    n_slot = 3 + 2 * rounds
    out = pl.pallas_call(
        functools.partial(fused_kernel, count),
        out_shape=jax.ShapeDtypeStruct(block, f32),
        in_specs=[_vmem()] * 2 + [smem] * 6,
        out_specs=_vmem(),
        scratch_shapes=[pltpu.VMEM(block, f32)] * 4
        + [pltpu.VMEM((n_co, species) + slab, f32), pltpu.VMEM((5, species) + slab, f32)]
        + [pltpu.VMEM((species,) + slab, f32)] * 2
        + [pltpu.VMEM((count,) + slab, f32)] * 6
        + [pltpu.VMEM((rounds, count) + slab, f32)] * 2
        + [pltpu.VMEM(slab, f32), pltpu.VMEM((2,) + slab, f32)]
        + [pltpu.SemaphoreType.DMA((2,))] * 2
        + [pltpu.VMEM(block, f32)]
        + [pltpu.VMEM((steps,) + slab, f32)] * 4
        + [pltpu.VMEM((steps, species) + slab, f32)]
        + [pltpu.VMEM((3, species) + slab, f32)]
        + [pltpu.VMEM((species,) + slab, f32)] * 4
        + [pltpu.VMEM((steps, rounds, species) + slab, f32)] * 4
        + [pltpu.SemaphoreType.DMA((steps, n_slot))] * 2,
        compiler_params=pltpu.CompilerParams(collective_id=0, has_side_effects=True),
        cost_estimate=pl.CostEstimate(
            flops=100 * steps * species * depth * wide * tall, transcendentals=0,
            bytes_accessed=3 * 4 * species * depth * wide * tall,
        ),
    )(values, zone, porosity, axial_number, courant, transverse, plan[0], feed_conc[0])
    return out[None]


def solution(mesh):
    in_specs = (
        P("col", None, "axial", None, "trans"),
        P("col", None, "trans"),
        P(),
        P(),
        P(),
        P(),
        P("col", None),
        P("col", None, None),
    )
    out_specs = P("col", None, "axial", None, "trans")
    return jax.shard_map(body, mesh=mesh, in_specs=in_specs, out_specs=out_specs, check_vma=False)
```

```python
import functools

import jax
import jax.numpy as jnp
from jax import lax
from jax.experimental import pallas as pl
from jax.experimental.pallas import tpu as pltpu
from jax.sharding import PartitionSpec as P


def swapped(array, axis, distance):
    return lax.ppermute(array, axis, [(i, i ^ 1 << distance) for i in range(lax.axis_size(axis))])


def from_behind(value, axis, steps):
    count = lax.axis_size(axis)
    initial, last = (max(0, -steps), min(count, count - steps))
    return lax.ppermute(value, axis, [(source, source + steps) for source in range(initial, last)])


def void_map(zone_map, porosity):
    voids = jnp.zeros(zone_map.shape, porosity.dtype)
    for number in range(porosity.shape[0]):
        voids = voids + jnp.where(zone_map == number, porosity[number], 0.0)
    return voids


def _vmem():
    return pl.BlockSpec(memory_space=pltpu.VMEM)


ROUNDS = (1, 2, 4, 8)
MESH = pl.DeviceIdType.MESH


def porosity_of(zone, por_ref):
    voids = jnp.zeros(zone.shape, jnp.float32)
    for number in range(por_ref.shape[0]):
        voids = voids + jnp.where(zone == number, por_ref[number], 0.0)
    return voids


def stencil_weights(voids, voids_lo, voids_hi, tr_ref, w_ref):
    wide, tall = voids.shape
    sublane = lax.broadcasted_iota(jnp.int32, (wide, tall), 0)
    lane = lax.broadcasted_iota(jnp.int32, (wide, tall), 1)
    p_xm = jnp.where(sublane == 0, 0.0, pltpu.roll(voids, 1, 0))
    p_xp = jnp.where(sublane == wide - 1, 0.0, pltpu.roll(voids, wide - 1, 0))
    p_ym = jnp.where(lane == 0, jnp.broadcast_to(voids_lo, (wide, tall)), pltpu.roll(voids, 1, 1))
    p_yp = jnp.where(lane == tall - 1, jnp.broadcast_to(voids_hi, (wide, tall)), pltpu.roll(voids, tall - 1, 1))
    faces = [2.0 * p / (voids + p) for p in (p_xm, p_xp, p_ym, p_yp)]
    for s in range(w_ref.shape[1]):
        scaled = [tr_ref[s] * face for face in faces]
        for direction in range(4):
            w_ref[1 + direction, s] = scaled[direction]
        w_ref[0, s] = 1.0 - (scaled[0] + scaled[1] + scaled[2] + scaled[3])


def setup(count, voids, ax_ref, cour_ref, cp_ref, ip_ref, l_ref, r_ref, co_ref, sub_ref, sup_ref,
          qf_ref, qb_ref, mf_ref, mb_ref, cprev_ref, hnext_ref, exf_ref, exb_ref):
    species, depth, wide, tall = cp_ref.shape
    position = lax.axis_index("axial")
    rounds = len(ROUNDS)
    at_outlet = position == count - 1
    for s in range(species):
        dispersion = ax_ref[s] + jnp.zeros((wide, tall), jnp.float32)
        flow_rate = cour_ref[s] / voids
        sub = -(dispersion + flow_rate)
        sup = -dispersion
        mi = 1.0 + 2.0 * dispersion + flow_rate
        me = 1.0 + dispersion + flow_rate
        sub_ref[s] = sub
        sup_ref[s] = sup
        coef = None
        for z in range(depth - 1):
            pivot = mi if z == 0 else mi - sub * coef
            inv = 1.0 / pivot
            coef = sup * inv
            ip_ref[s, z] = inv
            cp_ref[s, z] = coef

        down = ip_ref[s, 0]
        l_ref[s, 0] = down
        for z in range(1, depth - 1):
            down = -sub * down * ip_ref[s, z]
            l_ref[s, z] = down
        alpha = down
        beta = -cp_ref[s, depth - 2]
        for z in range(depth - 3, -1, -1):
            alpha = l_ref[s, z] - cp_ref[s, z] * alpha
            beta = -cp_ref[s, z] * beta

        def ends(last):
            inv_last = 1.0 / (last - sub * cp_ref[s, depth - 2])
            left_last = -sub * down * inv_last
            return alpha + beta * left_last, left_last, beta * inv_last, inv_last

        l0i, l1i, r0i, r1i = ends(mi)
        l0o, l1o, r0o, r1o = ends(me)

        own_last = jnp.where(at_outlet, me, mi)
        inv_last = 1.0 / (own_last - sub * cp_ref[s, depth - 2])
        ip_ref[s, depth - 1] = inv_last
        cp_ref[s, depth - 1] = sup * inv_last
        left = -sub * down * inv_last
        l_ref[s, depth - 1] = left
        l_ref[s, 0] = alpha + beta * left

        zero = jnp.zeros_like(sub)
        one = jnp.ones_like(sub)
        inner = (-sub * l0i, -sub * l1i, -sup * r0i, -sup * r1i)
        first = (zero, zero, inner[2], inner[3])
        outlet = (-sub * l0o, -sub * l1o, zero, zero)

        def couplings(j):
            return first if j == 0 else outlet if j == count - 1 else inner

        c_prev = zero
        for j in range(count):
            p0, p1, q0, q1 = couplings(j)
            inv = one if j == 0 else 1.0 / (1.0 - p0 * c_prev)
            qf_ref[j] = p1 * inv
            mf_ref[j] = p1 * c_prev * inv
            cprev_ref[j] = c_prev
            c_prev = q1 + p1 * c_prev * q0 * inv
        h_next = zero
        for j in range(count - 1, -1, -1):
            p0, p1, q0, q1 = couplings(j)
            inv = one if j == count - 1 else 1.0 / (1.0 - q1 * h_next)
            qb_ref[j] = q0 * inv
            mb_ref[j] = q0 * h_next * inv
            hnext_ref[j] = h_next
            h_next = p0 + q0 * h_next * p1 * inv

        for kk in range(count):
            exf_ref[0, kk] = one
            exb_ref[0, kk] = one
        for r in range(rounds - 1):
            d = ROUNDS[r]
            for kk in range(count):
                if kk - d >= 0:
                    exf_ref[r + 1, kk] = exf_ref[r, kk] * qf_ref[kk - d] * exf_ref[r, kk - d]
                else:
                    exf_ref[r + 1, kk] = one
                if kk + d < count:
                    exb_ref[r + 1, kk] = exb_ref[r, kk] * qb_ref[kk + d] * exb_ref[r, kk + d]
                else:
                    exb_ref[r + 1, kk] = one

        co_ref[0, s] = mf_ref[position]
        co_ref[1, s] = mb_ref[position]
        qf_own = qf_ref[position]
        qb_own = qb_ref[position]
        for r in range(rounds):
            wef = exf_ref[r, position]
            web = exb_ref[r, position]
            co_ref[2 + r, s] = wef
            co_ref[2 + rounds + r, s] = qf_own * wef
            co_ref[2 + 2 * rounds + r, s] = web
            co_ref[2 + 3 * rounds + r, s] = qb_own * web
        at_first = position == 0
        at_last = position == count - 1
        p0 = jnp.where(at_first, zero, jnp.where(at_last, outlet[0], inner[0]))
        p1 = jnp.where(at_first, zero, jnp.where(at_last, outlet[1], inner[1]))
        q0 = jnp.where(at_last, zero, inner[2])
        q1 = jnp.where(at_last, zero, inner[3])
        c_own = cprev_ref[position]
        h_own = hnext_ref[position]
        a11 = 1.0 - p0 * c_own
        a12 = -q0 * h_own
        a21 = -p1 * c_own
        a22 = 1.0 - q1 * h_own
        inv_det = 1.0 / (a11 * a22 - a12 * a21)
        base = 2 + 4 * rounds
        for i, value in enumerate(
            (p0, p1, q0, q1, c_own, h_own, a22 * inv_det, -a12 * inv_det, -a21 * inv_det, a11 * inv_det)
        ):
            co_ref[base + i, s] = value


def spike_rows(cp_ref, ip_ref, l_ref, r_ref):
    species, depth = cp_ref.shape[0], cp_ref.shape[1]
    for s in range(species):
        left = l_ref[s, depth - 1]
        right = ip_ref[s, depth - 1]
        r_ref[s, depth - 1] = right
        for z in range(depth - 2, 0, -1):
            left = l_ref[s, z] - cp_ref[s, z] * left
            l_ref[s, z] = left
            right = -cp_ref[s, z] * right
            r_ref[s, z] = right
        r_ref[s, 0] = -cp_ref[s, 0] * right


def fused_kernel(count, v_ref, zone_ref, por_ref, ax_ref, cour_ref, tr_ref, plan_ref, feed_ref,
                 o_ref,
                 cp_ref, ip_ref, l_ref, r_ref, co_ref, w_ref, sub_ref, sup_ref,
                 qf_ref, qb_ref, mf_ref, mb_ref, cprev_ref, hnext_ref, exf_ref, exb_ref,
                 vs_ref, vr_ref, vsem_s, vsem_r,
                 y_ref, hs_lo, hs_hi, hr_lo, hr_hi, face_in, g_ref, sf, sb, ef, eb,
                 snd_f, snd_b, rcv_f, rcv_b, send_sem, recv_sem):
    species, depth, wide, tall = v_ref.shape
    steps = plan_ref.shape[0]
    rounds = len(ROUNDS)
    position = lax.axis_index("axial")
    trans = lax.axis_index("trans")
    col = lax.axis_index("col")
    n_trans = lax.axis_size("trans")
    at_inlet = position == 0
    has_lo = trans > 0
    has_hi = trans < n_trans - 1
    lo_dev = (position, jnp.maximum(trans - 1, 0), col)
    hi_dev = (position, jnp.minimum(trans + 1, n_trans - 1), col)
    col_dev = (position, trans, 1 - col)
    lane = lax.broadcasted_iota(jnp.int32, (wide, tall), 1)
    base = 2 + 4 * rounds

    barrier = pltpu.get_barrier_semaphore()

    def greet(cond, device):
        @pl.when(cond)
        def _():
            pl.semaphore_signal(barrier, 1, device_id=device, device_id_type=MESH)

    greet(has_lo, lo_dev)
    greet(has_hi, hi_dev)
    greet(at_inlet, col_dev)
    partners = has_lo.astype(jnp.int32) + has_hi.astype(jnp.int32) + at_inlet.astype(jnp.int32)
    for d in ROUNDS:
        has_right = position + d < count
        has_left = position - d >= 0
        greet(has_right, (jnp.minimum(position + d, count - 1), trans, col))
        greet(has_left, (jnp.maximum(position - d, 0), trans, col))
        partners = partners + has_right.astype(jnp.int32) + has_left.astype(jnp.int32)
    voids = porosity_of(zone_ref[...], por_ref)
    vs_ref[...] = voids

    def run_setup():
        setup(count, voids, ax_ref, cour_ref, cp_ref, ip_ref, l_ref, r_ref, co_ref, sub_ref, sup_ref,
              qf_ref, qb_ref, mf_ref, mb_ref, cprev_ref, hnext_ref, exf_ref, exb_ref)

    pl.semaphore_wait(barrier, partners)

    zero_rows = jnp.zeros((species, wide, tall), jnp.float32)
    for h in range(steps):
        @pl.when(jnp.logical_not(has_lo))
        def _():
            hr_lo[h] = jnp.zeros((wide, tall), jnp.float32)

        @pl.when(jnp.logical_not(has_hi))
        def _():
            hr_hi[h] = jnp.zeros((wide, tall), jnp.float32)

        @pl.when(jnp.logical_not(at_inlet))
        def _():
            face_in[h] = zero_rows

    @pl.when(jnp.logical_not(has_lo))
    def _():
        vr_ref[0] = jnp.zeros((wide, tall), jnp.float32)

    @pl.when(jnp.logical_not(has_hi))
    def _():
        vr_ref[1] = jnp.zeros((wide, tall), jnp.float32)

    voids_up = pltpu.make_async_remote_copy(
        src_ref=vs_ref, dst_ref=vr_ref.at[0], send_sem=vsem_s.at[0], recv_sem=vsem_r.at[0],
        device_id=hi_dev, device_id_type=MESH,
    )
    voids_down = pltpu.make_async_remote_copy(
        src_ref=vs_ref, dst_ref=vr_ref.at[1], send_sem=vsem_s.at[1], recv_sem=vsem_r.at[1],
        device_id=lo_dev, device_id_type=MESH,
    )
    pl.when(has_hi)(voids_up.start)
    pl.when(has_lo)(voids_down.start)

    def exchange_start(h):
        src = v_ref if h == 0 else o_ref
        acc_lo = jnp.zeros((wide, tall), jnp.float32)
        acc_hi = jnp.zeros((wide, tall), jnp.float32)

        def column(s, z, c):
            if h == 0:
                return src[s, z, :, c : c + 1]
            cut = slice(c, c + 1)
            return (y_ref[s, z, :, cut] - ef[s, :, cut] * l_ref[s, z, :, cut]
                    - eb[s, :, cut] * r_ref[s, z, :, cut])

        for s in range(species):
            for z in range(depth):
                at = s * depth + z
                acc_lo = jnp.where(lane == at, jnp.broadcast_to(column(s, z, tall - 1), (wide, tall)), acc_lo)
                acc_hi = jnp.where(lane == at, jnp.broadcast_to(column(s, z, 0), (wide, tall)), acc_hi)
        hs_lo[h] = acc_lo
        hs_hi[h] = acc_hi
        copy_lo = pltpu.make_async_remote_copy(
            src_ref=hs_lo.at[h], dst_ref=hr_lo.at[h], send_sem=send_sem.at[h, 0], recv_sem=recv_sem.at[h, 0],
            device_id=hi_dev, device_id_type=MESH,
        )
        copy_hi = pltpu.make_async_remote_copy(
            src_ref=hs_hi.at[h], dst_ref=hr_hi.at[h], send_sem=send_sem.at[h, 1], recv_sem=recv_sem.at[h, 1],
            device_id=lo_dev, device_id_type=MESH,
        )
        copy_face = pltpu.make_async_remote_copy(
            src_ref=src.at[:, 0], dst_ref=face_in.at[h], send_sem=send_sem.at[h, 2], recv_sem=recv_sem.at[h, 2],
            device_id=col_dev, device_id_type=MESH,
        )
        pl.when(has_hi)(copy_lo.start)
        pl.when(has_lo)(copy_hi.start)
        pl.when(at_inlet)(copy_face.start)
        return copy_lo, copy_hi, copy_face

    def exchange_wait(copy_lo, copy_hi, copy_face):
        pl.when(has_lo)(copy_lo.wait_recv)
        pl.when(has_hi)(copy_hi.wait_recv)
        pl.when(has_hi)(copy_lo.wait_send)
        pl.when(has_lo)(copy_hi.wait_send)

    pending = exchange_start(0)
    run_setup()
    pl.when(has_lo)(voids_up.wait_recv)
    pl.when(has_hi)(voids_down.wait_recv)
    pl.when(has_hi)(voids_up.wait_send)
    pl.when(has_lo)(voids_down.wait_send)
    voids_lo = jnp.where(has_lo, vr_ref[0, :, tall - 1 : tall], 0.0)
    voids_hi = jnp.where(has_hi, vr_ref[1, :, 0:1], 0.0)
    stencil_weights(voids, voids_lo, voids_hi, tr_ref, w_ref)

    for h in range(steps):
        src = v_ref if h == 0 else o_ref
        copy_lo, copy_hi, copy_face = pending
        exchange_wait(copy_lo, copy_hi, copy_face)

        for s in range(species):
            w0 = w_ref[0, s]
            wxm = w_ref[1, s]
            wxp = w_ref[2, s]
            wym = w_ref[3, s]
            wyp = w_ref[4, s]
            sub = sub_ref[s]
            down = None
            for z in range(depth):
                v = src[s, z]
                xm = pltpu.roll(v, 1, 0)
                xp = pltpu.roll(v, wide - 1, 0)
                at = s * depth + z
                ym = jnp.where(lane == 0, hr_lo[h, :, at : at + 1], pltpu.roll(v, 1, 1))
                yp = jnp.where(lane == tall - 1, hr_hi[h, :, at : at + 1], pltpu.roll(v, tall - 1, 1))
                moved = w0 * v + ((wxp * xp + wxm * xm) + (wyp * yp + wym * ym))
                if z == 0:
                    down = moved * ip_ref[s, 0]
                else:
                    down = (moved - sub * down) * ip_ref[s, z]
                y_ref[s, z] = down
            g_ref[1, s] = down
        for z in range(depth - 2, -1, -1):
            for s in range(species):
                below = g_ref[1, s] if z == depth - 2 else y_ref[s, z + 1]
                y_ref[s, z] = y_ref[s, z] - cp_ref[s, z] * below
        for s in range(species):
            g_ref[0, s] = y_ref[s, 0]

        pl.when(at_inlet)(copy_face.wait_recv)
        pl.when(at_inlet)(copy_face.wait_send)
        for s in range(species):
            recycled = (plan_ref[h, s].astype(jnp.float32) + 1.0) * 0.25
            inlet = (1.0 - recycled) * feed_ref[s] + recycled * face_in[h, s]
            entry = jnp.where(at_inlet, -sub_ref[s] * inlet, 0.0)
            g_ref[2, s] = entry
            g_ref[0, s] = g_ref[0, s] + entry * l_ref[s, 0]
            g_ref[1, s] = g_ref[1, s] + entry * l_ref[s, depth - 1]
        g0 = g_ref[0]
        g1 = g_ref[1]
        sf[...] = g1 + co_ref[0] * g0
        sb[...] = g0 + co_ref[1] * g1
        ef[...] = zero_rows
        eb[...] = zero_rows
        sent = []
        for r in range(rounds):
            snd_f[h, r] = sf[...]
            snd_b[h, r] = sb[...]
            rank = r
            d = ROUNDS[r]
            has_right = position + d < count
            has_left = position - d >= 0
            right = jnp.minimum(position + d, count - 1)
            left = jnp.maximum(position - d, 0)
            copy_f = pltpu.make_async_remote_copy(
                src_ref=snd_f.at[h, r], dst_ref=rcv_f.at[h, r],
                send_sem=send_sem.at[h, 3 + r], recv_sem=recv_sem.at[h, 3 + r],
                device_id=(right, trans, col), device_id_type=MESH,
            )
            copy_b = pltpu.make_async_remote_copy(
                src_ref=snd_b.at[h, r], dst_ref=rcv_b.at[h, r],
                send_sem=send_sem.at[h, 3 + rounds + r], recv_sem=recv_sem.at[h, 3 + rounds + r],
                device_id=(left, trans, col), device_id_type=MESH,
            )
            pl.when(has_right)(copy_f.start)
            pl.when(has_left)(copy_b.start)
            last_round = r == rounds - 1
            if h == 0 and r == 0:
                spike_rows(cp_ref, ip_ref, l_ref, r_ref)

            @pl.when(has_left)
            def _():
                copy_f.wait_recv()
                got = rcv_f[h, r]
                ef[...] += co_ref[2 + rank] * got
                if not last_round:
                    sf[...] += co_ref[2 + rounds + rank] * got

            @pl.when(has_right)
            def _():
                copy_b.wait_recv()
                got = rcv_b[h, r]
                eb[...] += co_ref[2 + 2 * rounds + rank] * got
                if not last_round:
                    sb[...] += co_ref[2 + 3 * rounds + rank] * got

            sent.append((has_right, copy_f))
            sent.append((has_left, copy_b))

        before = ef[...]
        after = eb[...]
        r1 = g0 + co_ref[base + 0] * before + co_ref[base + 2] * after
        r2 = g1 + co_ref[base + 1] * before + co_ref[base + 3] * after
        top = r1 * co_ref[base + 6] + r2 * co_ref[base + 7]
        bottom = r1 * co_ref[base + 8] + r2 * co_ref[base + 9]
        ef[...] = sub_ref[...] * (before + co_ref[base + 4] * top)
        eb[...] = sup_ref[...] * (after + co_ref[base + 5] * bottom)
        for cond, copy in sent:
            pl.when(cond)(copy.wait_send)
        for s in range(species):
            ef[s] = ef[s] - g_ref[2, s]
        rows = range(depth)
        if h + 1 < steps:
            for s in range(species):
                o_ref[s, 0] = y_ref[s, 0] - ef[s] * l_ref[s, 0] - eb[s] * r_ref[s, 0]
            pending = exchange_start(h + 1)
            rows = range(1, depth)
        for s in range(species):
            left_coef = ef[s]
            right_coef = eb[s]
            for z in rows:
                o_ref[s, z] = y_ref[s, z] - left_coef * l_ref[s, z] - right_coef * r_ref[s, z]


def body(concentration, zone_map, porosity, axial_number, courant, transverse, feed_conc, plan):
    f32 = jnp.float32
    count = lax.axis_size("axial")
    values = concentration[0]
    species, depth, wide, tall = values.shape
    steps = plan.shape[1]
    zone = zone_map[0]
    assert species * depth <= tall
    rounds = len(ROUNDS)
    n_co = 2 + 4 * rounds + 10
    slab = (wide, tall)
    block = (species, depth) + slab
    smem = pl.BlockSpec(memory_space=pltpu.SMEM)

    n_slot = 3 + 2 * rounds
    out = pl.pallas_call(
        functools.partial(fused_kernel, count),
        out_shape=jax.ShapeDtypeStruct(block, f32),
        in_specs=[_vmem()] * 2 + [smem] * 6,
        out_specs=_vmem(),
        scratch_shapes=[pltpu.VMEM(block, f32)] * 4
        + [pltpu.VMEM((n_co, species) + slab, f32), pltpu.VMEM((5, species) + slab, f32)]
        + [pltpu.VMEM((species,) + slab, f32)] * 2
        + [pltpu.VMEM((count,) + slab, f32)] * 6
        + [pltpu.VMEM((rounds, count) + slab, f32)] * 2
        + [pltpu.VMEM(slab, f32), pltpu.VMEM((2,) + slab, f32)]
        + [pltpu.SemaphoreType.DMA((2,))] * 2
        + [pltpu.VMEM(block, f32)]
        + [pltpu.VMEM((steps,) + slab, f32)] * 4
        + [pltpu.VMEM((steps, species) + slab, f32)]
        + [pltpu.VMEM((3, species) + slab, f32)]
        + [pltpu.VMEM((species,) + slab, f32)] * 4
        + [pltpu.VMEM((steps, rounds, species) + slab, f32)] * 4
        + [pltpu.SemaphoreType.DMA((steps, n_slot))] * 2,
        compiler_params=pltpu.CompilerParams(collective_id=0, has_side_effects=True),
        cost_estimate=pl.CostEstimate(
            flops=100 * steps * species * depth * wide * tall, transcendentals=0,
            bytes_accessed=3 * 4 * species * depth * wide * tall,
        ),
    )(values, zone, porosity, axial_number, courant, transverse, plan[0], feed_conc[0])
    return out[None]


def solution(mesh):
    in_specs = (
        P("col", None, "axial", None, "trans"),
        P("col", None, "trans"),
        P(),
        P(),
        P(),
        P(),
        P("col", None),
        P("col", None, None),
    )
    out_specs = P("col", None, "axial", None, "trans")
    return jax.shard_map(body, mesh=mesh, in_specs=in_specs, out_specs=out_specs, check_vma=False)
```
